32 devices in a mesh: dp: 16 (over z, y, x), mp: 2 (over core).
Axes of the slice: x: 2, y: 2, z: 4, core: 2. Of those that a mesh axis runs over, the one named last changes fastest.
Arguments:
- tokens: bfloat16 [37632, 768], P('dp'), may hold values from -6 to 6
- counts: int32 [192], P('dp'), may hold values from 1 to 4, as said below
- visible: int32 [768, 49], P('dp'), may hold values from 0 to 195, as said below
- dest_device: int32 [768], P('dp'), may hold values from 0 to 15, as said below
- dest_slot: int32 [768], P('dp'), may hold values from 0 to 47, as said below
- cotangent: bfloat16 [768, 196, 512], P('dp', None, 'mp'), may hold values from -6 to 6
- weight_inproj: float32 [768, 3, 768], P('dp', None, 'mp'), as said below
- moment_inproj: float32 [768, 3, 768], P('dp', None, 'mp'), as said below
- square_inproj: float32 [768, 3, 768], P('dp', None, 'mp'), may hold values from 0.25 to 1
- weight_outproj: float32 [768, 768], P('mp', 'dp'), as said below
- moment_outproj: float32 [768, 768], P('mp', 'dp'), as said below
- square_outproj: float32 [768, 768], P('mp', 'dp'), may hold values from 0.25 to 1
- weight_expand: float32 [768, 3072], P('dp', 'mp'), as said below
- moment_expand: float32 [768, 3072], P('dp', 'mp'), as said below
- square_expand: float32 [768, 3072], P('dp', 'mp'), may hold values from 0.25 to 1
- weight_shrink: float32 [3072, 768], P('mp', 'dp'), as said below
- moment_shrink: float32 [3072, 768], P('mp', 'dp'), as said below
- square_shrink: float32 [3072, 768], P('mp', 'dp'), may hold values from 0.25 to 1
- weight_embedder: float32 [768, 512], P('dp', 'mp'), as said below
- moment_embedder: float32 [768, 512], P('dp', 'mp'), as said below
- square_embedder: float32 [768, 512], P('dp', 'mp'), may hold values from 0.25 to 1
- weight_lnparams: float32 [4, 768], P(None, 'dp'), may hold values from -2 to 2, as said below
- moment_lnparams: float32 [4, 768], P(None, 'dp'), may hold values from -9 to 9
- square_lnparams: float32 [4, 768], P(None, 'dp'), may hold values from 2.25 to 9
- weight_decparams: float32 [2, 2, 256], P(None, 'mp', 'dp'), may hold values from -3 to 3
- moment_decparams: float32 [2, 2, 256], P(None, 'mp', 'dp'), may hold values from -9 to 9
- square_decparams: float32 [2, 2, 256], P(None, 'mp', 'dp'), may hold values from 2.25 to 9
Outputs:
- decoded: bfloat16 [768, 196, 512], P('dp', None, 'mp')
- grad_tokens: bfloat16 [37632, 768], P('dp')
- clip_norm: float32 [1], replicated
- norms: float32 [2, 7], replicated
- grads_inproj: float32 [768, 3, 768], P('dp', None, 'mp')
- momenta_inproj: float32 [768, 3, 768], P('dp', None, 'mp')
- squares_inproj: float32 [768, 3, 768], P('dp', None, 'mp')
- updated_inproj: float32 [768, 3, 768], P('dp', None, 'mp')
- copies_inproj: bfloat16 [768, 3, 768], P('dp', None, 'mp')
- grads_outproj: float32 [768, 768], P('mp', 'dp')
- momenta_outproj: float32 [768, 768], P('mp', 'dp')
- squares_outproj: float32 [768, 768], P('mp', 'dp')
- updated_outproj: float32 [768, 768], P('mp', 'dp')
- copies_outproj: bfloat16 [768, 768], P('mp', 'dp')
- grads_expand: float32 [768, 3072], P('dp', 'mp')
- momenta_expand: float32 [768, 3072], P('dp', 'mp')
- squares_expand: float32 [768, 3072], P('dp', 'mp')
- updated_expand: float32 [768, 3072], P('dp', 'mp')
- copies_expand: bfloat16 [768, 3072], P('dp', 'mp')
- grads_shrink: float32 [3072, 768], P('mp', 'dp')
- momenta_shrink: float32 [3072, 768], P('mp', 'dp')
- squares_shrink: float32 [3072, 768], P('mp', 'dp')
- updated_shrink: float32 [3072, 768], P('mp', 'dp')
- copies_shrink: bfloat16 [3072, 768], P('mp', 'dp')
- grads_embedder: float32 [768, 512], P('dp', 'mp')
- momenta_embedder: float32 [768, 512], P('dp', 'mp')
- squares_embedder: float32 [768, 512], P('dp', 'mp')
- updated_embedder: float32 [768, 512], P('dp', 'mp')
- copies_embedder: bfloat16 [768, 512], P('dp', 'mp')
- grads_lnparams: float32 [4, 768], P(None, 'dp')
- momenta_lnparams: float32 [4, 768], P(None, 'dp')
- squares_lnparams: float32 [4, 768], P(None, 'dp')
- updated_lnparams: float32 [4, 768], P(None, 'dp')
- copies_lnparams: bfloat16 [4, 768], P(None, 'dp')
- grads_decparams: float32 [2, 2, 256], P(None, 'mp', 'dp')
- momenta_decparams: float32 [2, 2, 256], P(None, 'mp', 'dp')
- squares_decparams: float32 [2, 2, 256], P(None, 'mp', 'dp')
- updated_decparams: float32 [2, 2, 256], P(None, 'mp', 'dp')
- copies_decparams: bfloat16 [2, 2, 256], P(None, 'mp', 'dp')
The draws below stay inside these ranges and needn't reach their ends.
Inputs may be any that keep to these rules, and one draw needn't show every extreme that they name: `counts`: views of each episode; every value from 1 to 4 occurs. `visible`: each row names 49 different grid positions in increasing order. `dest_device`: every index of dp owns exactly 48 views, and no index of dp sends more than 3 of its views to one owner; that bound is reached. `dest_slot`: the views that one owner receives have different slots, so each of its 48 slots is taken once. `weight_lnparams`: rows 0 and 2 are gains, rows 1 and 3 biases. `weight_inproj`: entries of about the inverse root of 768 in size. `moment_inproj`: entries of mean zero. `weight_outproj`: entries of mean zero, of about 4 over the root of 768 in size. `moment_outproj`: entries of mean zero. `weight_expand`: entries of about the inverse root of 768 in size. `moment_expand`: entries of mean zero. `weight_shrink`: entries of mean zero, of about the inverse root of 3072 in size. `moment_shrink`: entries of mean zero. `weight_embedder`: entries of mean zero, of about the inverse root of 768 in size. `moment_embedder`: entries of mean zero.
All inputs are finite; a program needn't handle non-finite values.
Results may differ from the reference program's by a relative error of at most 0.02.
Values may be sent and summed in bfloat16 or wider, within the bound.
No kernel may reach another device: no remote copies, remote signals or barrier semaphores. Data moves between devices by JAX's collectives and lax.ppermute only.
A program may use at most 256 MiB of HBM per device.

```python
import math
import jax
import jax.numpy as jnp
from jax import lax

D = 768
HEADDIM = 64
FF = 3072
DDEC = 512
SIDE = 14
VPE = 4
EP_DEV = 12
GRID = 196
VIS = 49
VDEV = 48
TOK_DEV = 2352
SHARDS = 16
EPISODES = 192
NVIEWS = 768
TOKENS = 37632
PARAMS = 7475200
N_MP = 2


def draw_counts(key, part):
    table = jnp.array([1, 2, 3, 4, 4, 4, 4, 4, 4, 4, 4, 4, 4, 4, 4, 4], dtype=jnp.int32)
    picks = jax.random.randint(key, (EPISODES,), 0, 16)
    drawn = table[picks]
    anchor = jax.random.randint(jax.random.fold_in(key, 5), (), 0, EPISODES)
    drawn = drawn.at[anchor].set(4)
    drawn = drawn.at[(anchor + 1) % EPISODES].set(1)
    drawn = drawn.at[(anchor + 2) % EPISODES].set(2)
    drawn = drawn.at[(anchor + 3) % EPISODES].set(3)
    return drawn.astype(jnp.int32)


def draw_visible(key, part):
    scores = jax.random.randint(key, (NVIEWS, GRID), 0, 1 << 20) * GRID + jnp.arange(GRID, dtype=jnp.int32)[None, :]
    order = jnp.argsort(scores, axis=1, stable=True)
    return jnp.sort(order[:, :VIS], axis=1).astype(jnp.int32)


def routing(key):
    base = jax.random.fold_in(key, 41)
    owners = jax.random.permutation(jax.random.fold_in(base, 1), SHARDS)
    starts = jax.random.permutation(jax.random.fold_in(base, 2), SHARDS)
    offsets = jax.random.permutation(jax.random.fold_in(base, 3), SHARDS)
    ranks = jax.random.randint(jax.random.fold_in(base, 4), (SHARDS, VDEV), 0, 1 << 20) * VDEV + jnp.arange(VDEV, dtype=jnp.int32)[None, :]
    slots = jnp.argsort(ranks, axis=1, stable=True).astype(jnp.int32)
    shifted = offsets[slots % SHARDS]
    target = owners[(starts[:, None] + shifted) % SHARDS]
    return (target.reshape(-1).astype(jnp.int32), slots.reshape(-1).astype(jnp.int32))


def draw_dest_device(key, part):
    return routing(key)[0]


def draw_dest_slot(key, part):
    return routing(key)[1]


def draw_weight_lnparams(key, part):
    gains = jax.random.uniform(jax.random.fold_in(key, 1), (2, D), jnp.float32, 0.5, 1.5)
    biases = jnp.clip(0.5 * jax.random.normal(jax.random.fold_in(key, 2), (2, D), jnp.float32), -2.0, 2.0)
    return jnp.stack([gains[0], biases[0], gains[1], biases[1]])


def rising_draw(key, tag, shape, axis, scale, shared=0.0):
    top = 3.0
    mean_square = 13.0 / 3.0
    count = shape[axis]
    place = jnp.arange(count, dtype=jnp.float32) / (count - 1)
    factor = (1.0 + (top - 1.0) * place) / jnp.sqrt(mean_square)
    view = [1] * len(shape)
    view[axis] = count
    noise = jax.random.truncated_normal(jax.random.fold_in(key, tag), -6.0, 6.0, shape, jnp.float32)
    if shared > 0.0:
        keep = list(shape)
        keep[axis] = 1
        common = jax.random.truncated_normal(jax.random.fold_in(key, tag + 500), -6.0, 6.0, tuple(keep), jnp.float32)
        noise = (noise + common) * (1.0 / (1.0 + shared) ** 0.5)
    return noise * scale * factor.reshape(view)


def draw_weight_inproj(key, part):
    return rising_draw(key, 101, (D, 3, D), 0, D ** (-0.5), 1.0)


def draw_moment_inproj(key, part):
    return rising_draw(key, 102, (D, 3, D), 0, 0.5)


def draw_weight_outproj(key, part):
    return rising_draw(key, 103, (D, D), 1, (D // 16) ** (-0.5))


def draw_moment_outproj(key, part):
    return rising_draw(key, 104, (D, D), 1, 0.5)


def draw_weight_expand(key, part):
    return rising_draw(key, 105, (D, FF), 0, D ** (-0.5), 1.0)


def draw_moment_expand(key, part):
    return rising_draw(key, 106, (D, FF), 0, 0.5)


def draw_weight_shrink(key, part):
    return rising_draw(key, 107, (FF, D), 1, FF ** (-0.5))


def draw_moment_shrink(key, part):
    return rising_draw(key, 108, (FF, D), 1, 0.5)


def draw_weight_embedder(key, part):
    return rising_draw(key, 109, (D, DDEC), 0, D ** (-0.5))


def draw_moment_embedder(key, part):
    return rising_draw(key, 110, (D, DDEC), 0, 0.5)


def block_levels(own_key, extent, shards, smallest, high):
    def one(dim, parts):
        heights = jax.random.uniform(jax.random.fold_in(jax.random.fold_in(own_key, 6), dim), (parts,), jnp.float32, smallest / len(shards), high / len(shards))
        return jnp.repeat(jnp.exp(heights), extent[dim] // parts).reshape((-1,) + (1,) * (len(extent) - dim - 1))

    level = one(*shards[0])
    for cut in shards[1:]:
        level = level * one(*cut)
    return level


def scatter_about(key, extent, deviation, bound, shards=(), kind=jnp.bfloat16):
    entries = deviation * jax.random.normal(key, extent, jnp.float32)
    if shards:
        entries = entries * block_levels(key, extent, shards, -0.22, 0.18)
    return jnp.clip(entries, -bound, bound).astype(kind)


def setup_inputs(seed: int = 0) -> dict:
    streams_of = jax.random.split(jax.random.key(seed), 28)
    tokens = scatter_about(streams_of[0], (TOKENS, D), 1.0, 6.0, ((0, 16),))
    counts = draw_counts(jax.random.fold_in(streams_of[27], 71), 0)
    visible = draw_visible(jax.random.fold_in(streams_of[27], 71), 0)
    dest_device = draw_dest_device(jax.random.fold_in(streams_of[27], 71), 0)
    dest_slot = draw_dest_slot(jax.random.fold_in(streams_of[27], 71), 0)
    cotangent = scatter_about(streams_of[5], (NVIEWS, GRID, DDEC), 1.0, 6.0, ((0, 16), (2, 2)))
    weight_inproj = draw_weight_inproj(jax.random.fold_in(streams_of[27], 71), 0)
    moment_inproj = draw_moment_inproj(jax.random.fold_in(streams_of[27], 71), 0)
    square_inproj = jnp.clip(jnp.exp(math.log(1.0) - 1.3862944 * jax.random.uniform(streams_of[8], (D, 3, D), jnp.float32) ** block_levels(streams_of[8], (D, 3, D), ((0, 16), (2, 2)), -0.2, 0.2)), 0.25, 1.0)
    weight_outproj = draw_weight_outproj(jax.random.fold_in(streams_of[27], 71), 0)
    moment_outproj = draw_moment_outproj(jax.random.fold_in(streams_of[27], 71), 0)
    square_outproj = jnp.clip(jnp.exp(math.log(1.0) - 1.3862944 * jax.random.uniform(streams_of[11], (D, D), jnp.float32) ** block_levels(streams_of[11], (D, D), ((0, 2), (1, 16)), -0.2, 0.2)), 0.25, 1.0)
    weight_expand = draw_weight_expand(jax.random.fold_in(streams_of[27], 71), 0)
    moment_expand = draw_moment_expand(jax.random.fold_in(streams_of[27], 71), 0)
    square_expand = jnp.clip(jnp.exp(math.log(1.0) - 1.3862944 * jax.random.uniform(streams_of[14], (D, FF), jnp.float32) ** block_levels(streams_of[14], (D, FF), ((0, 16), (1, 2)), -0.2, 0.2)), 0.25, 1.0)
    weight_shrink = draw_weight_shrink(jax.random.fold_in(streams_of[27], 71), 0)
    moment_shrink = draw_moment_shrink(jax.random.fold_in(streams_of[27], 71), 0)
    square_shrink = jnp.clip(jnp.exp(math.log(1.0) - 1.3862944 * jax.random.uniform(streams_of[17], (FF, D), jnp.float32) ** block_levels(streams_of[17], (FF, D), ((0, 2), (1, 16)), -0.2, 0.2)), 0.25, 1.0)
    weight_embedder = draw_weight_embedder(jax.random.fold_in(streams_of[27], 71), 0)
    moment_embedder = draw_moment_embedder(jax.random.fold_in(streams_of[27], 71), 0)
    square_embedder = jnp.clip(jnp.exp(math.log(1.0) - 1.3862944 * jax.random.uniform(streams_of[20], (D, DDEC), jnp.float32) ** block_levels(streams_of[20], (D, DDEC), ((0, 16), (1, 2)), -0.2, 0.2)), 0.25, 1.0)
    weight_lnparams = draw_weight_lnparams(jax.random.fold_in(streams_of[27], 71), 0)
    moment_lnparams = scatter_about(streams_of[22], (4, D), 1.5, 9.0, ((1, 16),), jnp.float32)
    square_lnparams = jnp.clip(jnp.exp(math.log(9.0) - 1.3862944 * jax.random.uniform(streams_of[23], (4, D), jnp.float32) ** block_levels(streams_of[23], (4, D), ((1, 16),), -0.2, 0.2)), 2.25, 9.0)
    weight_decparams = scatter_about(streams_of[24], (2, N_MP, DDEC // N_MP), 0.5, 3.0, ((1, 2), (2, 16)), jnp.float32)
    moment_decparams = scatter_about(streams_of[25], (2, N_MP, DDEC // N_MP), 1.5, 9.0, ((1, 2), (2, 16)), jnp.float32)
    square_decparams = jnp.clip(jnp.exp(math.log(9.0) - 1.3862944 * jax.random.uniform(streams_of[26], (2, N_MP, DDEC // N_MP), jnp.float32) ** block_levels(streams_of[26], (2, N_MP, DDEC // N_MP), ((1, 2), (2, 16)), -0.2, 0.2)), 2.25, 9.0)
    return {"tokens": tokens, "counts": counts, "visible": visible, "dest_device": dest_device, "dest_slot": dest_slot, "cotangent": cotangent, "weight_inproj": weight_inproj, "moment_inproj": moment_inproj, "square_inproj": square_inproj, "weight_outproj": weight_outproj, "moment_outproj": moment_outproj, "square_outproj": square_outproj, "weight_expand": weight_expand, "moment_expand": moment_expand, "square_expand": square_expand, "weight_shrink": weight_shrink, "moment_shrink": moment_shrink, "square_shrink": square_shrink, "weight_embedder": weight_embedder, "moment_embedder": moment_embedder, "square_embedder": square_embedder, "weight_lnparams": weight_lnparams, "moment_lnparams": moment_lnparams, "square_lnparams": square_lnparams, "weight_decparams": weight_decparams, "moment_decparams": moment_decparams, "square_decparams": square_decparams}


HIGH = lax.Precision.HIGHEST
NORM_EPS = 1e-06
MASK_FILL = -1e+30
BETA_ONE = 0.5
BETA_TWO = 0.5
ADAM_EPS = 1e-06
DECAY_RATE = 0.01
LEARN_RATE = 0.5
TRUST_EPS = 1e-06

@jax.custom_vjp
def low(v):
    return lax.optimization_barrier(v.astype(jnp.bfloat16)).astype(jnp.float32)

@jax.custom_vjp
def low_back(v):
    return v

def low_keep(v):
    return (low(v), None)

def low_pass(kept, grad):
    return (grad,)

def back_keep(v):
    return (v, None)

def back_low(kept, grad):
    return (low(grad),)
low.defvjp(low_keep, low_pass)
low_back.defvjp(back_keep, back_low)

def layer_norm(values):
    centre = values - lax.optimization_barrier(jnp.mean(values, axis=-1, keepdims=True))
    spread = lax.optimization_barrier(jnp.mean(centre * centre, axis=-1, keepdims=True))
    return centre * lax.rsqrt(spread + NORM_EPS)

def allowed_mask(counts, span, per_view):
    slot_view = jnp.arange(span, dtype=jnp.int32) // per_view
    live = slot_view[None, :] < counts[:, None]
    same = slot_view[:, None] == slot_view[None, :]
    return live[:, None, :] | same[None]

def grid_positions(side, width):
    quarter = width // 4
    rate = 1.0 / 10000.0 ** (jnp.arange(quarter, dtype=jnp.float32) / quarter)
    place = jnp.arange(side * side, dtype=jnp.int32)
    row_pos = (place // side).astype(jnp.float32)
    col_pos = (place % side).astype(jnp.float32)
    row_angle = row_pos[:, None] * rate[None, :]
    col_angle = col_pos[:, None] * rate[None, :]
    return jnp.concatenate([jnp.sin(row_angle), jnp.cos(row_angle), jnp.sin(col_angle), jnp.cos(col_angle)], axis=1)

def gelu_exact(values):
    return 0.5 * values * (1.0 + lax.erf(values * (1.0 / math.sqrt(2.0))))

def lamb_terms(grad, moment, square, weight, factor):
    clipped = grad * factor
    moment_new = BETA_ONE * moment + (1.0 - BETA_ONE) * clipped
    square_new = BETA_TWO * square + (1.0 - BETA_TWO) * clipped * clipped
    direction = moment_new / (jnp.sqrt(square_new) + ADAM_EPS) + DECAY_RATE * weight
    return (clipped, moment_new, square_new, direction)

def encode_group(working, tokens, counts_group):
    inproj, outproj, expand, shrink, embedder, lnparams, decparams = working
    row_count = tokens.shape[0]
    episode_count = counts_group.shape[0]
    span = row_count // episode_count
    allowed = allowed_mask(counts_group, span, VIS)
    part_model = D // N_MP
    part_hidden = FF // N_MP
    part_dec = DDEC // N_MP
    scale = 1.0 / math.sqrt(HEADDIM)
    first = low(layer_norm(tokens) * lnparams[0] + lnparams[1])
    attn = jnp.zeros_like(tokens)
    for part in range(N_MP):
        share = low_back(first)
        columns = inproj[:, :, part * part_model:(part + 1) * part_model].reshape(D, 3 * part_model)
        packed = low_back(low(jnp.dot(share, columns, precision=HIGH)))
        packed = packed.reshape(episode_count, span, 3, part_model // HEADDIM, HEADDIM)
        query = packed[:, :, 0]
        key_rows = packed[:, :, 1]
        value_rows = packed[:, :, 2]
        scores = low_back(jnp.einsum('elhd,emhd->ehlm', query, key_rows, precision=HIGH))
        scores = jnp.where(allowed[:, None], scores * scale, MASK_FILL)
        probs = low(jax.nn.softmax(scores, axis=-1))
        mixed = jnp.einsum('ehlm,emhd->elhd', probs, value_rows, precision=HIGH).reshape(row_count, part_model)
        mixed = low_back(low(mixed))
        attn = attn + low(jnp.dot(mixed, outproj[part * part_model:(part + 1) * part_model], precision=HIGH))
    middle = tokens + low_back(attn)
    second = low(layer_norm(middle) * lnparams[2] + lnparams[3])
    mlp = jnp.zeros_like(tokens)
    for part in range(N_MP):
        share = low_back(second)
        pre = low_back(jnp.dot(share, expand[:, part * part_hidden:(part + 1) * part_hidden], precision=HIGH))
        act = low(gelu_exact(pre))
        mlp = mlp + low(jnp.dot(act, shrink[part * part_hidden:(part + 1) * part_hidden], precision=HIGH))
    final_low = low(middle + low_back(mlp))
    flat_dec = decparams.reshape(2, DDEC)
    pieces = []
    for part in range(N_MP):
        share = low_back(final_low)
        lo_col = part * part_dec
        hi_col = (part + 1) * part_dec
        pieces.append(low(jnp.dot(share, embedder[:, lo_col:hi_col], precision=HIGH) + flat_dec[0, lo_col:hi_col]))
    return jnp.concatenate(pieces, axis=1)

def assemble(z_block, decparams, vis_block, live_block, positions):
    flat = low(decparams).reshape(2, DDEC)
    place = (vis_block[:, None, :] == jnp.arange(GRID, dtype=jnp.int32)[None, :, None]).astype(jnp.float32)
    covered = lax.optimization_barrier(jnp.sum(place, axis=2))
    spread_rows = jnp.einsum('vgi,viw->vgw', place, z_block, precision=HIGH)
    filled = spread_rows + (1.0 - covered)[:, :, None] * flat[1]
    return low(live_block[:, None, None] * filled + positions[None])

def reference(tokens, counts, visible, dest_device, dest_slot, cotangent, weight_inproj, moment_inproj, square_inproj, weight_outproj, moment_outproj, square_outproj, weight_expand, moment_expand, square_expand, weight_shrink, moment_shrink, square_shrink, weight_embedder, moment_embedder, square_embedder, weight_lnparams, moment_lnparams, square_lnparams, weight_decparams, moment_decparams, square_decparams):
    masters = (weight_inproj, weight_outproj, weight_expand, weight_shrink, weight_embedder, weight_lnparams, weight_decparams)
    moments = (moment_inproj, moment_outproj, moment_expand, moment_shrink, moment_embedder, moment_lnparams, moment_decparams)
    squares = (square_inproj, square_outproj, square_expand, square_shrink, square_embedder, square_lnparams, square_decparams)
    live = (jnp.arange(NVIEWS, dtype=jnp.int32) % VPE < jnp.repeat(counts, VPE)).astype(jnp.float32)

    def encoder_all(params, inputs):
        working = tuple((low(weight) for weight in params))

        def one_group(carry, group):
            tok_group, count_group = group
            return (carry, encode_group(working, tok_group, count_group))
        _, outputs = lax.scan(jax.checkpoint(one_group), jnp.zeros((), jnp.float32), (inputs.reshape(SHARDS, TOK_DEV, D), counts.reshape(SHARDS, EP_DEV)))
        return outputs.reshape(NVIEWS, VIS, DDEC)
    z_views, encoder_back = jax.vjp(encoder_all, masters, tokens.astype(jnp.float32))
    owner_row = (dest_device * VDEV + dest_slot).astype(jnp.int32)
    inverse = jnp.zeros((NVIEWS,), jnp.int32).at[owner_row].set(jnp.arange(NVIEWS, dtype=jnp.int32))
    z_owner, order_back = jax.vjp(lambda values: values[inverse], z_views)
    positions = grid_positions(SIDE, DDEC)

    def per_owner(block):
        z_block, vis_block, live_block, cot_block = block
        out_block, back = jax.vjp(lambda zb, dp: assemble(zb, dp, vis_block, live_block, positions), z_block, weight_decparams)
        grad_z, grad_dec = back(cot_block.astype(jnp.float32))
        return (out_block.astype(jnp.bfloat16), grad_z, grad_dec)
    decoded, grad_owner, grad_decs = lax.map(per_owner, (z_owner.reshape(SHARDS, VDEV, VIS, DDEC), visible[inverse].reshape(SHARDS, VDEV, VIS), live[inverse].reshape(SHARDS, VDEV), cotangent.reshape(SHARDS, VDEV, GRID, DDEC)))
    grad_views, = order_back(grad_owner.reshape(NVIEWS, VIS, DDEC))
    grads_enc, grad_inputs = encoder_back(grad_views)
    grads = list(grads_enc)
    grads[6] = grads[6] + lax.optimization_barrier(jnp.sum(grad_decs, axis=0))
    grad_sq = jnp.stack([jnp.sum(g * g) for g in grads])
    clip_norm = jnp.sqrt(jnp.sum(grad_sq))
    factor = jnp.minimum(1.0, 0.5 * math.sqrt(PARAMS) / clip_norm)
    pieces = [lamb_terms(g, m, s, w, factor) for g, m, s, w in zip(grads, moments, squares, masters)]
    weight_norm = jnp.sqrt(jnp.stack([jnp.sum(w * w) for w in masters]))
    update_norm = jnp.sqrt(jnp.stack([jnp.sum(p[3] * p[3]) for p in pieces]))
    ratio = weight_norm / (update_norm + TRUST_EPS)
    res = []
    for index in range(7):
        updated = masters[index] - LEARN_RATE * ratio[index] * pieces[index][3]
        res.extend([pieces[index][0], pieces[index][1], pieces[index][2], updated, updated.astype(jnp.bfloat16)])
    return (decoded.reshape(NVIEWS, GRID, DDEC), grad_inputs.astype(jnp.bfloat16), clip_norm.reshape(1), jnp.stack([weight_norm, update_norm]), res[0], res[1], res[2], res[3], res[4], res[5], res[6], res[7], res[8], res[9], res[10], res[11], res[12], res[13], res[14], res[15], res[16], res[17], res[18], res[19], res[20], res[21], res[22], res[23], res[24], res[25], res[26], res[27], res[28], res[29], res[30], res[31], res[32], res[33], res[34])
```

```python
import math

import jax
import jax.numpy as jnp
from jax import lax
from jax.experimental import pallas as pl
from jax.experimental.pallas import tpu as pltpu
from jax.sharding import PartitionSpec as P

HEADDIM = 64
PARAMS = 7475200
NORM_EPS = 1e-06
MASK_FILL = -1e30
BETA_ONE = 0.5
BETA_TWO = 0.5
ADAM_EPS = 1e-06
DECAY_RATE = 0.01
LEARN_RATE = 0.5
TRUST_EPS = 1e-06

F32 = jnp.float32
BF16 = jnp.bfloat16
AXES = ("dp", "mp")
NT = (((1,), (1,)), ((), ()))
TN = (((0,), (0,)), ((), ()))
ROUND = 16
VMEM_BYTES = 58 << 20


def mm(a, b, dims=(((1,), (0,)), ((), ()))):
    return lax.dot_general(a, b, dims, preferred_element_type=F32)


def norm_rows(values):
    centre = values - jnp.mean(values, axis=-1, keepdims=True)
    spread = jnp.mean(centre * centre, axis=-1, keepdims=True)
    inverse = lax.rsqrt(spread + NORM_EPS)
    return centre * inverse, inverse


def norm_back(scaled, normed, inverse):
    return inverse * (
        scaled
        - jnp.mean(scaled, axis=-1, keepdims=True)
        - normed * jnp.mean(scaled * normed, axis=-1, keepdims=True)
    )


def grid_positions(side, width):
    quarter = width // 4
    rate = 1.0 / 10000.0 ** (jnp.arange(quarter, dtype=F32) / quarter)
    place = jnp.arange(side * side, dtype=jnp.int32)
    row_pos = (place // side).astype(F32)
    col_pos = (place % side).astype(F32)
    row_angle = row_pos[:, None] * rate[None, :]
    col_angle = col_pos[:, None] * rate[None, :]
    return jnp.concatenate(
        [jnp.sin(row_angle), jnp.cos(row_angle), jnp.sin(col_angle), jnp.cos(col_angle)], axis=1
    )


def any_spec():
    return pl.BlockSpec(memory_space=pl.ANY)


def params(limit=VMEM_BYTES):
    return pltpu.CompilerParams(vmem_limit_bytes=limit)


def cost(flops, nbytes):
    return pl.CostEstimate(flops=int(flops), bytes_accessed=int(nbytes), transcendentals=0)


def swap(array, peers, bits, core=0):
    bits = bits if isinstance(bits, tuple) else (bits, bits)
    pairs = [
        (d * 2 + m, (d ^ bits[m]) * 2 + (m ^ core)) for d in range(peers) for m in range(2)
    ]
    return lax.ppermute(array, AXES, pairs)


FAST_PEERS = 16
Z_STEPS = (4, 8, 12)


def gather_chunk(shard, peers):
    if peers != FAST_PEERS:
        return [lax.all_gather(lax.all_gather(shard, "dp", axis=0, tiled=True), "mp", axis=0)]
    along = jnp.stack([shard] + [swap(shard, peers, bits) for bits in Z_STEPS])
    first = swap(along, peers, (1, 2))
    mine = [along, first, swap(along, peers, (2, 1)), swap(first, peers, (2, 1))]
    return mine + [swap(piece, peers, 0, 1) for piece in mine]


def gather_table(me, core):
    one = jnp.where(core == 0, 1, 2)
    two = 3 - one
    zero = jnp.zeros_like(one)
    bases = jnp.stack([zero, one, two, one * 0 + 3, zero, two, one, one * 0 + 3])
    owners = me ^ bases[:, None] ^ jnp.array((0,) + Z_STEPS, jnp.int32)[None, :]
    cores = jnp.stack([core] * 4 + [1 - core] * 4)
    return jnp.concatenate([owners.reshape(-1), cores]).astype(jnp.int32)


def weight_copies(parts, table, target, sems):
    if len(parts) == 1:
        return [pltpu.make_async_copy(parts[0], target, sems.at[0])]
    copies = []
    for index, part in enumerate(parts):
        half = table[len(parts) * 4 + index]
        for inner in range(4):
            rows = part.shape[1]
            start = pl.multiple_of(table[index * 4 + inner] * rows, ROUND)
            copies.append(
                pltpu.make_async_copy(
                    part.at[inner], target.at[half, pl.ds(start, rows), :], sems.at[index * 4 + inner]
                )
            )
    return copies


def place_table(me, core):
    near = jnp.where(core == 0, 2, 1)
    far = 3 - near
    apart = jnp.arange(FAST_PEERS, dtype=jnp.int32) ^ me
    return (
        jnp.where((apart & near) != 0, 8, 0) + jnp.where((apart & far) != 0, 4, 0) + (apart >> 2)
    ).astype(jnp.int32)


def scatter_chunk(mine, other, peers):
    if peers != FAST_PEERS:
        whole = mine.astype(F32) + swap(other, peers, 0, 1).astype(F32)
        return lax.psum_scatter(
            whole.reshape(-1, whole.shape[-1]), "dp", scatter_dimension=0, tiled=True
        )
    got = swap(other, peers, 0, 1)
    add = lambda *terms: sum(term.astype(F32) for term in terms)
    got_one = swap(add(mine[8:], got[8:]).astype(BF16), peers, (2, 1))
    got_two = swap(add(mine[4:8], got[4:8], got_one[4:]).astype(BF16), peers, (1, 2))
    last = [
        swap(add(mine[i], got[i], got_one[i], got_two[i]).astype(BF16), peers, Z_STEPS[i - 1])
        for i in (1, 2, 3)
    ]
    return add(mine[0], got[0], got_one[0], got_two[0], *last)


def view_of(rows, per_view):
    view = jnp.zeros_like(rows)
    for edge in range(1, 5):
        view = view + (rows >= edge * per_view).astype(jnp.int32)
    return view


def allowed_bias(size, count, per_view):
    query = view_of(lax.broadcasted_iota(jnp.int32, (size, size), 0), per_view)
    key = view_of(lax.broadcasted_iota(jnp.int32, (size, size), 1), per_view)
    return jnp.where((key < count) | (key == query), 0.0, MASK_FILL)


def pair_masks(scale):
    lane = lax.broadcasted_iota(jnp.int32, (1, 2 * HEADDIM), 1)
    low = (lane < HEADDIM).astype(F32)
    return (low * scale).astype(BF16), ((1.0 - low) * scale).astype(BF16)


def attn_forward(mp_s, counts_s, table, tokens, norms, *rest, nparts, per_view, part):
    parts, (first_o, packed_o, attended_o, middle_o, second_o, lse_o), (weights, sems) = (
        rest[:nparts],
        rest[nparts : nparts + 6],
        rest[nparts + 6 :],
    )
    step = pl.program_id(0)
    copies = weight_copies(parts, table, weights, sems)

    @pl.when(step == 0)
    def _():
        for copy in copies:
            copy.start()
        for copy in copies:
            copy.wait()

    size = tokens.shape[0]
    scale = 1.0 / math.sqrt(HEADDIM)
    values = tokens[...].astype(F32)
    normed, _ = norm_rows(values)
    first = (normed * norms[0:1, :] + norms[1:2, :]).astype(BF16)
    first_o[...] = first
    bias = allowed_bias(size, counts_s[mp_s[0] * pl.num_programs(0) + step], per_view)
    masks = pair_masks(scale)
    lane = lax.broadcasted_iota(jnp.int32, (size, 2 * HEADDIM), 1)
    wide = 2 * HEADDIM
    lse = jnp.zeros((size, wide), F32)
    attn = jnp.zeros(values.shape, F32)
    for half in range(2):
        packed = mm(first, weights[half, :, : 3 * part]).astype(BF16)
        packed_o[:, half * 3 * part : (half + 1) * 3 * part] = packed
        for pair in range(part // wide):
            at = pair * wide
            query = packed[:, at : at + wide]
            key = packed[:, part + at : part + at + wide]
            value = packed[:, 2 * part + at : 2 * part + at + wide]
            outs = []
            for which in range(2):
                logits = mm(query * masks[which], key, NT) + bias
                top = jnp.max(logits, axis=-1, keepdims=True)
                exponent = jnp.exp(logits - top)
                total = jnp.sum(exponent, axis=-1, keepdims=True)
                probs = (exponent * (1.0 / total)).astype(BF16)
                outs.append(mm(probs, value))
                index = half * (part // HEADDIM) + pair * 2 + which
                lse = jnp.where(lane == index, top + jnp.log(total), lse)
            both = jnp.where(lane < HEADDIM, outs[0], outs[1]).astype(BF16)
            attended_o[:, half * part + at : half * part + at + wide] = both
        attn = attn + mm(
            attended_o[:, half * part : (half + 1) * part], weights[half, :, 3 * part :], NT
        )
    lse_o[...] = lse
    middle = values + attn
    middle_o[...] = middle
    normed, _ = norm_rows(middle)
    second_o[...] = (normed * norms[2:3, :] + norms[3:4, :]).astype(BF16)


def mlp_forward(mp_s, table, second, middle, dec_bias, *rest, nparts, per_view, part, wide, rows_each):
    up_parts, down_parts = rest[:nparts], rest[nparts : 2 * nparts]
    act_o, slope_o, final_o, keep_o, send_o = rest[2 * nparts : 2 * nparts + 5]
    up, down, up_sems, down_sems = rest[2 * nparts + 5 :]
    copies = weight_copies(up_parts, table, up, up_sems) + weight_copies(
        down_parts, table, down, down_sems
    )

    @pl.when(pl.program_id(0) == 0)
    def _():
        for copy in copies:
            copy.start()
        for copy in copies:
            copy.wait()

    acc = middle[...]
    rows = second[...]
    for half in range(2):
        for start in range(0, part, wide):
            pre = mm(rows, up[half, :, start : start + wide])
            cumulative = 0.5 * (1.0 + lax.erf(pre * (1.0 / math.sqrt(2.0))))
            act = (pre * cumulative).astype(BF16)
            slope = cumulative + pre * jnp.exp(-0.5 * pre * pre) * (1.0 / math.sqrt(2.0 * math.pi))
            act_o[:, half * part + start : half * part + start + wide] = act
            slope_o[:, half * part + start : half * part + start + wide] = slope.astype(BF16)
            acc = acc + mm(act, down[half, :, start : start + wide], NT)
    final = acc.astype(BF16)
    final_o[...] = final
    outs = [
        mm(final, down[half, :, part:]) + dec_bias[half : half + 1, :] for half in range(2)
    ]
    mine = jnp.where(mp_s[0] == 0, outs[0], outs[1])
    theirs = jnp.where(mp_s[0] == 0, outs[1], outs[0])
    views = rows_each // per_view
    for view in range(keep_o.shape[0]):
        at = (view // views) * rows_each + (view % views) * per_view
        keep_o[view] = mine[at : at + per_view].astype(BF16)
        send_o[view] = theirs[at : at + per_view].astype(BF16)


def mlp_backward(
    mp_s, where_s, table, mine, theirs, slope, middle, norms, *rest, nparts, per_view, part, wide, rows_each
):
    up_parts, down_parts = rest[:nparts], rest[nparts : 2 * nparts]
    rows_o, low_o, pre_o, mid_o, midlow_o, sums_o = rest[2 * nparts : 2 * nparts + 6]
    up, down, pieces, flat, up_sems, down_sems, piece_sems = rest[2 * nparts + 6 :]
    step = pl.program_id(0)
    nviews = pieces.shape[1]
    copies = weight_copies(up_parts, table, up, up_sems) + weight_copies(
        down_parts, table, down, down_sems
    )
    fetch = []
    for view in range(nviews):
        at = where_s[step * nviews + view]
        fetch.append(
            pltpu.make_async_copy(mine.at[at], pieces.at[mp_s[0], view], piece_sems.at[0, view])
        )
        fetch.append(
            pltpu.make_async_copy(theirs.at[at], pieces.at[1 - mp_s[0], view], piece_sems.at[1, view])
        )
    for copy in fetch:
        copy.start()

    @pl.when(step == 0)
    def _():
        for copy in copies:
            copy.start()
        flat[...] = jnp.zeros_like(flat)
        sums_o[...] = jnp.zeros_like(sums_o)
        for copy in copies:
            copy.wait()

    for copy in fetch:
        copy.wait()
    dec = pieces.shape[3]
    views = rows_each // per_view
    for view in range(nviews):
        at = (view // views) * rows_each + (view % views) * per_view
        for half in range(2):
            flat[at : at + per_view, half * dec : (half + 1) * dec] = pieces[half, view].astype(F32)
    rows = flat[...].astype(BF16)
    rows_o[...] = rows
    final = mm(rows[:, :dec], down[0, :, part:], NT) + mm(rows[:, dec:], down[1, :, part:], NT)
    low = final.astype(BF16)
    low_o[...] = low
    acc = jnp.zeros(final.shape, F32)
    for half in range(2):
        for start in range(0, part, wide):
            at = half * part + start
            hidden = mm(low, down[half, :, start : start + wide])
            pre = (hidden * slope[:, at : at + wide].astype(F32)).astype(BF16)
            pre_o[:, at : at + wide] = pre
            acc = acc + mm(pre, up[half, :, start : start + wide], NT)
    normed, inverse = norm_rows(middle[...])
    sums_o[0:1, :] += jnp.sum(acc * normed, axis=0, keepdims=True)
    sums_o[1:2, :] += jnp.sum(acc, axis=0, keepdims=True)
    mid = final + norm_back(acc * norms[2:3, :], normed, inverse)
    mid_o[...] = mid
    midlow_o[...] = mid.astype(BF16)


def attn_backward(
    mp_s, counts_s, table, tokens, packed, lse, mid, norms, *rest, nparts, per_view, part
):
    parts, (packed_o, tokens_o, sums_o), (weights, sems) = (
        rest[:nparts],
        rest[nparts : nparts + 3],
        rest[nparts + 3 :],
    )
    step = pl.program_id(0)
    copies = weight_copies(parts, table, weights, sems)

    @pl.when(step == 0)
    def _():
        for copy in copies:
            copy.start()
        sums_o[...] = jnp.zeros_like(sums_o)
        for copy in copies:
            copy.wait()

    size = tokens.shape[0]
    scale = 1.0 / math.sqrt(HEADDIM)
    wide = 2 * HEADDIM
    bias = allowed_bias(size, counts_s[mp_s[0] * pl.num_programs(0) + step], per_view)
    scaled_masks, masks = pair_masks(scale), pair_masks(1.0)
    lane = lax.broadcasted_iota(jnp.int32, (size, wide), 1)
    low = lane < HEADDIM
    middle = mid[...]
    middle_low = middle.astype(BF16)
    back = jnp.zeros(middle.shape, F32)
    for half in range(2):
        grad_att = mm(middle_low, weights[half, :, 3 * part :]).astype(BF16)
        base = half * 3 * part
        for pair in range(part // wide):
            at = pair * wide
            query = packed[:, base + at : base + at + wide]
            key = packed[:, base + part + at : base + part + at + wide]
            value = packed[:, base + 2 * part + at : base + 2 * part + at + wide]
            grad = grad_att[:, at : at + wide]
            outs = []
            for which in range(2):
                index = half * (part // HEADDIM) + pair * 2 + which
                logits = mm(query * scaled_masks[which], key, NT) + bias
                probs = jnp.exp(logits - lse[:, index : index + 1])
                grad_probs = mm(grad * masks[which], value, NT)
                weighted = probs * grad_probs
                centre = jnp.sum(weighted, axis=-1, keepdims=True)
                scores = ((weighted - probs * centre) * scale).astype(BF16)
                outs.append(
                    (
                        mm(scores, key),
                        mm(scores, query, TN),
                        mm(probs.astype(BF16), grad, TN),
                    )
                )
            for kind in range(3):
                both = jnp.where(low, outs[0][kind], outs[1][kind]).astype(BF16)
                packed_o[:, base + kind * part + at : base + kind * part + at + wide] = both
        back = back + mm(packed_o[:, base : base + 3 * part], weights[half, :, : 3 * part], NT)
    normed, inverse = norm_rows(tokens[...].astype(F32))
    sums_o[0:1, :] += jnp.sum(back * normed, axis=0, keepdims=True)
    sums_o[1:2, :] += jnp.sum(back, axis=0, keepdims=True)
    grads = middle + norm_back(back * norms[0:1, :], normed, inverse)
    tokens_o[0] = grads[: tokens_o.shape[1]].astype(BF16)


def weight_grad(mp_s, places, *rest, steps, rows_each):
    count = 2 * len(steps)
    sides, (other_o, mine_o), turned = rest[:count], rest[count : count + 2], rest[count + 2 :]
    half, step = pl.program_id(0), pl.program_id(1)
    begin = 0
    blocks = other_o.shape[0]
    for index, length in enumerate(steps):
        left, right, flip = sides[2 * index], sides[2 * index + 1], turned[index]

        @pl.when((half == 0) & (step == begin))
        def _(left=left, flip=flip):
            flip[...] = left[...].T

        @pl.when((step >= begin) & (step < begin + length))
        def _(right=right, flip=flip):
            product = mm(flip[...], right[...]).astype(BF16)

            @pl.when(half == 0)
            def _():
                for block in range(blocks):
                    other_o[places[blocks + block]] = product[block * rows_each : (block + 1) * rows_each]

            @pl.when(half == 1)
            def _():
                for block in range(blocks):
                    mine_o[places[block]] = product[block * rows_each : (block + 1) * rows_each]

        begin += length


def take_cells(slot_s, live_s, spots, *rest, each):
    cells, (rows_o, sums_o) = rest[:each], rest[each:]
    step = pl.program_id(0)

    @pl.when(step == 0)
    def _():
        sums_o[...] = jnp.zeros_like(sums_o)

    grid, width = cells[0].shape[1], spots.shape[1]
    per_view = rows_o.shape[1]
    cell = lax.broadcasted_iota(jnp.int32, (grid, width), 0)
    lane = lax.broadcasted_iota(jnp.int32, (grid, width), 1)
    for index in range(each):
        at = step * each + index
        live = live_s[at].astype(F32)
        place = (spots[pl.ds(at, 1), :] == cell).astype(F32)
        covered = jnp.sum(place, axis=1, keepdims=True)
        pick = (jnp.where(lane == per_view, 1.0 - covered, place) * live).astype(BF16)
        taken = mm(pick, cells[index][0], TN)
        rows_o[index] = taken[:per_view].astype(BF16)
        sums_o[0:1, :] += jnp.sum(taken[:per_view], axis=0, keepdims=True)
        sums_o[1:2, :] += taken[per_view : per_view + 1]


def put_cells(where_s, live_s, spots, mask, positions, *rest, each):
    rows, (cells_o,) = rest[:each], rest[each:]
    step = pl.program_id(0)
    grid, per_view = cells_o.shape[1], rows[0].shape[1]
    cell = lax.broadcasted_iota(jnp.int32, (grid, per_view), 0)
    for index in range(each):
        at = where_s[step * each + index]
        live = live_s[at].astype(F32)
        place = (spots[pl.ds(at, 1), :][:, :per_view] == cell).astype(F32)
        covered = jnp.sum(place, axis=1, keepdims=True)
        filled = mm(place.astype(BF16), rows[index][0]) + (1.0 - covered) * mask[...]
        cells_o[index] = (live * filled + positions[...]).astype(BF16)


def order_views(where_s, mp_s, own, theirs, out, sems):
    count = own.shape[0]
    copies = []
    for view in range(count):
        mine, other = mp_s[0] * count + view, (1 - mp_s[0]) * count + view
        copies.append(pltpu.make_async_copy(own.at[view], out.at[where_s[mine]], sems.at[view]))
        copies.append(
            pltpu.make_async_copy(theirs.at[view], out.at[where_s[other]], sems.at[count + view])
        )
    for copy in copies:
        copy.start()
    for copy in copies:
        copy.wait()


def tile_of(scalars, row):
    lane = lax.broadcasted_iota(jnp.int32, (8, 128), 1)
    line = lax.broadcasted_iota(jnp.int32, (8, 128), 0)
    tile = jnp.zeros((8, 128), F32)
    for index, value in enumerate(scalars):
        tile = jnp.where((lane == index) & (line == row), value, tile)
    return tile


def total(values):
    return jnp.sum(jnp.sum(values, axis=1, keepdims=True), axis=0, keepdims=True)


def squares_kernel(once_s, *refs):
    grads, masters, (tiles_o,) = refs[:7], refs[7:14], refs[14:]
    single = [1.0] * 5 + [once_s[0].astype(F32), 1.0]
    grad_sq, weight_sq = [], []
    for index in range(7):
        value = grads[index][...]
        grad_sq.append(total(value * value) * single[index])
        if index == 0:
            weight = sum(total(masters[0][k] * masters[0][k]) for k in range(3))
        else:
            weight = total(masters[index][...] * masters[index][...])
        weight_sq.append(weight * single[index])
    tile = tile_of(grad_sq, 0) + tile_of(weight_sq, 1)
    for peer in range(tiles_o.shape[0]):
        tiles_o[peer] = tile


def lamb_kernel(once_s, tiles, *refs):
    grads, masters, moments, squares = refs[:7], refs[7:14], refs[14:21], refs[21:28]
    outs = refs[28:]
    clip_o, moment_o, square_o, step_o = outs[:7], outs[7:14], outs[14:21], outs[21:28]
    sum_o, tiles_o = outs[28:]
    summed = jnp.sum(tiles[...], axis=0)
    sum_o[...] = summed
    lane = lax.broadcasted_iota(jnp.int32, (1, 128), 1)
    clip = jnp.sqrt(total(jnp.where(lane < 7, summed[0:1, :], 0.0)))
    factor = jnp.minimum(1.0, 0.5 * math.sqrt(PARAMS) / clip)
    single = [1.0] * 5 + [once_s[0].astype(F32), 1.0]
    update_sq = []
    for index in range(7):
        amount = jnp.zeros((1, 1), F32)
        for piece in range(3 if index == 0 else 1):
            at = piece if index == 0 else Ellipsis
            value = grads[index][...]
            if index == 0:
                width = masters[0].shape[2]
                value = value[:, piece * width : (piece + 1) * width]
            clipped = value * factor
            moment = BETA_ONE * moments[index][at] + (1.0 - BETA_ONE) * clipped
            square = BETA_TWO * squares[index][at] + (1.0 - BETA_TWO) * clipped * clipped
            step = moment / (jnp.sqrt(square) + ADAM_EPS) + DECAY_RATE * masters[index][at]
            clip_o[index][at] = clipped
            moment_o[index][at] = moment
            square_o[index][at] = square
            step_o[index][at] = step
            amount = amount + total(step * step)
        update_sq.append(amount * single[index])
    tile = tile_of(update_sq, 0)
    for peer in range(tiles_o.shape[0]):
        tiles_o[peer] = tile


def update_kernel(tiles, summed, *refs):
    masters, steps, outs = refs[:7], refs[7:14], refs[14:]
    updated_o, copy_o, (norms_o,) = outs[:7], outs[7:14], outs[14:]
    lane = lax.broadcasted_iota(jnp.int32, (1, 128), 1)
    squared = summed[...]
    clip = jnp.sqrt(total(jnp.where(lane < 7, squared[0:1, :], 0.0)))
    weight_norm = jnp.sqrt(squared[1:2, :])
    update_norm = jnp.sqrt(jnp.sum(tiles[...], axis=0)[0:1, :])
    ratio = weight_norm / (update_norm + TRUST_EPS)
    norms_o[0:1, :] = weight_norm
    norms_o[1:2, :] = update_norm
    norms_o[2:3, :] = jnp.broadcast_to(clip, (1, 128))
    for index in range(7):
        rate = LEARN_RATE * total(jnp.where(lane == index, ratio, 0.0))
        for piece in range(3 if index == 0 else 1):
            at = piece if index == 0 else Ellipsis
            updated = masters[index][at] - rate * steps[index][at]
            updated_o[index][at] = updated
            copy_o[index][at] = updated.astype(BF16)


def shape(dims, dtype=F32):
    return jax.ShapeDtypeStruct(tuple(dims), dtype)


def whole(kernel, outs, scalars, operands, **kw):
    return pl.pallas_call(
        kernel,
        out_shape=outs,
        in_specs=[pl.BlockSpec(memory_space=pltpu.SMEM)] * len(scalars)
        + [pl.BlockSpec(memory_space=pltpu.VMEM)] * len(operands),
        out_specs=[pl.BlockSpec(memory_space=pltpu.VMEM)] * len(outs),
        compiler_params=params(),
        **kw,
    )(*scalars, *operands)


def per_device(
    tokens,
    counts,
    visible,
    dest_device,
    dest_slot,
    cotangent,
    *state,
):
    masters = [state[3 * index] for index in range(7)]
    moments = [state[3 * index + 1] for index in range(7)]
    squares = [state[3 * index + 2] for index in range(7)]

    def flat_state(arrays):
        a, b, c, d, e, f, g = arrays
        return [a.transpose(1, 0, 2), b.T, c, d.T, e, f, g[:, 0, :]]

    def natural(arrays):
        a, b, c, d, e, f, g = arrays
        return [a.transpose(1, 0, 2), b.T, c, d.T, e, f, g[:, None, :]]

    masters, moments, squares = flat_state(masters), flat_state(moments), flat_state(squares)

    peers, cores = lax.axis_size("dp"), lax.axis_size("mp")
    me, core = lax.axis_index("dp"), lax.axis_index("mp")
    core_s = core.astype(jnp.int32).reshape(1)
    once_s = 1 - core_s
    model = tokens.shape[1]
    nviews, per_view = visible.shape
    episodes = counts.shape[0]
    views_each = nviews // episodes
    span = views_each * per_view
    size = -(-span // ROUND) * ROUND
    here = episodes // cores
    rows = here * size
    cells, dec = cotangent.shape[1:]
    part = masters[1].shape[1]
    hidden = masters[2].shape[1]
    shard_rows = masters[2].shape[0]
    room = (nviews + peers - 1) // peers
    npos = peers * room
    fast = peers == FAST_PEERS

    low = [m.astype(BF16) for m in masters]
    chunk_a = jnp.concatenate([low[0][0], low[0][1], low[0][2], low[1]], axis=1)
    chunk_b = low[2]
    chunk_c = jnp.concatenate([low[3], low[4]], axis=1)

    same = dest_device[:, None] == dest_device[None, :]
    earlier = jnp.arange(nviews)[None, :] < jnp.arange(nviews)[:, None]
    rank = jnp.sum((same & earlier).astype(jnp.int32), axis=1)
    where_view = (dest_device * room + rank).astype(jnp.int32)
    layout = jnp.arange(npos, dtype=jnp.int32)[:, None] == where_view[None, :]
    live_view = (
        jnp.arange(nviews, dtype=jnp.int32) % views_each < jnp.repeat(counts, views_each)
    ).astype(jnp.int32)
    details = jnp.concatenate(
        [jnp.ones((nviews, 1), jnp.int32), dest_slot[:, None], live_view[:, None], visible], axis=1
    )
    fields = details.shape[1]
    sent = jnp.dot(layout.astype(BF16), details.astype(BF16), preferred_element_type=F32)
    sent = sent.astype(BF16).reshape(peers, room * fields)
    small = jnp.concatenate([low[5].reshape(-1), low[6].reshape(-1)])
    message = jnp.concatenate(
        [sent, jnp.broadcast_to(small[None], (peers, small.shape[0]))], axis=1
    )
    message = jnp.broadcast_to(message[:, None], (peers, cores, message.shape[1]))
    message = lax.all_to_all(
        message.reshape(peers * cores, -1), AXES, split_axis=0, concat_axis=0, tiled=True
    ).reshape(peers, cores, -1)
    got = message[:, 0, : room * fields].reshape(npos, fields).astype(jnp.int32)
    nln = 4 * shard_rows
    ln_full = (
        message[:, 0, room * fields : room * fields + nln]
        .reshape(peers, 4, shard_rows)
        .transpose(1, 0, 2)
        .reshape(4, model)
        .astype(F32)
    )
    norms = jnp.concatenate([ln_full, jnp.zeros((4, model), F32)], axis=0)
    dec_full = (
        message[:, :, room * fields + nln :]
        .reshape(peers, cores, 2, dec // peers)
        .transpose(2, 1, 0, 3)
        .reshape(2, cores, dec)
        .astype(F32)
    )
    mask_token = lax.dynamic_index_in_dim(dec_full[1], core, 0, keepdims=True)
    slot_pos, live_pos = got[:, 1], got[:, 2]
    width = -(-(per_view + 1) // 8) * 8
    spots = jnp.concatenate(
        [got[:, 3:], jnp.full((npos, width - per_view), -1, jnp.int32)], axis=1
    )
    filled = (slot_pos[None, :] == jnp.arange(nviews, dtype=jnp.int32)[:, None]) & (
        got[:, 0][None, :] > 0
    )
    where_slot = jnp.sum(
        jnp.where(filled, jnp.arange(npos, dtype=jnp.int32)[None, :], 0), axis=1
    ).astype(jnp.int32)

    parts_a, parts_b, parts_c = (gather_chunk(c, peers) for c in (chunk_a, chunk_b, chunk_c))
    nparts = len(parts_a)
    table = gather_table(me, core)
    nsem = 4 * nparts if fast else 1

    each = 4
    cot_spec = lambda index: pl.BlockSpec(
        (1, cells, dec), lambda i, slot, live, index=index: (slot[i * each + index], 0, 0)
    )
    returned, dec_sums = pl.pallas_call(
        lambda *refs: take_cells(*refs, each=each),
        out_shape=[shape((npos, per_view, dec), BF16), shape((8, dec))],
        grid_spec=pltpu.PrefetchScalarGridSpec(
            num_scalar_prefetch=2,
            grid=(npos // each,),
            in_specs=[pl.BlockSpec((npos, width), lambda i, *_: (0, 0))]
            + [cot_spec(index) for index in range(each)],
            out_specs=[
                pl.BlockSpec((each, per_view, dec), lambda i, *_: (i, 0, 0)),
                pl.BlockSpec((8, dec), lambda i, *_: (0, 0)),
            ],
        ),
        compiler_params=params(),
        cost_estimate=cost(2 * npos * cells * 56 * dec, cotangent.size * 2),
        name="take_cells",
    )(slot_pos, live_pos, spots, *([cotangent] * each))
    came_mine = lax.all_to_all(returned, "dp", split_axis=0, concat_axis=0, tiled=True)
    came_theirs = swap(came_mine, peers, 0, 1)

    start = core * (here * span)
    own = lax.dynamic_slice_in_dim(tokens, start, here * span, 0).reshape(here, span, model)
    own = jnp.pad(own, ((0, 0), (0, size - span), (0, 0))).reshape(rows, model)
    smem = pl.BlockSpec(memory_space=pltpu.SMEM)
    ep = lambda cols: pl.BlockSpec((size, cols), lambda i: (i, 0))
    fixed = lambda dims: pl.BlockSpec(dims, lambda i: (0,) * len(dims))
    chunk_cols = [chunk_a.shape[1], chunk_b.shape[1], chunk_c.shape[1]]
    weight_bytes = [2 * 2 * model * cols for cols in chunk_cols]
    first, packed, attended, middle, second, lse = pl.pallas_call(
        lambda *refs: attn_forward(*refs, nparts=nparts, per_view=per_view, part=part),
        grid=(here,),
        out_shape=[
            shape((rows, model), BF16),
            shape((rows, 6 * part), BF16),
            shape((rows, 2 * part), BF16),
            shape((rows, model)),
            shape((rows, model), BF16),
            shape((rows, 2 * HEADDIM)),
        ],
        in_specs=[smem, smem, smem, ep(model), fixed((8, model))] + [any_spec()] * nparts,
        out_specs=[ep(model), ep(6 * part), ep(2 * part), ep(model), ep(model), ep(2 * HEADDIM)],
        scratch_shapes=[
            pltpu.VMEM((2, model, chunk_cols[0]), BF16),
            pltpu.SemaphoreType.DMA((nsem,)),
        ],
        compiler_params=params(),
        cost_estimate=cost(3 * 2 * rows * model * 8 * part, weight_bytes[0] + rows * model * 16),
        name="attn_forward",
    )(core_s, counts, table, own, norms, *parts_a)

    group = 2
    chunk = group * size
    steps = here // group
    gviews = group * views_each
    blk = lambda cols: pl.BlockSpec((chunk, cols), lambda i: (i, 0))
    wide = 512 if hidden % 512 == 0 else hidden
    mlp_scratch = [
        pltpu.VMEM((2, model, chunk_cols[1]), BF16),
        pltpu.VMEM((2, model, chunk_cols[2]), BF16),
    ]
    act, slope, final, emb_keep, emb_send = pl.pallas_call(
        lambda *refs: mlp_forward(
            *refs, nparts=nparts, per_view=per_view, part=hidden, wide=wide, rows_each=size
        ),
        grid=(steps,),
        out_shape=[
            shape((rows, 2 * hidden), BF16),
            shape((rows, 2 * hidden), BF16),
            shape((rows, model), BF16),
            shape((steps * gviews, per_view, dec), BF16),
            shape((steps * gviews, per_view, dec), BF16),
        ],
        in_specs=[smem, smem, blk(model), blk(model), fixed((2, dec))] + [any_spec()] * (2 * nparts),
        out_specs=[
            blk(2 * hidden),
            blk(2 * hidden),
            blk(model),
            pl.BlockSpec((gviews, per_view, dec), lambda i: (i, 0, 0)),
            pl.BlockSpec((gviews, per_view, dec), lambda i: (i, 0, 0)),
        ],
        scratch_shapes=mlp_scratch + [pltpu.SemaphoreType.DMA((nsem,))] * 2,
        compiler_params=params(),
        cost_estimate=cost(
            4 * rows * model * 2 * hidden, weight_bytes[1] + weight_bytes[2] + rows * hidden * 8
        ),
        name="mlp_forward",
    )(core_s, table, second, middle, dec_full[0], *parts_b, *parts_c)

    emb_other = swap(emb_send, peers, 0, 1)
    outgoing = pl.pallas_call(
        order_views,
        out_shape=shape((npos, per_view, dec), BF16),
        in_specs=[smem, smem, any_spec(), any_spec()],
        out_specs=any_spec(),
        scratch_shapes=[pltpu.SemaphoreType.DMA((nviews,))],
        compiler_params=params(8 << 20),
        cost_estimate=cost(0, 4 * nviews * per_view * dec),
        name="order_views",
    )(where_view, core_s, emb_keep, emb_other)
    arrived = lax.all_to_all(outgoing, "dp", split_axis=0, concat_axis=0, tiled=True)

    where_mine = lax.dynamic_slice_in_dim(where_view, core * (nviews // cores), nviews // cores)
    emb_rows, glow, gpre, gmid, gmid_low, ln_two = pl.pallas_call(
        lambda *refs: mlp_backward(
            *refs, nparts=nparts, per_view=per_view, part=hidden, wide=wide, rows_each=size
        ),
        grid=(steps,),
        out_shape=[
            shape((rows, 2 * dec), BF16),
            shape((rows, model), BF16),
            shape((rows, 2 * hidden), BF16),
            shape((rows, model)),
            shape((rows, model), BF16),
            shape((8, model)),
        ],
        in_specs=[smem, smem, smem, any_spec(), any_spec(), blk(2 * hidden), blk(model), fixed((8, model))]
        + [any_spec()] * (2 * nparts),
        out_specs=[blk(2 * dec), blk(model), blk(2 * hidden), blk(model), blk(model), fixed((8, model))],
        scratch_shapes=mlp_scratch
        + [
            pltpu.VMEM((2, gviews, per_view, dec), BF16),
            pltpu.VMEM((chunk, 2 * dec), F32),
            pltpu.SemaphoreType.DMA((nsem,)),
            pltpu.SemaphoreType.DMA((nsem,)),
            pltpu.SemaphoreType.DMA((2, gviews)),
        ],
        compiler_params=params(),
        cost_estimate=cost(
            4 * rows * model * 2 * hidden, weight_bytes[1] + weight_bytes[2] + rows * hidden * 8
        ),
        name="mlp_backward",
    )(core_s, where_mine, table, came_mine, came_theirs, slope, middle, norms, *parts_b, *parts_c)

    blocks = FAST_PEERS
    if fast:
        places = jnp.concatenate([place_table(me, core), place_table(me, 1 - core)])
    else:
        places = jnp.tile(jnp.arange(blocks, dtype=jnp.int32), 2)

    def grads_of(pairs, block, name):
        lengths = [right.shape[1] // 2 // block for _, right in pairs]
        many = sum(lengths)
        begins = [sum(lengths[:index]) for index in range(len(lengths))]

        def column(begin, length):
            def at(h, j, core_ref, places_ref):
                side = jnp.where(h == 0, 1 - core_ref[0], core_ref[0])
                return (0, side * length + jnp.clip(j - begin, 0, length - 1))

            return at

        in_specs, operands = [], []
        for (left, right), begin, length in zip(pairs, begins, lengths):
            in_specs += [
                pl.BlockSpec((rows, model), lambda h, j, *_: (0, 0)),
                pl.BlockSpec((rows, block), column(begin, length)),
            ]
            operands += [left, right]
        other, mine = pl.pallas_call(
            lambda *refs: weight_grad(*refs, steps=lengths, rows_each=model // blocks),
            out_shape=[shape((blocks, model // blocks, many * block), BF16)] * 2,
            grid_spec=pltpu.PrefetchScalarGridSpec(
                num_scalar_prefetch=2,
                grid=(2, many),
                in_specs=in_specs,
                out_specs=[
                    pl.BlockSpec(
                        (blocks, model // blocks, block),
                        lambda h, j, *_: (0, 0, jnp.where(h == 0, j, many - 1)),
                    ),
                    pl.BlockSpec(
                        (blocks, model // blocks, block),
                        lambda h, j, *_: (0, 0, jnp.where(h == 0, 0, j)),
                    ),
                ],
                scratch_shapes=[pltpu.VMEM((model, rows), BF16)] * len(pairs),
            ),
            compiler_params=params(),
            cost_estimate=cost(
                4 * rows * model * many * block, 2 * rows * (2 * many * block + model)
            ),
            name=name,
        )(core_s, places, *operands)
        return scatter_chunk(mine, other, peers)

    sum_c = grads_of([(glow, act), (final, emb_rows)], 256, "grad_down_emb")
    sum_b = grads_of([(second, gpre)], 512, "grad_up")

    grad_packed, grad_own, ln_one = pl.pallas_call(
        lambda *refs: attn_backward(*refs, nparts=nparts, per_view=per_view, part=part),
        grid=(here,),
        out_shape=[
            shape((rows, 6 * part), BF16),
            shape((here, span, model), BF16),
            shape((8, model)),
        ],
        in_specs=[smem, smem, smem, ep(model), ep(6 * part), ep(2 * HEADDIM), ep(model), fixed((8, model))]
        + [any_spec()] * nparts,
        out_specs=[
            ep(6 * part),
            pl.BlockSpec((1, span, model), lambda i: (i, 0, 0)),
            fixed((8, model)),
        ],
        scratch_shapes=[
            pltpu.VMEM((2, model, chunk_cols[0]), BF16),
            pltpu.SemaphoreType.DMA((nsem,)),
        ],
        compiler_params=params(),
        cost_estimate=cost(4 * 2 * rows * model * 8 * part, weight_bytes[0] + rows * model * 16),
        name="attn_backward",
    )(core_s, counts, table, own, packed, lse, gmid, norms, *parts_a)
    sum_a = grads_of([(first, grad_packed), (gmid_low, attended)], part, "grad_in_out")

    grad_other = swap(grad_own, peers, 0, 1)
    grad_tokens = jnp.where(
        core == 0,
        jnp.concatenate([grad_own, grad_other]),
        jnp.concatenate([grad_other, grad_own]),
    ).reshape(tokens.shape)

    ln_sums = jnp.concatenate([ln_one[:2], ln_two[:2]])
    ln_send = ln_sums.reshape(4, peers, shard_rows).transpose(1, 0, 2).reshape(peers, nln)
    dec_send = dec_sums[:2].reshape(2, peers, dec // peers).transpose(1, 0, 2).reshape(peers, -1)
    small_send = jnp.concatenate([ln_send, dec_send], axis=1)
    small_send = jnp.broadcast_to(small_send[:, None], (peers, cores, small_send.shape[1]))
    small_got = lax.all_to_all(
        small_send.reshape(peers * cores, -1), AXES, split_axis=0, concat_axis=0, tiled=True
    ).reshape(peers, cores, -1)
    grad_ln = jnp.sum(small_got[:, :, :nln], axis=(0, 1)).reshape(4, shard_rows)
    grad_dec = jnp.sum(
        lax.dynamic_index_in_dim(small_got[:, :, nln:], core, 1, keepdims=False), axis=0
    ).reshape(2, dec // peers)

    positions = lax.dynamic_slice_in_dim(
        grid_positions(math.isqrt(cells), dec * cores), core * dec, dec, 1
    )
    row_spec = lambda index: pl.BlockSpec(
        (1, per_view, dec), lambda i, where, live, index=index: (where[i * each + index], 0, 0)
    )
    decoded = pl.pallas_call(
        lambda *refs: put_cells(*refs, each=each),
        out_shape=shape((nviews, cells, dec), BF16),
        grid_spec=pltpu.PrefetchScalarGridSpec(
            num_scalar_prefetch=2,
            grid=(nviews // each,),
            in_specs=[
                pl.BlockSpec((npos, width), lambda i, *_: (0, 0)),
                pl.BlockSpec((1, dec), lambda i, *_: (0, 0)),
                pl.BlockSpec((cells, dec), lambda i, *_: (0, 0)),
            ]
            + [row_spec(index) for index in range(each)],
            out_specs=pl.BlockSpec((each, cells, dec), lambda i, *_: (i, 0, 0)),
        ),
        compiler_params=params(),
        cost_estimate=cost(2 * nviews * cells * 56 * dec, cotangent.size * 2),
        name="put_cells",
    )(where_slot, live_pos, spots, mask_token, positions, *([arrived] * each))

    grads = [
        sum_a[:, : 3 * part],
        sum_a[:, 3 * part :],
        sum_b,
        sum_c[:, :hidden],
        sum_c[:, hidden:],
        grad_ln,
        grad_dec,
    ]
    world = peers * cores
    (tiles,) = whole(squares_kernel, [shape((world, 8, 128))], [once_s], grads + masters, name="squares")
    tiles = lax.all_to_all(tiles, AXES, split_axis=0, concat_axis=0, tiled=True)
    same_shapes = [shape(m.shape) for m in masters]
    lamb = whole(
        lamb_kernel,
        same_shapes * 4 + [shape((8, 128)), shape((world, 8, 128))],
        [once_s],
        [tiles] + grads + masters + moments + squares,
        name="lamb",
    )
    summed = lamb[28]
    steps_tiles = lax.all_to_all(lamb[29], AXES, split_axis=0, concat_axis=0, tiled=True)
    update = whole(
        update_kernel,
        same_shapes + [shape(m.shape, BF16) for m in masters] + [shape((8, 128))],
        [],
        [steps_tiles, summed] + masters + list(lamb[21:28]),
        name="update",
    )
    results = [
        natural(group)
        for group in (lamb[:7], lamb[7:14], lamb[14:21], update[:7], update[7:14])
    ]
    outs = [decoded, grad_tokens, update[14][2, :1], update[14][:2, :7]]
    for index in range(7):
        outs += [group[index] for group in results]
    return tuple(outs)


def solution(mesh):
    tensor_specs = [
        P("dp", None, "mp"),
        P("mp", "dp"),
        P("dp", "mp"),
        P("mp", "dp"),
        P("dp", "mp"),
        P(None, "dp"),
        P(None, "mp", "dp"),
    ]
    in_specs = (
        P("dp", None),
        P("dp"),
        P("dp", None),
        P("dp"),
        P("dp"),
        P("dp", None, "mp"),
    ) + tuple(spec for spec in tensor_specs for _ in range(3))
    out_specs = (P("dp", None, "mp"), P("dp", None), P(), P()) + tuple(
        spec for spec in tensor_specs for _ in range(5)
    )
    return jax.shard_map(
        per_device, mesh=mesh, in_specs=in_specs, out_specs=out_specs, check_vma=False
    )
```

```python
import math

import jax
import jax.numpy as jnp
from jax import lax
from jax.experimental import pallas as pl
from jax.experimental.pallas import tpu as pltpu
from jax.sharding import PartitionSpec as P

HEADDIM = 64
PARAMS = 7475200
NORM_EPS = 1e-06
MASK_FILL = -1e30
BETA_ONE = 0.5
BETA_TWO = 0.5
ADAM_EPS = 1e-06
DECAY_RATE = 0.01
LEARN_RATE = 0.5
TRUST_EPS = 1e-06

F32 = jnp.float32
BF16 = jnp.bfloat16
AXES = ("dp", "mp")
NT = (((1,), (1,)), ((), ()))
TN = (((0,), (0,)), ((), ()))
ROUND = 16
VMEM_BYTES = 58 << 20


def mm(a, b, dims=(((1,), (0,)), ((), ()))):
    return lax.dot_general(a, b, dims, preferred_element_type=F32)


def norm_rows(values):
    centre = values - jnp.mean(values, axis=-1, keepdims=True)
    spread = jnp.mean(centre * centre, axis=-1, keepdims=True)
    inverse = lax.rsqrt(spread + NORM_EPS)
    return centre * inverse, inverse


def norm_back(scaled, normed, inverse):
    return inverse * (
        scaled
        - jnp.mean(scaled, axis=-1, keepdims=True)
        - normed * jnp.mean(scaled * normed, axis=-1, keepdims=True)
    )


def grid_positions(side, width):
    quarter = width // 4
    rate = 1.0 / 10000.0 ** (jnp.arange(quarter, dtype=F32) / quarter)
    place = jnp.arange(side * side, dtype=jnp.int32)
    row_pos = (place // side).astype(F32)
    col_pos = (place % side).astype(F32)
    row_angle = row_pos[:, None] * rate[None, :]
    col_angle = col_pos[:, None] * rate[None, :]
    return jnp.concatenate(
        [jnp.sin(row_angle), jnp.cos(row_angle), jnp.sin(col_angle), jnp.cos(col_angle)], axis=1
    )


def any_spec():
    return pl.BlockSpec(memory_space=pl.ANY)


def params(limit=VMEM_BYTES):
    return pltpu.CompilerParams(vmem_limit_bytes=limit)


def cost(flops, nbytes):
    return pl.CostEstimate(flops=int(flops), bytes_accessed=int(nbytes), transcendentals=0)


def swap(array, peers, bits, core=0):
    bits = bits if isinstance(bits, tuple) else (bits, bits)
    pairs = [
        (d * 2 + m, (d ^ bits[m]) * 2 + (m ^ core)) for d in range(peers) for m in range(2)
    ]
    return lax.ppermute(array, AXES, pairs)


FAST_PEERS = 16
Z_STEPS = (4, 8, 12)


def after(array, *others):
    return lax.optimization_barrier((array,) + others)[0]


def reach_z(shard, peers):
    return [swap(shard, peers, bits) for bits in Z_STEPS]


def hold_all(arrays, others):
    return list(lax.optimization_barrier((tuple(arrays), tuple(others)))[0])


def gather_plain(shard):
    return [lax.all_gather(lax.all_gather(shard, "dp", axis=0, tiled=True), "mp", axis=0)]


class Gather:
    def __init__(self, shards, peers):
        self.peers = peers
        self.one, self.two, self.three = shards

    def near(self, array):
        return swap(array, self.peers, (1, 2))

    def far(self, array):
        return swap(array, self.peers, (2, 1))

    def across(self, array):
        return swap(array, self.peers, 0, 1)

    def begin(self, beside_z, beside_near):
        z_one = reach_z(self.one, self.peers)
        (along_one,) = hold_all([jnp.stack([self.one] + z_one)], beside_z)
        (two,) = hold_all([self.two], z_one)
        near_one, z_two = self.near(along_one), reach_z(two, self.peers)
        done = [near_one] + z_two + list(beside_near(along_one))
        half_one, along_two, three = hold_all(
            [jnp.concatenate([along_one, near_one]), jnp.stack([two] + z_two), self.three], done
        )
        far_one, side_one = self.far(half_one), self.across(half_one)
        near_two, z_three = self.near(along_two), reach_z(three, self.peers)
        far_one, half_two, along_three = hold_all(
            [far_one, jnp.concatenate([along_two, near_two]), jnp.stack([three] + z_three)],
            [far_one, near_two] + z_three,
        )
        self.half_two, self.along_three = half_two, along_three
        self.far_two, self.side_two = self.far(half_two), self.across(half_two)
        self.near_three = self.near(along_three)
        return [half_one, far_one, side_one, self.across(far_one)]

    def later(self):
        return [self.far_two, self.near_three, self.side_two]

    def second(self, beside):
        far_two, along_three, near_three = hold_all(
            [self.far_two, self.along_three, self.near_three], [beside]
        )
        self.half_three = jnp.concatenate([along_three, near_three])
        self.far_three, self.side_three = self.far(self.half_three), self.across(self.half_three)
        self.parts_two = [self.half_two, far_two, self.side_two, self.across(far_two)]

    def finish(self, beside):
        (far_three,) = hold_all([self.far_three], [beside] + self.parts_two[2:])
        parts_three = [self.half_three, far_three, self.side_three, self.across(far_three)]
        return self.parts_two, parts_three


PIECE = 8


def gather_table(me, core):
    one = jnp.where(core == 0, 1, 2)
    two = 3 - one
    along = jnp.array((0,) + Z_STEPS, jnp.int32)
    mine = jnp.concatenate([along, along ^ one])
    theirs = jnp.concatenate([along, along ^ two])
    apart = jnp.concatenate([mine, mine ^ two, theirs, theirs ^ one])
    cores = jnp.stack([core, core, 1 - core, 1 - core])
    return jnp.concatenate([me ^ apart, cores]).astype(jnp.int32)


def weight_copies(parts, table, target, sems):
    if len(parts) == 1:
        return [pltpu.make_async_copy(parts[0], target, sems.at[0])]
    copies = []
    for index, part in enumerate(parts):
        half = table[len(parts) * PIECE + index]
        for inner in range(PIECE):
            at = index * PIECE + inner
            rows = part.shape[1]
            start = pl.multiple_of(table[at] * rows, ROUND)
            copies.append(
                pltpu.make_async_copy(
                    part.at[inner], target.at[half, pl.ds(start, rows), :], sems.at[at]
                )
            )
    return copies


def place_table(me, core):
    near = jnp.where(core == 0, 2, 1)
    far = 3 - near
    apart = jnp.arange(FAST_PEERS, dtype=jnp.int32) ^ me
    return (
        jnp.where((apart & near) != 0, 8, 0) + jnp.where((apart & far) != 0, 4, 0) + (apart >> 2)
    ).astype(jnp.int32)


def add(*terms):
    return sum(term.astype(F32) for term in terms)


def leaf(send):
    return send[0] if isinstance(send, tuple) else send


def scatter_start(pair, peers):
    mine, got = pair
    if peers != FAST_PEERS:
        return [mine, got]
    return [(mine, got), add(mine[8:], got[8:]).astype(BF16)]


def scatter_near(state, peers, *held):
    if peers != FAST_PEERS:
        return state
    terms, send = state
    got = swap(leaf(send), peers, (2, 1))
    terms = terms + (after(got, *held) if held else got,)
    return [terms, add(*(term[4:8] for term in terms)).astype(BF16)]


def scatter_far(state, peers, *held):
    if peers != FAST_PEERS:
        return state
    terms, send = state
    got = swap(leaf(send), peers, (1, 2))
    terms = terms + (after(got, *held) if held else got,)
    return [terms, tuple(add(*(term[i] for term in terms)).astype(BF16) for i in (1, 2, 3))]


def scatter_end(state, peers, *held):
    if peers != FAST_PEERS:
        mine, got = state
        whole = mine.astype(F32) + got.astype(F32)
        return lax.psum_scatter(
            whole.reshape(-1, whole.shape[-1]), "dp", scatter_dimension=0, tiled=True
        )
    terms, sends = state
    last = [swap(send, peers, bits) for send, bits in zip(sends, Z_STEPS)]
    last = hold_all(last, held) if held else last
    return add(*(term[0] for term in terms), *last)


def view_of(rows, per_view):
    view = jnp.zeros_like(rows)
    for edge in range(1, 5):
        view = view + (rows >= edge * per_view).astype(jnp.int32)
    return view


def allowed_bias(size, count, per_view):
    query = view_of(lax.broadcasted_iota(jnp.int32, (size, size), 0), per_view)
    key = view_of(lax.broadcasted_iota(jnp.int32, (size, size), 1), per_view)
    return jnp.where((key < count) | (key == query), 0.0, MASK_FILL)


def pair_masks(scale):
    lane = lax.broadcasted_iota(jnp.int32, (1, 2 * HEADDIM), 1)
    low = (lane < HEADDIM).astype(F32)
    return (low * scale).astype(BF16), ((1.0 - low) * scale).astype(BF16)


def attn_forward(mp_s, counts_s, table, tokens, norms, *rest, nparts, per_view, part, begin, here):
    parts = rest[:nparts]
    first_o, packed_o, attended_o, middle_o, second_o, lse_o, weights, sems = rest[-8:]
    step = pl.program_id(0)
    copies = weight_copies(parts, table, weights, sems)

    @pl.when(step == 0)
    def _():
        for copy in copies:
            copy.start()
        for copy in copies:
            copy.wait()

    size = tokens.shape[0]
    scale = 1.0 / math.sqrt(HEADDIM)
    values = tokens[...].astype(F32)
    normed, _ = norm_rows(values)
    first = (normed * norms[0:1, :] + norms[1:2, :]).astype(BF16)
    first_o[...] = first
    bias = allowed_bias(size, counts_s[mp_s[0] * here + begin + step], per_view)
    bias = jnp.concatenate([bias, bias], axis=0)
    masks = pair_masks(scale)
    lane = lax.broadcasted_iota(jnp.int32, (size, 2 * HEADDIM), 1)
    wide = 2 * HEADDIM
    lse = jnp.zeros((size, wide), F32)
    attn = jnp.zeros(values.shape, F32)
    for half in range(2):
        packed = mm(first, weights[half, :, : 3 * part]).astype(BF16)
        packed_o[:, half * 3 * part : (half + 1) * 3 * part] = packed
        pairs = range(part // wide)
        logits, probs = [], []
        for pair in pairs:
            at = pair * wide
            query = packed[:, at : at + wide]
            key = packed[:, part + at : part + at + wide]
            both = jnp.concatenate([query * masks[0], query * masks[1]], axis=0)
            logits.append(mm(both, key, NT) + bias)
        for pair in pairs:
            top = jnp.max(logits[pair], axis=-1, keepdims=True)
            exponent = jnp.exp(logits[pair] - top)
            total = jnp.sum(exponent, axis=-1, keepdims=True)
            probs.append((exponent * (1.0 / total)).astype(BF16))
            top = top + jnp.log(total)
            index = half * (part // HEADDIM) + pair * 2
            lse = jnp.where(lane == index, top[:size], lse)
            lse = jnp.where(lane == index + 1, top[size:], lse)
        for pair in pairs:
            at = pair * wide
            outs = mm(probs[pair], packed[:, 2 * part + at : 2 * part + at + wide])
            both = jnp.where(lane < HEADDIM, outs[:size], outs[size:]).astype(BF16)
            attended_o[:, half * part + at : half * part + at + wide] = both
        attn = attn + mm(
            attended_o[:, half * part : (half + 1) * part], weights[half, :, 3 * part :], NT
        )
    lse_o[...] = lse
    middle = values + attn
    middle_o[...] = middle
    normed, _ = norm_rows(middle)
    second_o[...] = (normed * norms[2:3, :] + norms[3:4, :]).astype(BF16)


def mlp_forward(mp_s, table, second, middle, dec_bias, *rest, nparts, per_view, part, wide, rows_each):
    up_parts, down_parts = rest[:nparts], rest[nparts : 2 * nparts]
    act_o, slope_o, final_o, keep_o, send_o = rest[2 * nparts : 2 * nparts + 5]
    up, down, up_sems, down_sems = rest[2 * nparts + 5 :]
    copies = weight_copies(up_parts, table, up, up_sems) + weight_copies(
        down_parts, table, down, down_sems
    )

    @pl.when(pl.program_id(0) == 0)
    def _():
        for copy in copies:
            copy.start()
        for copy in copies:
            copy.wait()

    acc = middle[...]
    rows = second[...]
    for half in range(2):
        for start in range(0, part, wide):
            pre = mm(rows, up[half, :, start : start + wide])
            cumulative = 0.5 * (1.0 + lax.erf(pre * (1.0 / math.sqrt(2.0))))
            act = (pre * cumulative).astype(BF16)
            slope = cumulative + pre * jnp.exp(-0.5 * pre * pre) * (1.0 / math.sqrt(2.0 * math.pi))
            act_o[:, half * part + start : half * part + start + wide] = act
            slope_o[:, half * part + start : half * part + start + wide] = slope.astype(BF16)
            acc = acc + mm(act, down[half, :, start : start + wide], NT)
    final = acc.astype(BF16)
    final_o[...] = final
    outs = [
        mm(final, down[half, :, part:]) + dec_bias[half : half + 1, :] for half in range(2)
    ]
    mine = jnp.where(mp_s[0] == 0, outs[0], outs[1])
    theirs = jnp.where(mp_s[0] == 0, outs[1], outs[0])
    views = rows_each // per_view
    for view in range(keep_o.shape[0]):
        at = (view // views) * rows_each + (view % views) * per_view
        keep_o[view] = mine[at : at + per_view].astype(BF16)
        send_o[view] = theirs[at : at + per_view].astype(BF16)


def mlp_backward(
    mp_s, where_s, table, mine, theirs, slope, middle, norms, *rest, nparts, per_view, part, wide, rows_each
):
    up_parts, down_parts = rest[:nparts], rest[nparts : 2 * nparts]
    rows_o, low_o, pre_o, mid_o, midlow_o, sums_o = rest[2 * nparts : 2 * nparts + 6]
    up, down, pieces, flat, up_sems, down_sems, piece_sems = rest[2 * nparts + 6 :]
    step = pl.program_id(0)
    nviews = pieces.shape[1]
    copies = weight_copies(up_parts, table, up, up_sems) + weight_copies(
        down_parts, table, down, down_sems
    )
    fetch = []
    for view in range(nviews):
        at = where_s[step * nviews + view]
        fetch.append(
            pltpu.make_async_copy(mine.at[at], pieces.at[mp_s[0], view], piece_sems.at[0, view])
        )
        fetch.append(
            pltpu.make_async_copy(theirs.at[at], pieces.at[1 - mp_s[0], view], piece_sems.at[1, view])
        )
    for copy in fetch:
        copy.start()

    @pl.when(step == 0)
    def _():
        for copy in copies:
            copy.start()
        flat[...] = jnp.zeros_like(flat)
        sums_o[...] = jnp.zeros_like(sums_o)
        for copy in copies:
            copy.wait()

    for copy in fetch:
        copy.wait()
    dec = pieces.shape[3]
    views = rows_each // per_view
    for view in range(nviews):
        at = (view // views) * rows_each + (view % views) * per_view
        for half in range(2):
            flat[at : at + per_view, half * dec : (half + 1) * dec] = pieces[half, view].astype(F32)
    rows = flat[...].astype(BF16)
    rows_o[...] = rows
    final = mm(rows[:, :dec], down[0, :, part:], NT) + mm(rows[:, dec:], down[1, :, part:], NT)
    low = final.astype(BF16)
    low_o[...] = low
    acc = jnp.zeros(final.shape, F32)
    for half in range(2):
        for start in range(0, part, wide):
            at = half * part + start
            hidden = mm(low, down[half, :, start : start + wide])
            pre = (hidden * slope[:, at : at + wide].astype(F32)).astype(BF16)
            pre_o[:, at : at + wide] = pre
            acc = acc + mm(pre, up[half, :, start : start + wide], NT)
    normed, inverse = norm_rows(middle[...])
    sums_o[0:1, :] += jnp.sum(acc * normed, axis=0, keepdims=True)
    sums_o[1:2, :] += jnp.sum(acc, axis=0, keepdims=True)
    mid = final + norm_back(acc * norms[2:3, :], normed, inverse)
    mid_o[...] = mid
    midlow_o[...] = mid.astype(BF16)


def attn_backward(
    mp_s, counts_s, table, tokens, packed, lse, mid, norms, *rest, nparts, per_view, part, begin, here
):
    parts = rest[:nparts]
    packed_o, tokens_o, sums_o, weights, sems = rest[-5:]
    step = pl.program_id(0)
    copies = weight_copies(parts, table, weights, sems)

    @pl.when(step == 0)
    def _():
        for copy in copies:
            copy.start()
        sums_o[...] = jnp.zeros_like(sums_o)
        for copy in copies:
            copy.wait()

    size = tokens.shape[0]
    scale = 1.0 / math.sqrt(HEADDIM)
    wide = 2 * HEADDIM
    bias = allowed_bias(size, counts_s[mp_s[0] * here + begin + step], per_view)
    bias = jnp.concatenate([bias, bias], axis=0)
    masks = pair_masks(1.0)
    lane = lax.broadcasted_iota(jnp.int32, (size, wide), 1)
    low = lane < HEADDIM
    middle = mid[...]
    middle_low = middle.astype(BF16)
    back = jnp.zeros(middle.shape, F32)
    for half in range(2):
        grad_att = mm(middle_low, weights[half, :, 3 * part :]).astype(BF16)
        base = half * 3 * part
        pairs = range(part // wide)
        sides, logits, grad_probs, lows = [], [], [], []
        for pair in pairs:
            at = pair * wide
            query = packed[:, base + at : base + at + wide]
            key = packed[:, base + part + at : base + part + at + wide]
            value = packed[:, base + 2 * part + at : base + 2 * part + at + wide]
            grad = grad_att[:, at : at + wide]
            query = jnp.concatenate([query * masks[0], query * masks[1]], axis=0)
            grad = jnp.concatenate([grad * masks[0], grad * masks[1]], axis=0)
            sides.append((query, key, grad))
            logits.append(mm(query, key, NT) * scale + bias)
            grad_probs.append(mm(grad, value, NT))
        for pair in pairs:
            index = half * (part // HEADDIM) + pair * 2
            top = jnp.concatenate([lse[:, index : index + 1], lse[:, index + 1 : index + 2]], axis=0)
            probs = jnp.exp(logits[pair] - top)
            weighted = probs * grad_probs[pair]
            centre = jnp.sum(weighted, axis=-1, keepdims=True)
            scores = ((weighted - probs * centre) * scale).astype(BF16)
            lows.append((scores, probs.astype(BF16)))
        for pair in pairs:
            query, key, grad = sides[pair]
            scores, probs = lows[pair]
            at = base + pair * wide
            grad_query = mm(scores, key)
            packed_o[:, at : at + wide] = jnp.where(
                low, grad_query[:size], grad_query[size:]
            ).astype(BF16)
            at = at + part
            packed_o[:, at : at + wide] = mm(scores, query, TN).astype(BF16)
            at = at + part
            packed_o[:, at : at + wide] = mm(probs, grad, TN).astype(BF16)
        back = back + mm(packed_o[:, base : base + 3 * part], weights[half, :, : 3 * part], NT)
    normed, inverse = norm_rows(tokens[...].astype(F32))
    sums_o[0:1, :] += jnp.sum(back * normed, axis=0, keepdims=True)
    sums_o[1:2, :] += jnp.sum(back, axis=0, keepdims=True)
    grads = middle + norm_back(back * norms[0:1, :], normed, inverse)
    tokens_o[0] = grads[: tokens_o.shape[1]].astype(BF16)


def weight_grad(side_s, places, *rest, steps, rows_each):
    count = len(steps)
    sides, (grads_o, left_pad, right_pad) = rest[: 2 * count], rest[2 * count :]
    step = pl.program_id(0)
    begin = 0
    blocks = grads_o.shape[0]

    @pl.when(step == 0)
    def _():
        left_pad[...] = jnp.zeros_like(left_pad)
        right_pad[...] = jnp.zeros_like(right_pad)

    for index, length in enumerate(steps):
        left, right = sides[2 * index], sides[2 * index + 1]

        @pl.when(step == begin)
        def _(left=left):
            left_pad[: left.shape[0], :] = left[...]

        @pl.when((step >= begin) & (step < begin + length))
        def _(right=right):
            right_pad[: right.shape[0], :] = right[...]

        begin += length
    product = mm(left_pad[...], right_pad[...], TN).astype(BF16)
    for block in range(blocks):
        grads_o[places[block]] = product[block * rows_each : (block + 1) * rows_each]


def take_cells(where_s, marks, live_row, cells, rows_o, sums_o, *, per_view, stride):
    step = pl.program_id(0)

    @pl.when(step == 0)
    def _():
        sums_o[...] = jnp.zeros_like(sums_o)

    grid, each, dec = cells.shape
    flat = cells[...].reshape(grid * each, dec)
    lane = lax.broadcasted_iota(jnp.int32, (each * stride, grid * each), 1)
    pick = (marks[...] == lane).astype(F32)
    covered = jnp.sum(pick, axis=0, keepdims=True)
    open_cells = jnp.broadcast_to(live_row[0] - covered, (8, grid * each)).astype(BF16)
    taken = mm(pick.astype(BF16), flat)
    masked = mm(open_cells, flat)
    for index in range(each):
        rows_o[where_s[step * each + index]] = taken[index * stride : index * stride + per_view].astype(BF16)
    sums_o[0:1, :] += jnp.sum(taken, axis=0, keepdims=True)
    sums_o[1:2, :] += masked[0:1]


def put_cells(where_s, live_s, marks, mask, positions, rows, cells_o, held):
    step = pl.program_id(0)
    grid, each, dec = cells_o.shape
    per_view = rows.shape[1]
    stride = held.shape[0] // each

    @pl.when(step == 0)
    def _():
        held[...] = jnp.zeros_like(held)

    slot = lax.broadcasted_iota(jnp.int32, (1, each, 1), 1)
    live = jnp.zeros((1, each, 1), F32)
    for index in range(each):
        at = step * each + index
        held[index * stride : index * stride + per_view, :] = rows[where_s[at]]
        live = jnp.where(slot == index, live_s[at].astype(F32), live)
    line = lax.broadcasted_iota(jnp.int32, (grid * each, held.shape[0]), 0)
    place = (marks[0] == line).astype(F32)
    covered = jnp.sum(place, axis=1, keepdims=True)
    live = jnp.broadcast_to(live, (grid, each, 1)).reshape(grid * each, 1)
    filled = mm(place.astype(BF16), held[...]) + (live - covered) * mask[...]
    filled = filled.reshape(grid, each, dec) + positions[...][:, None, :]
    cells_o[...] = filled.astype(BF16)


def order_views(where_s, mp_s, own, theirs, out, sems):
    count = own.shape[0]
    copies = []
    for view in range(count):
        mine, other = mp_s[0] * count + view, (1 - mp_s[0]) * count + view
        copies.append(pltpu.make_async_copy(own.at[view], out.at[where_s[mine]], sems.at[view]))
        copies.append(
            pltpu.make_async_copy(theirs.at[view], out.at[where_s[other]], sems.at[count + view])
        )
    for copy in copies:
        copy.start()
    for copy in copies:
        copy.wait()


def tile_of(scalars, row):
    lane = lax.broadcasted_iota(jnp.int32, (8, 128), 1)
    line = lax.broadcasted_iota(jnp.int32, (8, 128), 0)
    tile = jnp.zeros((8, 128), F32)
    for index, value in enumerate(scalars):
        tile = jnp.where((lane == index) & (line == row), value, tile)
    return tile


def total(values):
    return jnp.sum(jnp.sum(values, axis=1, keepdims=True), axis=0, keepdims=True)


def squares_kernel(once_s, *refs):
    grads, masters, (tiles_o,) = refs[:7], refs[7:14], refs[14:]
    single = [1.0] * 5 + [once_s[0].astype(F32), 1.0]
    grad_sq, weight_sq = [], []
    for index in range(7):
        value = grads[index][...]
        grad_sq.append(total(value * value) * single[index])
        if index == 0:
            weight = sum(total(masters[0][k] * masters[0][k]) for k in range(3))
        else:
            weight = total(masters[index][...] * masters[index][...])
        weight_sq.append(weight * single[index])
    tile = tile_of(grad_sq, 0) + tile_of(weight_sq, 1)
    for peer in range(tiles_o.shape[0]):
        tiles_o[peer] = tile


def lamb_kernel(once_s, tiles, *refs):
    grads, masters, moments, squares = refs[:7], refs[7:14], refs[14:21], refs[21:28]
    outs = refs[28:]
    clip_o, moment_o, square_o, step_o = outs[:7], outs[7:14], outs[14:21], outs[21:28]
    sum_o, tiles_o = outs[28:]
    summed = jnp.sum(tiles[...], axis=0)
    sum_o[...] = summed
    lane = lax.broadcasted_iota(jnp.int32, (1, 128), 1)
    clip = jnp.sqrt(total(jnp.where(lane < 7, summed[0:1, :], 0.0)))
    factor = jnp.minimum(1.0, 0.5 * math.sqrt(PARAMS) / clip)
    single = [1.0] * 5 + [once_s[0].astype(F32), 1.0]
    update_sq = []
    for index in range(7):
        amount = jnp.zeros((1, 1), F32)
        for piece in range(3 if index == 0 else 1):
            at = piece if index == 0 else Ellipsis
            value = grads[index][...]
            if index == 0:
                width = masters[0].shape[2]
                value = value[:, piece * width : (piece + 1) * width]
            clipped = value * factor
            moment = BETA_ONE * moments[index][at] + (1.0 - BETA_ONE) * clipped
            square = BETA_TWO * squares[index][at] + (1.0 - BETA_TWO) * clipped * clipped
            step = moment / (jnp.sqrt(square) + ADAM_EPS) + DECAY_RATE * masters[index][at]
            clip_o[index][at] = clipped
            moment_o[index][at] = moment
            square_o[index][at] = square
            step_o[index][at] = step
            amount = amount + total(step * step)
        update_sq.append(amount * single[index])
    tile = tile_of(update_sq, 0)
    for peer in range(tiles_o.shape[0]):
        tiles_o[peer] = tile


def update_kernel(tiles, summed, *refs):
    masters, steps, outs = refs[:7], refs[7:14], refs[14:]
    updated_o, copy_o, (norms_o,) = outs[:7], outs[7:14], outs[14:]
    lane = lax.broadcasted_iota(jnp.int32, (1, 128), 1)
    squared = summed[...]
    clip = jnp.sqrt(total(jnp.where(lane < 7, squared[0:1, :], 0.0)))
    weight_norm = jnp.sqrt(squared[1:2, :])
    update_norm = jnp.sqrt(jnp.sum(tiles[...], axis=0)[0:1, :])
    ratio = weight_norm / (update_norm + TRUST_EPS)
    norms_o[0:1, :] = weight_norm
    norms_o[1:2, :] = update_norm
    norms_o[2:3, :] = jnp.broadcast_to(clip, (1, 128))
    for index in range(7):
        rate = LEARN_RATE * total(jnp.where(lane == index, ratio, 0.0))
        for piece in range(3 if index == 0 else 1):
            at = piece if index == 0 else Ellipsis
            updated = masters[index][at] - rate * steps[index][at]
            updated_o[index][at] = updated
            copy_o[index][at] = updated.astype(BF16)


def shape(dims, dtype=F32):
    return jax.ShapeDtypeStruct(tuple(dims), dtype)


def whole(kernel, outs, scalars, operands, **kw):
    return pl.pallas_call(
        kernel,
        out_shape=outs,
        in_specs=[pl.BlockSpec(memory_space=pltpu.SMEM)] * len(scalars)
        + [pl.BlockSpec(memory_space=pltpu.VMEM)] * len(operands),
        out_specs=[pl.BlockSpec(memory_space=pltpu.VMEM)] * len(outs),
        compiler_params=params(),
        **kw,
    )(*scalars, *operands)


def per_device(
    tokens,
    counts,
    visible,
    dest_device,
    dest_slot,
    cotangent,
    *state,
):
    masters = [state[3 * index] for index in range(7)]
    moments = [state[3 * index + 1] for index in range(7)]
    squares = [state[3 * index + 2] for index in range(7)]

    def flat_state(arrays):
        a, b, c, d, e, f, g = arrays
        return [a.transpose(1, 0, 2), b.T, c, d.T, e, f, g[:, 0, :]]

    def natural(arrays):
        a, b, c, d, e, f, g = arrays
        return [a.transpose(1, 0, 2), b.T, c, d.T, e, f, g[:, None, :]]

    masters, moments, squares = flat_state(masters), flat_state(moments), flat_state(squares)

    peers, cores = lax.axis_size("dp"), lax.axis_size("mp")
    me, core = lax.axis_index("dp"), lax.axis_index("mp")
    core_s = core.astype(jnp.int32).reshape(1)
    once_s = 1 - core_s
    model = tokens.shape[1]
    nviews, per_view = visible.shape
    episodes = counts.shape[0]
    views_each = nviews // episodes
    span = views_each * per_view
    size = -(-span // ROUND) * ROUND
    here = episodes // cores
    rows = here * size
    cells, dec = cotangent.shape[1:]
    part = masters[1].shape[1]
    hidden = masters[2].shape[1]
    shard_rows = masters[2].shape[0]
    room = (nviews + peers - 1) // peers
    npos = peers * room
    fast = peers == FAST_PEERS

    low = [m.astype(BF16) for m in masters]
    chunk_a = jnp.concatenate([low[0][0], low[0][1], low[0][2], low[1]], axis=1)
    chunk_b = low[2]
    chunk_c = jnp.concatenate([low[3], low[4]], axis=1)

    same = dest_device[:, None] == dest_device[None, :]
    earlier = jnp.arange(nviews)[None, :] < jnp.arange(nviews)[:, None]
    rank = jnp.sum((same & earlier).astype(jnp.int32), axis=1)
    where_view = (dest_device * room + rank).astype(jnp.int32)
    layout = jnp.arange(npos, dtype=jnp.int32)[:, None] == where_view[None, :]
    live_view = (
        jnp.arange(nviews, dtype=jnp.int32) % views_each < jnp.repeat(counts, views_each)
    ).astype(jnp.int32)
    details = jnp.concatenate(
        [jnp.ones((nviews, 1), jnp.int32), dest_slot[:, None], live_view[:, None], visible], axis=1
    )
    fields = details.shape[1]
    sent = jnp.dot(layout.astype(BF16), details.astype(BF16), preferred_element_type=F32)
    sent = sent.astype(BF16).reshape(peers, room * fields)
    small = jnp.concatenate([low[5].reshape(-1), low[6].reshape(-1)])
    message = jnp.concatenate(
        [sent, jnp.broadcast_to(small[None], (peers, small.shape[0]))], axis=1
    )
    message = jnp.broadcast_to(message[:, None], (peers, cores, message.shape[1]))
    message = lax.all_to_all(
        message.reshape(peers * cores, -1), AXES, split_axis=0, concat_axis=0, tiled=True
    ).reshape(peers, cores, -1)
    got = message[:, 0, : room * fields].reshape(npos, fields).astype(jnp.int32)
    nln = 4 * shard_rows
    ln_full = (
        message[:, 0, room * fields : room * fields + nln]
        .reshape(peers, 4, shard_rows)
        .transpose(1, 0, 2)
        .reshape(4, model)
        .astype(F32)
    )
    norms = jnp.concatenate([ln_full, jnp.zeros((4, model), F32)], axis=0)
    dec_full = (
        message[:, :, room * fields + nln :]
        .reshape(peers, cores, 2, dec // peers)
        .transpose(2, 1, 0, 3)
        .reshape(2, cores, dec)
        .astype(F32)
    )
    mask_token = lax.dynamic_index_in_dim(dec_full[1], core, 0, keepdims=True)
    held_slot = got[:, 1]
    filled = (held_slot[None, :] == jnp.arange(nviews, dtype=jnp.int32)[:, None]) & (
        got[:, 0][None, :] > 0
    )
    where_slot = jnp.sum(
        jnp.where(filled, jnp.arange(npos, dtype=jnp.int32)[None, :], 0), axis=1
    ).astype(jnp.int32)
    owned = jnp.dot(
        filled.astype(BF16), got.astype(BF16), preferred_element_type=F32
    ).astype(jnp.int32)
    live_slot, owned_spots = owned[:, 2], owned[:, 3:]
    each = 8
    groups = nviews // each
    marks = jnp.where(
        live_slot[:, None] > 0,
        owned_spots * each + (jnp.arange(nviews, dtype=jnp.int32) % each)[:, None],
        -1,
    )
    stride_take, stride_put = -(-per_view // 8) * 8, -(-per_view // 64) * 64
    take_marks = jnp.pad(marks, ((0, 0), (0, stride_take - per_view)), constant_values=-1)
    take_marks = take_marks.reshape(nviews * stride_take, 1)
    put_marks = jnp.pad(marks, ((0, 0), (0, stride_put - per_view)), constant_values=-1)
    put_marks = put_marks.reshape(groups, 1, each * stride_put)
    live_row = jnp.broadcast_to(
        live_slot.astype(F32).reshape(groups, 1, each), (groups, cells, each)
    ).reshape(groups, 1, cells * each)

    take_call = pl.pallas_call(
        lambda *refs: take_cells(*refs, per_view=per_view, stride=stride_take),
        out_shape=[shape((npos, per_view, dec), BF16), shape((8, dec))],
        grid_spec=pltpu.PrefetchScalarGridSpec(
            num_scalar_prefetch=1,
            grid=(groups,),
            in_specs=[
                pl.BlockSpec((each * stride_take, 1), lambda i, _: (i, 0)),
                pl.BlockSpec((1, 1, cells * each), lambda i, _: (i, 0, 0)),
                pl.BlockSpec((cells, each, dec), lambda i, _: (0, i, 0)),
            ],
            out_specs=[
                pl.BlockSpec((npos, per_view, dec), lambda i, _: (0, 0, 0)),
                pl.BlockSpec((8, dec), lambda i, _: (0, 0)),
            ],
        ),
        compiler_params=params(),
        cost_estimate=cost(2 * nviews * stride_take * cells * each * dec, cotangent.size * 2),
        name="take_cells",
    )

    start = core * (here * span)
    own = lax.dynamic_slice_in_dim(tokens, start, here * span, 0).reshape(here, span, model)
    own = jnp.pad(own, ((0, 0), (0, size - span), (0, 0))).reshape(rows, model)
    taken = []

    def take(*others):
        marks_held = after(take_marks, *others) if others else take_marks
        taken.extend(take_call(where_slot, marks_held, live_row, cotangent.transpose(1, 0, 2)))
        return taken[:1]

    if fast:
        gather = Gather((chunk_a, chunk_b, chunk_c), peers)
        parts_a = gather.begin((own, take_marks), take)
    else:
        take()
        parts_a = gather_plain(chunk_a)
    returned, dec_sums = taken
    nparts = len(parts_a)
    table = gather_table(me, core)
    nsem = PIECE * nparts if fast else 1

    smem = pl.BlockSpec(memory_space=pltpu.SMEM)
    fixed = lambda dims: pl.BlockSpec(dims, lambda i: (0,) * len(dims))
    chunk_cols = [chunk_a.shape[1], chunk_b.shape[1], chunk_c.shape[1]]
    weight_bytes = [2 * 2 * model * cols for cols in chunk_cols]
    calls = 2 if here % 2 == 0 else 1
    each_call = here // calls

    def attn_forward_call(call, own, earlier):
        begin = call * each_call
        ep = lambda cols: pl.BlockSpec((size, cols), lambda i: (i + begin, 0))
        return pl.pallas_call(
            lambda *refs: attn_forward(
                *refs, nparts=nparts, per_view=per_view, part=part, begin=begin, here=here
            ),
            grid=(each_call,),
            out_shape=[
                shape((rows, model), BF16),
                shape((rows, 6 * part), BF16),
                shape((rows, 2 * part), BF16),
                shape((rows, model)),
                shape((rows, model), BF16),
                shape((rows, 2 * HEADDIM)),
            ],
            in_specs=[smem, smem, smem, ep(model), fixed((8, model))]
            + [any_spec()] * (nparts + len(earlier)),
            out_specs=[ep(model), ep(6 * part), ep(2 * part), ep(model), ep(model), ep(2 * HEADDIM)],
            scratch_shapes=[
                pltpu.VMEM((2, model, chunk_cols[0]), BF16),
                pltpu.SemaphoreType.DMA((nsem,)),
            ],
            input_output_aliases={5 + nparts + index: index for index in range(len(earlier))},
            compiler_params=params(),
            cost_estimate=cost(
                6 * rows * model * 8 * part // calls, weight_bytes[0] + rows * model * 16 // calls
            ),
            name="attn_forward",
        )(core_s, counts, table, own, norms, *parts_a, *earlier)

    attn = []
    for call in range(calls):
        gates = gather.later() if fast and call > 0 else []
        attn = attn_forward_call(call, after(own, *gates) if gates else own, attn)
        if call == 0 and fast:
            returned = after(returned, gather.near_three)
            gather.second(attn[0])
    if fast:
        parts_b, parts_c = gather.finish(attn[0])
    else:
        parts_b, parts_c = gather_plain(chunk_b), gather_plain(chunk_c)
    came_mine = lax.all_to_all(returned, "dp", split_axis=0, concat_axis=0, tiled=True)
    came_theirs = swap(came_mine, peers, 0, 1)
    first, packed, attended, middle, second, lse = attn

    group = 2
    chunk = group * size
    steps = here // group
    gviews = group * views_each
    blk = lambda cols: pl.BlockSpec((chunk, cols), lambda i: (i, 0))
    wide = hidden
    mlp_scratch = [
        pltpu.VMEM((2, model, chunk_cols[1]), BF16),
        pltpu.VMEM((2, model, chunk_cols[2]), BF16),
    ]
    act, slope, final, emb_keep, emb_send = pl.pallas_call(
        lambda *refs: mlp_forward(
            *refs, nparts=nparts, per_view=per_view, part=hidden, wide=wide, rows_each=size
        ),
        grid=(steps,),
        out_shape=[
            shape((rows, 2 * hidden), BF16),
            shape((rows, 2 * hidden), BF16),
            shape((rows, model), BF16),
            shape((steps * gviews, per_view, dec), BF16),
            shape((steps * gviews, per_view, dec), BF16),
        ],
        in_specs=[smem, smem, blk(model), blk(model), fixed((2, dec))] + [any_spec()] * (2 * nparts),
        out_specs=[
            blk(2 * hidden),
            blk(2 * hidden),
            blk(model),
            pl.BlockSpec((gviews, per_view, dec), lambda i: (i, 0, 0)),
            pl.BlockSpec((gviews, per_view, dec), lambda i: (i, 0, 0)),
        ],
        scratch_shapes=mlp_scratch + [pltpu.SemaphoreType.DMA((nsem,))] * 2,
        compiler_params=params(),
        cost_estimate=cost(
            4 * rows * model * 2 * hidden, weight_bytes[1] + weight_bytes[2] + rows * hidden * 8
        ),
        name="mlp_forward",
    )(core_s, table, second, middle, dec_full[0], *parts_b, *parts_c)

    where_mine = lax.dynamic_slice_in_dim(where_view, core * (nviews // cores), nviews // cores)
    emb_rows, glow, gpre, gmid, gmid_low, ln_two = pl.pallas_call(
        lambda *refs: mlp_backward(
            *refs, nparts=nparts, per_view=per_view, part=hidden, wide=wide, rows_each=size
        ),
        grid=(steps,),
        out_shape=[
            shape((rows, 2 * dec), BF16),
            shape((rows, model), BF16),
            shape((rows, 2 * hidden), BF16),
            shape((rows, model)),
            shape((rows, model), BF16),
            shape((8, model)),
        ],
        in_specs=[smem, smem, smem, any_spec(), any_spec(), blk(2 * hidden), blk(model), fixed((8, model))]
        + [any_spec()] * (2 * nparts),
        out_specs=[blk(2 * dec), blk(model), blk(2 * hidden), blk(model), blk(model), fixed((8, model))],
        scratch_shapes=mlp_scratch
        + [
            pltpu.VMEM((2, gviews, per_view, dec), BF16),
            pltpu.VMEM((chunk, 2 * dec), F32),
            pltpu.SemaphoreType.DMA((nsem,)),
            pltpu.SemaphoreType.DMA((nsem,)),
            pltpu.SemaphoreType.DMA((2, gviews)),
        ],
        compiler_params=params(),
        cost_estimate=cost(
            4 * rows * model * 2 * hidden, weight_bytes[1] + weight_bytes[2] + rows * hidden * 8
        ),
        name="mlp_backward",
    )(core_s, where_mine, table, came_mine, came_theirs, slope, middle, norms, *parts_b, *parts_c)

    emb_other = swap(emb_send, peers, 0, 1)
    if fast:
        emb_other = after(emb_other, glow)
    outgoing = pl.pallas_call(
        order_views,
        out_shape=shape((npos, per_view, dec), BF16),
        in_specs=[smem, smem, any_spec(), any_spec()],
        out_specs=any_spec(),
        scratch_shapes=[pltpu.SemaphoreType.DMA((nviews,))],
        compiler_params=params(8 << 20),
        cost_estimate=cost(0, 4 * nviews * per_view * dec),
        name="order_views",
    )(where_view, core_s, emb_keep, emb_other)
    arrived = lax.all_to_all(outgoing, "dp", split_axis=0, concat_axis=0, tiled=True)

    blocks = FAST_PEERS
    if fast:
        places = [place_table(me, core), place_table(me, 1 - core)]
    else:
        places = [jnp.arange(blocks, dtype=jnp.int32)] * 2

    deep = -(-rows // 256) * 256

    def side_grads(pairs, block, name, mine):
        lengths = [right.shape[1] // 2 // block for _, right in pairs]
        many = sum(lengths)
        begins = [sum(lengths[:index]) for index in range(len(lengths))]

        def column(begin, length):
            return lambda j, side, _: (0, side[0] * length + jnp.clip(j - begin, 0, length - 1))

        in_specs, operands = [], []
        for index, (left, right) in enumerate(pairs):
            in_specs += [
                pl.BlockSpec((rows, model), lambda j, *_: (0, 0)),
                pl.BlockSpec((rows, block), column(begins[index], lengths[index])),
            ]
            operands += [left, right]
        grad_shape = (blocks, model // blocks, many * block)
        return pl.pallas_call(
            lambda *refs: weight_grad(*refs, steps=lengths, rows_each=model // blocks),
            out_shape=shape(grad_shape, BF16),
            grid_spec=pltpu.PrefetchScalarGridSpec(
                num_scalar_prefetch=2,
                grid=(many,),
                in_specs=in_specs,
                out_specs=pl.BlockSpec(grad_shape[:2] + (block,), lambda j, *_: (0, 0, j)),
                scratch_shapes=[pltpu.VMEM((deep, model), BF16), pltpu.VMEM((deep, block), BF16)],
            ),
            compiler_params=params(),
            cost_estimate=cost(2 * rows * model * many * block, 2 * rows * (many * block + model)),
            name=name,
        )(core_s if mine else 1 - core_s, places[0 if mine else 1], *operands)

    def attn_backward_call(call, mid, earlier):
        begin = call * each_call
        ep = lambda cols: pl.BlockSpec((size, cols), lambda i: (i + begin, 0))
        return pl.pallas_call(
            lambda *refs: attn_backward(
                *refs, nparts=nparts, per_view=per_view, part=part, begin=begin, here=here
            ),
            grid=(each_call,),
            out_shape=[
                shape((rows, 6 * part), BF16),
                shape((here, span, model), BF16),
                shape((8, model)),
            ],
            in_specs=[smem, smem, smem, ep(model), ep(6 * part), ep(2 * HEADDIM), ep(model), fixed((8, model))]
            + [any_spec()] * (nparts + len(earlier)),
            out_specs=[
                ep(6 * part),
                pl.BlockSpec((1, span, model), lambda i: (i + begin, 0, 0)),
                fixed((8, model)),
            ],
            scratch_shapes=[
                pltpu.VMEM((2, model, chunk_cols[0]), BF16),
                pltpu.SemaphoreType.DMA((nsem,)),
            ],
            input_output_aliases={8 + nparts + index: index for index in range(len(earlier))},
            compiler_params=params(),
            cost_estimate=cost(
                8 * rows * model * 8 * part // calls, weight_bytes[0] + rows * model * 16 // calls
            ),
            name="attn_backward",
        )(core_s, counts, table, own, packed, lse, mid, norms, *parts_a, *earlier)

    hold = after if fast else (lambda array, *others: array)
    leaves = jax.tree.leaves

    def holds(state, *others):
        return [state[0], tuple(hold_all(leaves(state[1]), leaves(others)))] if fast else state

    def chunk_start(pairs, block, name, *gate):
        left, right = pairs[0]
        pairs = [(left, hold(right, *gate))] + pairs[1:]
        other = side_grads(pairs, block, name + "_send", False)
        got = swap(other, peers, 0, 1)
        left, right = pairs[0]
        pairs = [(left, hold(right, other))] + pairs[1:]
        mine = side_grads(pairs, block, name + "_keep", True)
        return scatter_start((mine, got), peers), mine

    sum_c, last = chunk_start([(glow, act), (final, emb_rows)], 256, "grad_down_emb", outgoing)
    sum_b, last = chunk_start(
        [(second, gpre), (gmid_low, attended)], part, "grad_up_out", last, sum_c[1]
    )
    sum_c = scatter_near(sum_c, peers, last)
    ln_one = jnp.zeros((8, model), F32)
    back = []
    for call in range(calls):
        if call == 0:
            gates = [last, sum_c[1], sum_b[1], arrived]
        else:
            gates = [sum_c[1], sum_b[1]]
        *back, sums = attn_backward_call(call, hold(gmid, *leaves(gates)), back)
        ln_one = ln_one + sums
        if call == 0:
            sum_c = scatter_far(sum_c, peers, back[0])
            sum_b = scatter_near(sum_b, peers, back[0])
    grad_packed, grad_own = back
    sum_c = scatter_end(sum_c, peers, grad_own)
    sum_b = scatter_far(sum_b, peers, grad_own)
    sum_a, last = chunk_start(
        [(first, grad_packed)], part, "grad_in", sum_c, *leaves(sum_b[1])
    )
    sum_a = scatter_near(sum_a, peers)
    sum_b = scatter_end(sum_b, peers, last)

    grad_other = swap(grad_own, peers, 0, 1)
    grad_tokens = jnp.where(
        core == 0,
        jnp.concatenate([grad_own, grad_other]),
        jnp.concatenate([grad_other, grad_own]),
    ).reshape(tokens.shape)

    ln_sums = jnp.concatenate([ln_one[:2], ln_two[:2]])
    ln_send = ln_sums.reshape(4, peers, shard_rows).transpose(1, 0, 2).reshape(peers, nln)
    dec_send = dec_sums[:2].reshape(2, peers, dec // peers).transpose(1, 0, 2).reshape(peers, -1)
    small_send = jnp.concatenate([ln_send, dec_send], axis=1)
    small_send = jnp.broadcast_to(small_send[:, None], (peers, cores, small_send.shape[1]))
    small_got = lax.all_to_all(
        small_send.reshape(peers * cores, -1), AXES, split_axis=0, concat_axis=0, tiled=True
    ).reshape(peers, cores, -1)
    grad_ln = jnp.sum(small_got[:, :, :nln], axis=(0, 1)).reshape(4, shard_rows)
    grad_dec = jnp.sum(
        lax.dynamic_index_in_dim(small_got[:, :, nln:], core, 1, keepdims=False), axis=0
    ).reshape(2, dec // peers)

    positions = lax.dynamic_slice_in_dim(
        grid_positions(math.isqrt(cells), dec * cores), core * dec, dec, 1
    )
    decoded = pl.pallas_call(
        put_cells,
        out_shape=shape((cells, nviews, dec), BF16),
        grid_spec=pltpu.PrefetchScalarGridSpec(
            num_scalar_prefetch=2,
            grid=(groups,),
            in_specs=[
                pl.BlockSpec((1, 1, each * stride_put), lambda i, *_: (i, 0, 0)),
                pl.BlockSpec((1, dec), lambda i, *_: (0, 0)),
                pl.BlockSpec((cells, dec), lambda i, *_: (0, 0)),
                pl.BlockSpec((npos, per_view, dec), lambda i, *_: (0, 0, 0)),
            ],
            out_specs=pl.BlockSpec((cells, each, dec), lambda i, *_: (0, i, 0)),
            scratch_shapes=[pltpu.VMEM((each * stride_put, dec), BF16)],
        ),
        compiler_params=params(),
        cost_estimate=cost(2 * nviews * stride_put * cells * each * dec, cotangent.size * 2),
        name="put_cells",
    )(where_slot, live_slot, hold(put_marks, last), mask_token, positions, arrived)
    sum_a = scatter_far(holds(sum_a, decoded, sum_b), peers)
    decoded = decoded.transpose(1, 0, 2)
    sum_a = scatter_end(holds(sum_a, grad_tokens), peers)

    grads = [
        sum_a,
        sum_b[:, hidden:],
        sum_b[:, :hidden],
        sum_c[:, :hidden],
        sum_c[:, hidden:],
        grad_ln,
        grad_dec,
    ]
    world = peers * cores
    (tiles,) = whole(squares_kernel, [shape((world, 8, 128))], [once_s], grads + masters, name="squares")
    tiles = lax.all_to_all(tiles, AXES, split_axis=0, concat_axis=0, tiled=True)
    same_shapes = [shape(m.shape) for m in masters]
    lamb = whole(
        lamb_kernel,
        same_shapes * 4 + [shape((8, 128)), shape((world, 8, 128))],
        [once_s],
        [tiles] + grads + masters + moments + squares,
        name="lamb",
    )
    summed = lamb[28]
    steps_tiles = lax.all_to_all(lamb[29], AXES, split_axis=0, concat_axis=0, tiled=True)
    update = whole(
        update_kernel,
        same_shapes + [shape(m.shape, BF16) for m in masters] + [shape((8, 128))],
        [],
        [steps_tiles, summed] + masters + list(lamb[21:28]),
        name="update",
    )
    results = [
        natural(group)
        for group in (lamb[:7], lamb[7:14], lamb[14:21], update[:7], update[7:14])
    ]
    outs = [decoded, grad_tokens, update[14][2, :1], update[14][:2, :7]]
    for index in range(7):
        outs += [group[index] for group in results]
    return tuple(outs)


def solution(mesh):
    tensor_specs = [
        P("dp", None, "mp"),
        P("mp", "dp"),
        P("dp", "mp"),
        P("mp", "dp"),
        P("dp", "mp"),
        P(None, "dp"),
        P(None, "mp", "dp"),
    ]
    in_specs = (
        P("dp", None),
        P("dp"),
        P("dp", None),
        P("dp"),
        P("dp"),
        P("dp", None, "mp"),
    ) + tuple(spec for spec in tensor_specs for _ in range(3))
    out_specs = (P("dp", None, "mp"), P("dp", None), P(), P()) + tuple(
        spec for spec in tensor_specs for _ in range(5)
    )
    return jax.shard_map(
        per_device, mesh=mesh, in_specs=in_specs, out_specs=out_specs, check_vma=False
    )
```

```python
import math

import jax
import jax.numpy as jnp
from jax import lax
from jax.experimental import pallas as pl
from jax.experimental.pallas import tpu as pltpu
from jax.sharding import PartitionSpec as P

HEADDIM = 64
PARAMS = 7475200
NORM_EPS = 1e-06
MASK_FILL = -1e30
BETA_ONE = 0.5
BETA_TWO = 0.5
ADAM_EPS = 1e-06
DECAY_RATE = 0.01
LEARN_RATE = 0.5
TRUST_EPS = 1e-06

F32 = jnp.float32
BF16 = jnp.bfloat16
AXES = ("dp", "mp")
NT = (((1,), (1,)), ((), ()))
TN = (((0,), (0,)), ((), ()))
ROUND = 16
VMEM_BYTES = 58 << 20
COST = 3.0


def mm(a, b, dims=(((1,), (0,)), ((), ()))):
    return lax.dot_general(a, b, dims, preferred_element_type=F32)


def norm_rows(values):
    centre = values - jnp.mean(values, axis=-1, keepdims=True)
    spread = jnp.mean(centre * centre, axis=-1, keepdims=True)
    inverse = lax.rsqrt(spread + NORM_EPS)
    return centre * inverse, inverse


def norm_back(scaled, normed, inverse):
    return inverse * (
        scaled
        - jnp.mean(scaled, axis=-1, keepdims=True)
        - normed * jnp.mean(scaled * normed, axis=-1, keepdims=True)
    )


def grid_positions(side, width):
    quarter = width // 4
    rate = 1.0 / 10000.0 ** (jnp.arange(quarter, dtype=F32) / quarter)
    place = jnp.arange(side * side, dtype=jnp.int32)
    row_pos = (place // side).astype(F32)
    col_pos = (place % side).astype(F32)
    row_angle = row_pos[:, None] * rate[None, :]
    col_angle = col_pos[:, None] * rate[None, :]
    return jnp.concatenate(
        [jnp.sin(row_angle), jnp.cos(row_angle), jnp.sin(col_angle), jnp.cos(col_angle)], axis=1
    )


def any_spec():
    return pl.BlockSpec(memory_space=pl.ANY)


def params(limit=VMEM_BYTES):
    return pltpu.CompilerParams(vmem_limit_bytes=limit)


def cost(flops, nbytes):
    return pl.CostEstimate(flops=int(COST * flops), bytes_accessed=int(nbytes), transcendentals=0)


def swap(array, peers, bits, core=0):
    bits = bits if isinstance(bits, tuple) else (bits, bits)
    pairs = [
        (d * 2 + m, (d ^ bits[m]) * 2 + (m ^ core)) for d in range(peers) for m in range(2)
    ]
    return lax.ppermute(array, AXES, pairs)


FAST_PEERS = 16
Z_STEPS = (4, 8, 12)


def after(array, *others):
    return lax.optimization_barrier((array,) + others)[0]


def reach_z(shard, peers):
    return [swap(shard, peers, bits) for bits in Z_STEPS]


def hold_all(arrays, others):
    return list(lax.optimization_barrier((tuple(arrays), tuple(others)))[0])


def gather_plain(shard):
    return [lax.all_gather(lax.all_gather(shard, "dp", axis=0, tiled=True), "mp", axis=0)]


class Gather:
    def __init__(self, shards, peers):
        self.peers = peers
        self.one, self.two, self.three = shards

    def near(self, array):
        return swap(array, self.peers, (1, 2))

    def far(self, array):
        return swap(array, self.peers, (2, 1))

    def across(self, array):
        return swap(array, self.peers, 0, 1)

    def step_z(self, beside):
        z_one = reach_z(self.one, self.peers)
        (self.along_one,) = hold_all([jnp.stack([self.one] + z_one)], beside)
        (self.two,) = hold_all([self.two], z_one)
        return z_one

    def step_near(self, beside):
        near_one, z_two = self.near(self.along_one), reach_z(self.two, self.peers)
        (self.half_one,) = hold_all([jnp.concatenate([self.along_one, near_one])], beside)
        self.along_two, self.three = hold_all(
            [jnp.stack([self.two] + z_two), self.three], [near_one] + z_two
        )
        return [near_one]

    def step_far(self, beside):
        far_one, side_one = self.far(self.half_one), self.across(self.half_one)
        near_two, z_three = self.near(self.along_two), reach_z(self.three, self.peers)
        far_one, half_two, along_three = hold_all(
            [far_one, jnp.concatenate([self.along_two, near_two]), jnp.stack([self.three] + z_three)],
            [far_one, near_two] + z_three + list(beside),
        )
        self.half_two, self.along_three = half_two, along_three
        self.far_two, self.side_two = self.far(half_two), self.across(half_two)
        self.near_three = self.near(along_three)
        return [self.half_one, far_one, side_one, self.across(far_one)]

    def later(self):
        return [self.far_two, self.near_three, self.side_two]

    def second(self, beside):
        far_two, along_three, near_three = hold_all(
            [self.far_two, self.along_three, self.near_three], [beside]
        )
        self.half_three = jnp.concatenate([along_three, near_three])
        self.far_three, self.side_three = self.far(self.half_three), self.across(self.half_three)
        self.parts_two = [self.half_two, far_two, self.side_two, self.across(far_two)]

    def finish(self, beside):
        (far_three,) = hold_all([self.far_three], [beside] + self.parts_two[2:])
        parts_three = [self.half_three, far_three, self.side_three, self.across(far_three)]
        return self.parts_two, parts_three


PIECE = 8


def gather_table(me, core):
    one = jnp.where(core == 0, 1, 2)
    two = 3 - one
    along = jnp.array((0,) + Z_STEPS, jnp.int32)
    mine = jnp.concatenate([along, along ^ one])
    theirs = jnp.concatenate([along, along ^ two])
    apart = jnp.concatenate([mine, mine ^ two, theirs, theirs ^ one])
    cores = jnp.stack([core, core, 1 - core, 1 - core])
    return jnp.concatenate([me ^ apart, cores]).astype(jnp.int32)


def weight_copies(parts, table, target, sems):
    if len(parts) == 1:
        return [pltpu.make_async_copy(parts[0], target, sems.at[0])]
    copies = []
    for index, part in enumerate(parts):
        half = table[len(parts) * PIECE + index]
        for inner in range(PIECE):
            at = index * PIECE + inner
            rows = part.shape[1]
            start = pl.multiple_of(table[at] * rows, ROUND)
            copies.append(
                pltpu.make_async_copy(
                    part.at[inner], target.at[half, pl.ds(start, rows), :], sems.at[at]
                )
            )
    return copies


def place_table(me, core):
    near = jnp.where(core == 0, 2, 1)
    far = 3 - near
    apart = jnp.arange(FAST_PEERS, dtype=jnp.int32) ^ me
    return (
        jnp.where((apart & near) != 0, 8, 0) + jnp.where((apart & far) != 0, 4, 0) + (apart >> 2)
    ).astype(jnp.int32)


def add(*terms):
    return sum(term.astype(F32) for term in terms)


def scatter_near(state, peers, *held):
    if peers != FAST_PEERS:
        return state
    terms, send = state
    got = swap(send, peers, (2, 1))
    terms = terms + (after(got, *held) if held else got,)
    return [terms, add(*(term[4:8] for term in terms)).astype(BF16)]


def scatter_far(state, peers, *held):
    if peers != FAST_PEERS:
        return state
    terms, send = state
    got = swap(send, peers, (1, 2))
    terms = terms + (after(got, *held) if held else got,)
    return [terms, tuple(add(*(term[i] for term in terms)).astype(BF16) for i in (1, 2, 3))]


def scatter_end(state, peers, *held):
    if peers != FAST_PEERS:
        (keep,), send = state
        whole = jnp.concatenate([keep, send]).astype(F32)
        return lax.psum_scatter(
            whole.reshape(-1, whole.shape[-1]), "dp", scatter_dimension=0, tiled=True
        )
    terms, sends = state
    last = [swap(send, peers, bits) for send, bits in zip(sends, Z_STEPS)]
    last = hold_all(last, held) if held else last
    return add(*(term[0] for term in terms), *last)


def view_of(rows, per_view):
    view = jnp.zeros_like(rows)
    for edge in range(1, 5):
        view = view + (rows >= edge * per_view).astype(jnp.int32)
    return view


def allowed_bias(size, count, per_view):
    query = view_of(lax.broadcasted_iota(jnp.int32, (size, size), 0), per_view)
    key = view_of(lax.broadcasted_iota(jnp.int32, (size, size), 1), per_view)
    return jnp.where((key < count) | (key == query), 0.0, MASK_FILL)


def pair_masks(scale):
    lane = lax.broadcasted_iota(jnp.int32, (1, 2 * HEADDIM), 1)
    low = (lane < HEADDIM).astype(F32)
    return (low * scale).astype(BF16), ((1.0 - low) * scale).astype(BF16)


def attn_forward(mp_s, counts_s, table, tokens, norms, *rest, nparts, per_view, part, begin, here):
    parts = rest[:nparts]
    first_o, packed_o, attended_o, middle_o, second_o, lse_o, weights, sems = rest[-8:]
    step = pl.program_id(0)
    copies = weight_copies(parts, table, weights, sems)

    @pl.when(step == 0)
    def _():
        for copy in copies:
            copy.start()
        for copy in copies:
            copy.wait()

    size = tokens.shape[0]
    scale = 1.0 / math.sqrt(HEADDIM)
    values = tokens[...].astype(F32)
    normed, _ = norm_rows(values)
    first = (normed * norms[0:1, :] + norms[1:2, :]).astype(BF16)
    first_o[...] = first
    bias = allowed_bias(size, counts_s[mp_s[0] * here + begin + step], per_view)
    bias = jnp.concatenate([bias, bias], axis=0)
    masks = pair_masks(scale)
    lane = lax.broadcasted_iota(jnp.int32, (size, 2 * HEADDIM), 1)
    wide = 2 * HEADDIM
    lse = jnp.zeros((size, wide), F32)
    attn = jnp.zeros(values.shape, F32)
    for half in range(2):
        packed = mm(first, weights[half, :, : 3 * part]).astype(BF16)
        packed_o[:, half * 3 * part : (half + 1) * 3 * part] = packed
        pairs = range(part // wide)
        logits, probs = [], []
        for pair in pairs:
            at = pair * wide
            query = packed[:, at : at + wide]
            key = packed[:, part + at : part + at + wide]
            both = jnp.concatenate([query * masks[0], query * masks[1]], axis=0)
            logits.append(mm(both, key, NT) + bias)
        for pair in pairs:
            top = jnp.max(logits[pair], axis=-1, keepdims=True)
            exponent = jnp.exp(logits[pair] - top)
            total = jnp.sum(exponent, axis=-1, keepdims=True)
            probs.append((exponent * (1.0 / total)).astype(BF16))
            top = top + jnp.log(total)
            index = half * (part // HEADDIM) + pair * 2
            lse = jnp.where(lane == index, top[:size], lse)
            lse = jnp.where(lane == index + 1, top[size:], lse)
        for pair in pairs:
            at = pair * wide
            outs = mm(probs[pair], packed[:, 2 * part + at : 2 * part + at + wide])
            both = jnp.where(lane < HEADDIM, outs[:size], outs[size:]).astype(BF16)
            attended_o[:, half * part + at : half * part + at + wide] = both
        attn = attn + mm(
            attended_o[:, half * part : (half + 1) * part], weights[half, :, 3 * part :], NT
        )
    lse_o[...] = lse
    middle = values + attn
    middle_o[...] = middle
    normed, _ = norm_rows(middle)
    second_o[...] = (normed * norms[2:3, :] + norms[3:4, :]).astype(BF16)


def mlp_forward(mp_s, table, second, middle, dec_bias, *rest, nparts, per_view, part, wide, rows_each):
    up_parts, down_parts = rest[:nparts], rest[nparts : 2 * nparts]
    act_o, slope_o, final_o, keep_o, send_o = rest[2 * nparts : 2 * nparts + 5]
    up, down, up_sems, down_sems = rest[2 * nparts + 5 :]
    up_copies = weight_copies(up_parts, table, up, up_sems)
    down_copies = weight_copies(down_parts, table, down, down_sems)

    @pl.when(pl.program_id(0) == 0)
    def _():
        for copy in up_copies + down_copies:
            copy.start()
        for copy in up_copies + down_copies:
            copy.wait()

    acc = middle[...]
    rows = second[...]
    for half in range(2):
        for start in range(0, part, wide):
            pre = mm(rows, up[half, :, start : start + wide])
            cumulative = 0.5 * (1.0 + lax.erf(pre * (1.0 / math.sqrt(2.0))))
            act = (pre * cumulative).astype(BF16)
            slope = cumulative + pre * jnp.exp(-0.5 * pre * pre) * (1.0 / math.sqrt(2.0 * math.pi))
            act_o[:, half * part + start : half * part + start + wide] = act
            slope_o[:, half * part + start : half * part + start + wide] = slope.astype(BF16)

            acc = acc + mm(act, down[half, :, start : start + wide], NT)
    final = acc.astype(BF16)
    final_o[...] = final
    outs = [
        mm(final, down[half, :, part:]) + dec_bias[half : half + 1, :] for half in range(2)
    ]
    mine = jnp.where(mp_s[0] == 0, outs[0], outs[1])
    theirs = jnp.where(mp_s[0] == 0, outs[1], outs[0])
    views = rows_each // per_view
    for view in range(keep_o.shape[0]):
        at = (view // views) * rows_each + (view % views) * per_view
        keep_o[view, :per_view, :] = mine[at : at + per_view].astype(BF16)
        send_o[view, :per_view, :] = theirs[at : at + per_view].astype(BF16)


def mlp_backward(
    mp_s, where_s, table, mine, theirs, slope, middle, norms, *rest, nparts, per_view, part, wide, rows_each
):
    up_parts, down_parts = rest[:nparts], rest[nparts : 2 * nparts]
    rows_o, low_o, pre_o, mid_o, midlow_o, sums_o = rest[2 * nparts : 2 * nparts + 6]
    up, down, pieces, flat, up_sems, down_sems, piece_sems = rest[2 * nparts + 6 :]
    step = pl.program_id(0)
    nviews = pieces.shape[1]
    up_copies = weight_copies(up_parts, table, up, up_sems)
    down_copies = weight_copies(down_parts, table, down, down_sems)
    fetch = []
    for view in range(nviews):
        at = where_s[step * nviews + view]
        fetch.append(
            pltpu.make_async_copy(mine.at[at], pieces.at[mp_s[0], view], piece_sems.at[0, view])
        )
        fetch.append(
            pltpu.make_async_copy(theirs.at[at], pieces.at[1 - mp_s[0], view], piece_sems.at[1, view])
        )
    for copy in fetch:
        copy.start()

    @pl.when(step == 0)
    def _():
        for copy in down_copies + up_copies:
            copy.start()
        flat[...] = jnp.zeros_like(flat)
        sums_o[...] = jnp.zeros_like(sums_o)
        for copy in down_copies + up_copies:
            copy.wait()

    for copy in fetch:
        copy.wait()
    dec = pieces.shape[3]
    views = rows_each // per_view
    for view in range(nviews):
        at = (view // views) * rows_each + (view % views) * per_view
        for half in range(2):
            flat[at : at + per_view, half * dec : (half + 1) * dec] = pieces[half, view][
                :per_view
            ].astype(F32)
    rows = flat[...].astype(BF16)
    rows_o[...] = rows
    final = mm(rows[:, :dec], down[0, :, part:], NT) + mm(rows[:, dec:], down[1, :, part:], NT)
    low = final.astype(BF16)
    low_o[...] = low
    acc = jnp.zeros(final.shape, F32)
    for half in range(2):
        for start in range(0, part, wide):
            at = half * part + start
            hidden = mm(low, down[half, :, start : start + wide])
            pre = (hidden * slope[:, at : at + wide].astype(F32)).astype(BF16)
            pre_o[:, at : at + wide] = pre

            acc = acc + mm(pre, up[half, :, start : start + wide], NT)
    normed, inverse = norm_rows(middle[...])
    sums_o[0:1, :] += jnp.sum(acc * normed, axis=0, keepdims=True)
    sums_o[1:2, :] += jnp.sum(acc, axis=0, keepdims=True)
    mid = final + norm_back(acc * norms[2:3, :], normed, inverse)
    mid_o[...] = mid
    midlow_o[...] = mid.astype(BF16)


def attn_backward(
    mp_s, counts_s, table, tokens, packed, lse, mid, norms, *rest, nparts, per_view, part, begin, here
):
    parts = rest[:nparts]
    packed_o, tokens_o, sums_o, weights, sems = rest[-5:]
    step = pl.program_id(0)
    copies = weight_copies(parts, table, weights, sems)

    @pl.when(step == 0)
    def _():
        for copy in copies:
            copy.start()
        sums_o[...] = jnp.zeros_like(sums_o)
        for copy in copies:
            copy.wait()

    size = tokens.shape[0]
    scale = 1.0 / math.sqrt(HEADDIM)
    wide = 2 * HEADDIM
    bias = allowed_bias(size, counts_s[mp_s[0] * here + begin + step], per_view)
    bias = jnp.concatenate([bias, bias], axis=0)
    masks = pair_masks(1.0)
    lane = lax.broadcasted_iota(jnp.int32, (size, wide), 1)
    low = lane < HEADDIM
    middle = mid[...]
    middle_low = middle.astype(BF16)
    back = jnp.zeros(middle.shape, F32)
    for half in range(2):
        grad_att = mm(middle_low, weights[half, :, 3 * part :]).astype(BF16)
        base = half * 3 * part
        pairs = range(part // wide)
        sides, logits, grad_probs, lows = [], [], [], []
        for pair in pairs:
            at = pair * wide
            query = packed[:, base + at : base + at + wide]
            key = packed[:, base + part + at : base + part + at + wide]
            value = packed[:, base + 2 * part + at : base + 2 * part + at + wide]
            grad = grad_att[:, at : at + wide]
            query = jnp.concatenate([query * masks[0], query * masks[1]], axis=0)
            grad = jnp.concatenate([grad * masks[0], grad * masks[1]], axis=0)
            sides.append((query, key, grad))
            logits.append(mm(query, key, NT) * scale + bias)
            grad_probs.append(mm(grad, value, NT))
        for pair in pairs:
            index = half * (part // HEADDIM) + pair * 2
            top = jnp.concatenate([lse[:, index : index + 1], lse[:, index + 1 : index + 2]], axis=0)
            probs = jnp.exp(logits[pair] - top)
            weighted = probs * grad_probs[pair]
            centre = jnp.sum(weighted, axis=-1, keepdims=True)
            scores = ((weighted - probs * centre) * scale).astype(BF16)
            lows.append((scores, probs.astype(BF16)))
        for pair in pairs:
            query, key, grad = sides[pair]
            scores, probs = lows[pair]
            at = base + pair * wide
            grad_query = mm(scores, key)
            packed_o[:, at : at + wide] = jnp.where(
                low, grad_query[:size], grad_query[size:]
            ).astype(BF16)
            at = at + part
            packed_o[:, at : at + wide] = mm(scores, query, TN).astype(BF16)
            at = at + part
            packed_o[:, at : at + wide] = mm(probs, grad, TN).astype(BF16)
        back = back + mm(packed_o[:, base : base + 3 * part], weights[half, :, : 3 * part], NT)
    normed, inverse = norm_rows(tokens[...].astype(F32))
    sums_o[0:1, :] += jnp.sum(back * normed, axis=0, keepdims=True)
    sums_o[1:2, :] += jnp.sum(back, axis=0, keepdims=True)
    grads = middle + norm_back(back * norms[0:1, :], normed, inverse)
    tokens_o[0] = grads[: tokens_o.shape[1]].astype(BF16)


def weight_grad(side_s, places, *rest, steps, rows_each, add_other):
    count = len(steps)
    sides, rest = rest[: 2 * count], rest[2 * count :]
    left_pad, right_pad = rest[-2:]
    step = pl.program_id(0 if places is not None else 1)
    begin = 0

    @pl.when(step == 0)
    def _():
        left_pad[...] = jnp.zeros_like(left_pad)
        right_pad[...] = jnp.zeros_like(right_pad)

    for index, length in enumerate(steps):
        left, right = sides[2 * index], sides[2 * index + 1]

        @pl.when(step == begin)
        def _(left=left):
            left_pad[: left.shape[0], :] = left[...]

        @pl.when((step >= begin) & (step < begin + length))
        def _(right=right):
            right_pad[: right.shape[0], :] = right[...]

        begin += length
    product = mm(left_pad[...], right_pad[...], TN)
    if places is None:
        grads_o = rest[0]
        for block in range(grads_o.shape[0]):
            grads_o[block, 0] = product[block * rows_each : (block + 1) * rows_each].astype(BF16)
    elif add_other:
        other, keep_o, send_o, held = rest[:4]
        half = keep_o.shape[0]
        for block in range(2 * half):
            held[places[block]] = product[block * rows_each : (block + 1) * rows_each]
        keep_o[...] = (held[:half] + other[:half].astype(F32)).astype(BF16)
        send_o[...] = (held[half:] + other[half:].astype(F32)).astype(BF16)
    else:
        product = product.astype(BF16)
        grads_o = rest[0]
        for block in range(grads_o.shape[0]):
            grads_o[places[block]] = product[block * rows_each : (block + 1) * rows_each]


def take_cells(where_s, marks, live_row, cells, rows_o, sums_o, *, per_view, stride):
    step = pl.program_id(0)

    @pl.when(step == 0)
    def _():
        sums_o[...] = jnp.zeros_like(sums_o)

    grid, each, dec = cells.shape
    flat = cells[...].reshape(grid * each, dec)
    lane = lax.broadcasted_iota(jnp.int32, (each * stride, grid * each), 1)
    pick = (marks[...] == lane).astype(F32)
    covered = jnp.sum(pick, axis=0, keepdims=True)
    open_cells = jnp.broadcast_to(live_row[0] - covered, (8, grid * each)).astype(BF16)
    taken = mm(pick.astype(BF16), flat)
    masked = mm(open_cells, flat)
    for index in range(each):
        rows_o[where_s[step * each + index]] = taken[index * stride : (index + 1) * stride].astype(BF16)
    sums_o[0:1, :] += jnp.sum(taken, axis=0, keepdims=True)
    sums_o[1:2, :] += masked[0:1]


def put_cells(where_s, live_s, marks, mask, positions, rows, cells_o, held, *, per_view):
    step = pl.program_id(0)
    grid, each, dec = cells_o.shape
    stride = held.shape[0] // each

    @pl.when(step == 0)
    def _():
        held[...] = jnp.zeros_like(held)

    slot = lax.broadcasted_iota(jnp.int32, (1, each, 1), 1)
    live = jnp.zeros((1, each, 1), F32)
    for index in range(each):
        at = step * each + index
        held[index * stride : index * stride + per_view, :] = rows[where_s[at]][:per_view]
        live = jnp.where(slot == index, live_s[at].astype(F32), live)
    line = lax.broadcasted_iota(jnp.int32, (grid * each, held.shape[0]), 0)
    place = (marks[0] == line).astype(F32)
    covered = jnp.sum(place, axis=1, keepdims=True)
    live = jnp.broadcast_to(live, (grid, each, 1)).reshape(grid * each, 1)
    filled = mm(place.astype(BF16), held[...]) + (live - covered) * mask[...]
    filled = filled.reshape(grid, each, dec) + positions[...][:, None, :]
    cells_o[...] = filled.astype(BF16)


def order_views(where_s, mp_s, own, theirs, out, sems):
    count = own.shape[0]
    copies = []
    for view in range(count):
        mine, other = mp_s[0] * count + view, (1 - mp_s[0]) * count + view
        copies.append(pltpu.make_async_copy(own.at[view], out.at[where_s[mine]], sems.at[view]))
        copies.append(
            pltpu.make_async_copy(theirs.at[view], out.at[where_s[other]], sems.at[count + view])
        )
    for copy in copies:
        copy.start()
    for copy in copies:
        copy.wait()


def tile_of(scalars, begin=0):
    lane = lax.broadcasted_iota(jnp.int32, (1, 128), 1)
    tile = jnp.zeros((1, 128), F32)
    for index, value in enumerate(scalars):
        tile = jnp.where(lane == begin + index, value, tile)
    return tile


def total(values):
    return jnp.sum(jnp.sum(values, axis=1, keepdims=True), axis=0, keepdims=True)


def grad_views(refs, masters):
    first, second, third, norms, dec = refs
    wide, thin = masters[2].shape[1], masters[4].shape[1]
    return [
        first,
        second.at[:, pl.ds(wide, masters[1].shape[1])],
        second.at[:, pl.ds(0, wide)],
        third.at[:, pl.ds(0, wide)],
        third.at[:, pl.ds(wide, thin)],
        norms,
        dec,
    ]


def squares_kernel(once_s, *refs):
    masters, (tiles_o,) = refs[5:12], refs[12:]
    grads = grad_views(refs[:5], masters)
    single = [1.0] * 5 + [once_s[0].astype(F32), 1.0]
    grad_sq, weight_sq = [], []
    for index in range(7):
        value = grads[index][...]
        grad_sq.append(total(value * value) * single[index])
        if index == 0:
            weight = sum(total(masters[0][k] * masters[0][k]) for k in range(3))
        else:
            weight = total(masters[index][...] * masters[index][...])
        weight_sq.append(weight * single[index])
    tile = tile_of(grad_sq) + tile_of(weight_sq, 64)
    for peer in range(tiles_o.shape[0]):
        tiles_o[peer] = tile


def lamb_kernel(once_s, tiles, *refs):
    masters, moments, squares = refs[5:12], refs[12:19], refs[19:26]
    grads = grad_views(refs[:5], masters)
    outs = refs[26:]
    clip_o, moment_o, square_o, step_o = outs[:7], outs[7:14], outs[14:21], outs[21:28]
    sum_o, tiles_o = outs[28:]
    summed = jnp.sum(tiles[...], axis=0)
    sum_o[...] = summed
    lane = lax.broadcasted_iota(jnp.int32, (1, 128), 1)
    clip = jnp.sqrt(total(jnp.where(lane < 7, summed, 0.0)))
    factor = jnp.minimum(1.0, 0.5 * math.sqrt(PARAMS) / clip)
    single = [1.0] * 5 + [once_s[0].astype(F32), 1.0]
    update_sq = []
    for index in range(7):
        amount = jnp.zeros((1, 1), F32)
        for piece in range(3 if index == 0 else 1):
            at = piece if index == 0 else Ellipsis
            value = grads[index][...]
            if index == 0:
                width = masters[0].shape[2]
                value = value[:, piece * width : (piece + 1) * width]
            clipped = value * factor
            moment = BETA_ONE * moments[index][at] + (1.0 - BETA_ONE) * clipped
            square = BETA_TWO * squares[index][at] + (1.0 - BETA_TWO) * clipped * clipped
            step = moment / (jnp.sqrt(square) + ADAM_EPS) + DECAY_RATE * masters[index][at]
            clip_o[index][at] = clipped
            moment_o[index][at] = moment
            square_o[index][at] = square
            step_o[index][at] = step
            amount = amount + total(step * step)
        update_sq.append(amount * single[index])
    tile = tile_of(update_sq)
    for peer in range(tiles_o.shape[0]):
        tiles_o[peer] = tile


def update_kernel(tiles, summed, *refs):
    masters, steps, outs = refs[:7], refs[7:14], refs[14:]
    updated_o, copy_o, (norms_o, clip_o) = outs[:7], outs[7:14], outs[14:]
    lane = lax.broadcasted_iota(jnp.int32, (1, 128), 1)
    squared = summed[...]
    clip = jnp.sqrt(total(jnp.where(lane < 7, squared, 0.0)))
    weight_norm = jnp.sqrt(jnp.concatenate([squared[:, 64:], squared[:, :64]], axis=1))
    update_norm = jnp.sqrt(jnp.sum(tiles[...], axis=0))
    ratio = weight_norm / (update_norm + TRUST_EPS)
    norms_o[0:1, :] = weight_norm[:, :7]
    norms_o[1:2, :] = update_norm[:, :7]
    clip_o[...] = clip
    for index in range(7):
        rate = LEARN_RATE * total(jnp.where(lane == index, ratio, 0.0))
        for piece in range(3 if index == 0 else 1):
            at = piece if index == 0 else Ellipsis
            updated = masters[index][at] - rate * steps[index][at]
            updated_o[index][at] = updated
            copy_o[index][at] = updated.astype(BF16)


def shape(dims, dtype=F32):
    return jax.ShapeDtypeStruct(tuple(dims), dtype)


def whole(kernel, outs, scalars, operands, **kw):
    return pl.pallas_call(
        kernel,
        out_shape=outs,
        in_specs=[pl.BlockSpec(memory_space=pltpu.SMEM)] * len(scalars)
        + [pl.BlockSpec(memory_space=pltpu.VMEM)] * len(operands),
        out_specs=[pl.BlockSpec(memory_space=pltpu.VMEM)] * len(outs),
        compiler_params=params(),
        **kw,
    )(*scalars, *operands)


def per_device(
    tokens,
    counts,
    visible,
    dest_device,
    dest_slot,
    cotangent,
    *state,
):
    masters = [state[3 * index] for index in range(7)]
    moments = [state[3 * index + 1] for index in range(7)]
    squares = [state[3 * index + 2] for index in range(7)]

    def flat_state(arrays):
        a, b, c, d, e, f, g = arrays
        return [a.transpose(1, 0, 2), b.T, c, d.T, e, f, g[:, 0, :]]

    def natural(arrays):
        a, b, c, d, e, f, g = arrays
        return [a.transpose(1, 0, 2), b.T, c, d.T, e, f, g[:, None, :]]

    masters, moments, squares = flat_state(masters), flat_state(moments), flat_state(squares)

    peers, cores = lax.axis_size("dp"), lax.axis_size("mp")
    me, core = lax.axis_index("dp"), lax.axis_index("mp")
    core_s = core.astype(jnp.int32).reshape(1)
    once_s = 1 - core_s
    model = tokens.shape[1]
    nviews, per_view = visible.shape
    episodes = counts.shape[0]
    views_each = nviews // episodes
    span = views_each * per_view
    size = -(-span // ROUND) * ROUND
    here = episodes // cores
    rows = here * size
    cells, dec = cotangent.shape[1:]
    part = masters[1].shape[1]
    hidden = masters[2].shape[1]
    shard_rows = masters[2].shape[0]
    room = (nviews + peers - 1) // peers
    npos = peers * room
    fast = peers == FAST_PEERS

    low = [m.astype(BF16) for m in masters]
    chunk_a = jnp.concatenate([low[0][0], low[0][1], low[0][2], low[1]], axis=1)
    chunk_b = low[2]
    chunk_c = jnp.concatenate([low[3], low[4]], axis=1)

    same = dest_device[:, None] == dest_device[None, :]
    earlier = jnp.arange(nviews)[None, :] < jnp.arange(nviews)[:, None]
    rank = jnp.sum((same & earlier).astype(jnp.int32), axis=1)
    where_view = (dest_device * room + rank).astype(jnp.int32)
    layout = jnp.arange(npos, dtype=jnp.int32)[:, None] == where_view[None, :]
    live_view = (
        jnp.arange(nviews, dtype=jnp.int32) % views_each < jnp.repeat(counts, views_each)
    ).astype(jnp.int32)
    details = jnp.concatenate(
        [jnp.ones((nviews, 1), jnp.int32), dest_slot[:, None], live_view[:, None], visible], axis=1
    )
    fields = details.shape[1]
    sent = jnp.dot(layout.astype(BF16), details.astype(BF16), preferred_element_type=F32)
    sent = sent.astype(BF16).reshape(peers, room * fields)
    small = jnp.concatenate([low[5].reshape(-1), low[6].reshape(-1)])
    message = jnp.concatenate(
        [sent, jnp.broadcast_to(small[None], (peers, small.shape[0]))], axis=1
    )
    message = jnp.broadcast_to(message[:, None], (peers, cores, message.shape[1]))
    if fast:
        gather = Gather((chunk_a, chunk_b, chunk_c), peers)
        z_one = gather.step_z((message,))
    message = lax.all_to_all(
        message.reshape(peers * cores, -1), AXES, split_axis=0, concat_axis=0, tiled=True
    ).reshape(peers, cores, -1)
    got = message[:, 0, : room * fields].reshape(npos, fields).astype(jnp.int32)
    nln = 4 * shard_rows
    ln_full = (
        message[:, 0, room * fields : room * fields + nln]
        .reshape(peers, 4, shard_rows)
        .transpose(1, 0, 2)
        .reshape(4, model)
        .astype(F32)
    )
    norms = jnp.concatenate([ln_full, jnp.zeros((4, model), F32)], axis=0)
    dec_full = (
        message[:, :, room * fields + nln :]
        .reshape(peers, cores, 2, dec // peers)
        .transpose(2, 1, 0, 3)
        .reshape(2, cores, dec)
        .astype(F32)
    )
    mask_token = lax.dynamic_index_in_dim(dec_full[1], core, 0, keepdims=True)
    held_slot = got[:, 1]
    filled = (held_slot[None, :] == jnp.arange(nviews, dtype=jnp.int32)[:, None]) & (
        got[:, 0][None, :] > 0
    )
    where_slot = jnp.sum(
        jnp.where(filled, jnp.arange(npos, dtype=jnp.int32)[None, :], 0), axis=1
    ).astype(jnp.int32)
    owned = jnp.dot(
        filled.astype(BF16), got.astype(BF16), preferred_element_type=F32
    ).astype(jnp.int32)
    live_slot, owned_spots = owned[:, 2], owned[:, 3:]
    each = 8
    groups = nviews // each
    marks = jnp.where(
        live_slot[:, None] > 0,
        owned_spots * each + (jnp.arange(nviews, dtype=jnp.int32) % each)[:, None],
        -1,
    )
    tall = -(-per_view // 8) * 8
    stride_take, stride_put = tall, -(-per_view // 64) * 64
    take_marks = jnp.pad(marks, ((0, 0), (0, stride_take - per_view)), constant_values=-1)
    take_marks = take_marks.reshape(nviews * stride_take, 1)
    put_marks = jnp.pad(marks, ((0, 0), (0, stride_put - per_view)), constant_values=-1)
    put_marks = put_marks.reshape(groups, 1, each * stride_put)
    live_row = jnp.broadcast_to(
        live_slot.astype(F32).reshape(groups, 1, each), (groups, cells, each)
    ).reshape(groups, 1, cells * each)

    take_call = pl.pallas_call(
        lambda *refs: take_cells(*refs, per_view=per_view, stride=stride_take),
        out_shape=[shape((npos, tall, dec), BF16), shape((8, dec))],
        grid_spec=pltpu.PrefetchScalarGridSpec(
            num_scalar_prefetch=1,
            grid=(groups,),
            in_specs=[
                pl.BlockSpec((each * stride_take, 1), lambda i, _: (i, 0)),
                pl.BlockSpec((1, 1, cells * each), lambda i, _: (i, 0, 0)),
                pl.BlockSpec((cells, each, dec), lambda i, _: (0, i, 0)),
            ],
            out_specs=[
                pl.BlockSpec((npos, tall, dec), lambda i, _: (0, 0, 0)),
                pl.BlockSpec((8, dec), lambda i, _: (0, 0)),
            ],
        ),
        compiler_params=params(),
        cost_estimate=cost(2 * nviews * stride_take * cells * each * dec, cotangent.size * 2),
        name="take_cells",
    )

    positions = lax.dynamic_slice_in_dim(
        grid_positions(math.isqrt(cells), dec * cores), core * dec, dec, 1
    )
    own = lax.dynamic_slice_in_dim(
        after(tokens, *z_one) if fast else tokens, core * (here * span), here * span, 0
    ).reshape(here, span, model)
    own = jnp.pad(own, ((0, 0), (0, size - span), (0, 0))).reshape(rows, model)
    begun = gather.step_near((take_marks, live_row, own)) if fast else []
    hold = after if fast else (lambda array, *others: array)
    leaves = jax.tree.leaves
    returned, dec_sums = take_call(
        where_slot, hold(take_marks, *begun), live_row, cotangent.transpose(1, 0, 2)
    )
    if fast:
        later = (positions, mask_token, put_marks, dec_full, norms)
        parts_a = gather.step_far((returned,) + later)
        positions, mask_token, put_marks, dec_full, norms = hold_all(later, parts_a[:1])
    else:
        parts_a = gather_plain(chunk_a)
    nparts = len(parts_a)
    table = gather_table(me, core)
    nsem = PIECE * nparts if fast else 1

    smem = pl.BlockSpec(memory_space=pltpu.SMEM)
    fixed = lambda dims: pl.BlockSpec(dims, lambda i: (0,) * len(dims))
    chunk_cols = [chunk_a.shape[1], chunk_b.shape[1], chunk_c.shape[1]]
    weight_bytes = [2 * 2 * model * cols for cols in chunk_cols]
    calls = 2 if here % 2 == 0 else 1
    each_call = here // calls

    def attn_forward_call(call, own, earlier):
        begin = call * each_call
        ep = lambda cols: pl.BlockSpec((size, cols), lambda i: (i + begin, 0))
        return pl.pallas_call(
            lambda *refs: attn_forward(
                *refs, nparts=nparts, per_view=per_view, part=part, begin=begin, here=here
            ),
            grid=(each_call,),
            out_shape=[
                shape((rows, model), BF16),
                shape((rows, 6 * part), BF16),
                shape((rows, 2 * part), BF16),
                shape((rows, model)),
                shape((rows, model), BF16),
                shape((rows, 2 * HEADDIM)),
            ],
            in_specs=[smem, smem, smem, ep(model), fixed((8, model))]
            + [any_spec()] * (nparts + len(earlier)),
            out_specs=[ep(model), ep(6 * part), ep(2 * part), ep(model), ep(model), ep(2 * HEADDIM)],
            scratch_shapes=[
                pltpu.VMEM((2, model, chunk_cols[0]), BF16),
                pltpu.SemaphoreType.DMA((nsem,)),
            ],
            input_output_aliases={5 + nparts + index: index for index in range(len(earlier))},
            compiler_params=params(),
            cost_estimate=cost(
                6 * rows * model * 8 * part // calls, weight_bytes[0] + rows * model * 16 // calls
            ),
            name="attn_forward",
        )(core_s, counts, table, own, norms, *parts_a, *earlier)

    attn = []
    for call in range(calls):
        gates = gather.later() if fast and call > 0 else []
        attn = attn_forward_call(call, after(own, *gates) if gates else own, attn)
        if call == 0 and fast:
            returned = after(returned, attn[0])
            gather.second(attn[0])
    if fast:
        parts_b, parts_c = gather.finish(attn[0])
    else:
        parts_b, parts_c = gather_plain(chunk_b), gather_plain(chunk_c)
    came_mine = lax.all_to_all(returned, "dp", split_axis=0, concat_axis=0, tiled=True)
    came_theirs = swap(came_mine, peers, 0, 1)
    first, packed, attended, middle, second, lse = attn

    group = 2
    chunk = group * size
    steps = here // group
    gviews = group * views_each
    blk = lambda cols: pl.BlockSpec((chunk, cols), lambda i: (i, 0))
    wide = hidden
    mlp_scratch = [
        pltpu.VMEM((2, model, chunk_cols[1]), BF16),
        pltpu.VMEM((2, model, chunk_cols[2]), BF16),
    ]
    act, slope, final, emb_keep, emb_send = pl.pallas_call(
        lambda *refs: mlp_forward(
            *refs, nparts=nparts, per_view=per_view, part=hidden, wide=wide, rows_each=size
        ),
        grid=(steps,),
        out_shape=[
            shape((rows, 2 * hidden), BF16),
            shape((rows, 2 * hidden), BF16),
            shape((rows, model), BF16),
            shape((steps * gviews, tall, dec), BF16),
            shape((steps * gviews, tall, dec), BF16),
        ],
        in_specs=[smem, smem, blk(model), blk(model), fixed((2, dec))] + [any_spec()] * (2 * nparts),
        out_specs=[
            blk(2 * hidden),
            blk(2 * hidden),
            blk(model),
            pl.BlockSpec((gviews, tall, dec), lambda i: (i, 0, 0)),
            pl.BlockSpec((gviews, tall, dec), lambda i: (i, 0, 0)),
        ],
        scratch_shapes=mlp_scratch + [pltpu.SemaphoreType.DMA((nsem,))] * 2,
        compiler_params=params(),
        cost_estimate=cost(
            4 * rows * model * 2 * hidden, weight_bytes[1] + weight_bytes[2] + rows * hidden * 8
        ),
        name="mlp_forward",
    )(core_s, table, second, middle, dec_full[0], *parts_b, *parts_c)

    where_mine = lax.dynamic_slice_in_dim(where_view, core * (nviews // cores), nviews // cores)
    emb_rows, glow, gpre, gmid, gmid_low, ln_two = pl.pallas_call(
        lambda *refs: mlp_backward(
            *refs, nparts=nparts, per_view=per_view, part=hidden, wide=wide, rows_each=size
        ),
        grid=(steps,),
        out_shape=[
            shape((rows, 2 * dec), BF16),
            shape((rows, model), BF16),
            shape((rows, 2 * hidden), BF16),
            shape((rows, model)),
            shape((rows, model), BF16),
            shape((8, model)),
        ],
        in_specs=[smem, smem, smem, any_spec(), any_spec(), blk(2 * hidden), blk(model), fixed((8, model))]
        + [any_spec()] * (2 * nparts),
        out_specs=[blk(2 * dec), blk(model), blk(2 * hidden), blk(model), blk(model), fixed((8, model))],
        scratch_shapes=mlp_scratch
        + [
            pltpu.VMEM((2, gviews, tall, dec), BF16),
            pltpu.VMEM((chunk, 2 * dec), F32),
            pltpu.SemaphoreType.DMA((nsem,)),
            pltpu.SemaphoreType.DMA((nsem,)),
            pltpu.SemaphoreType.DMA((2, gviews)),
        ],
        compiler_params=params(),
        cost_estimate=cost(
            4 * rows * model * 2 * hidden, weight_bytes[1] + weight_bytes[2] + rows * hidden * 8
        ),
        name="mlp_backward",
    )(core_s, where_mine, table, came_mine, came_theirs, slope, middle, norms, *parts_b, *parts_c)

    emb_other = swap(emb_send, peers, 0, 1)
    if fast:
        emb_other = after(emb_other, glow)
    outgoing = pl.pallas_call(
        order_views,
        out_shape=shape((npos, tall, dec), BF16),
        in_specs=[smem, smem, any_spec(), any_spec()],
        out_specs=any_spec(),
        scratch_shapes=[pltpu.SemaphoreType.DMA((nviews,))],
        compiler_params=params(8 << 20),
        cost_estimate=cost(0, 4 * nviews * per_view * dec),
        name="order_views",
    )(where_view, core_s, emb_keep, emb_other)
    arrived = lax.all_to_all(outgoing, "dp", split_axis=0, concat_axis=0, tiled=True)

    blocks = FAST_PEERS
    if fast:
        places = [place_table(me, core), place_table(me, 1 - core)]
    else:
        places = [jnp.arange(blocks, dtype=jnp.int32)] * 2

    deep = -(-rows // 256) * 256

    deep = -(-rows // 256) * 256

    def side_grads(pairs, block, name, other=None):
        lengths = [right.shape[1] // 2 // block for _, right in pairs]
        many = sum(lengths)
        begins = [sum(lengths[:index]) for index in range(len(lengths))]

        def column(begin, length):
            return lambda j, side, _: (0, side[0] * length + jnp.clip(j - begin, 0, length - 1))

        in_specs, operands = [], []
        for index, (left, right) in enumerate(pairs):
            in_specs += [
                pl.BlockSpec((rows, model), lambda j, *_: (0, 0)),
                pl.BlockSpec((rows, block), column(begins[index], lengths[index])),
            ]
            operands += [left, right]
        each_row = model // blocks
        spec = lambda count: pl.BlockSpec((count, each_row, block), lambda j, *_: (0, 0, j))
        dims = lambda count: shape((count, each_row, many * block), BF16)
        adding = other is not None
        return pl.pallas_call(
            lambda *refs: weight_grad(*refs, steps=lengths, rows_each=each_row, add_other=adding),
            out_shape=[dims(blocks // 2)] * 2 if adding else dims(blocks),
            grid_spec=pltpu.PrefetchScalarGridSpec(
                num_scalar_prefetch=2,
                grid=(many,),
                in_specs=in_specs + [spec(blocks)] * adding,
                out_specs=[spec(blocks // 2)] * 2 if adding else spec(blocks),
                scratch_shapes=[pltpu.VMEM((blocks, each_row, block), F32)] * adding
                + [pltpu.VMEM((deep, model), BF16), pltpu.VMEM((deep, block), BF16)],
            ),
            compiler_params=params(),
            cost_estimate=cost(2 * rows * model * many * block, 2 * rows * (many * block + model)),
            name=name,
        )(
            core_s if adding else 1 - core_s,
            places[0 if adding else 1],
            *operands,
            *([other] if adding else []),
        )

    def whole_grads(pairs, block, name):
        lengths = [right.shape[1] // 2 // block for _, right in pairs]
        many = sum(lengths)
        begins = [sum(lengths[:index]) for index in range(len(lengths))]

        def column(begin, length):
            return lambda h, j: (0, h * length + jnp.clip(j - begin, 0, length - 1))

        in_specs, operands = [], []
        for index, (left, right) in enumerate(pairs):
            in_specs += [
                pl.BlockSpec((rows, model), lambda h, j: (0, 0)),
                pl.BlockSpec((rows, block), column(begins[index], lengths[index])),
            ]
            operands += [left, right]
        return pl.pallas_call(
            lambda *refs: weight_grad(
                None, None, *refs, steps=lengths, rows_each=shard_rows, add_other=False
            ),
            out_shape=shape((peers, 2, shard_rows, many * block), BF16),
            grid=(2, many),
            in_specs=in_specs,
            out_specs=pl.BlockSpec((peers, 1, shard_rows, block), lambda h, j: (0, h, 0, j)),
            scratch_shapes=[pltpu.VMEM((deep, model), BF16), pltpu.VMEM((deep, block), BF16)],
            compiler_params=params(),
            cost_estimate=cost(4 * rows * model * many * block, 4 * rows * (many * block + model)),
            name=name,
        )(*operands)

    def attn_backward_call(call, mid, earlier):
        begin = call * each_call
        ep = lambda cols: pl.BlockSpec((size, cols), lambda i: (i + begin, 0))
        return pl.pallas_call(
            lambda *refs: attn_backward(
                *refs, nparts=nparts, per_view=per_view, part=part, begin=begin, here=here
            ),
            grid=(each_call,),
            out_shape=[
                shape((rows, 6 * part), BF16),
                shape((here, span, model), BF16),
                shape((8, model)),
            ],
            in_specs=[smem, smem, smem, ep(model), ep(6 * part), ep(2 * HEADDIM), ep(model), fixed((8, model))]
            + [any_spec()] * (nparts + len(earlier)),
            out_specs=[
                ep(6 * part),
                pl.BlockSpec((1, span, model), lambda i: (i + begin, 0, 0)),
                fixed((8, model)),
            ],
            scratch_shapes=[
                pltpu.VMEM((2, model, chunk_cols[0]), BF16),
                pltpu.SemaphoreType.DMA((nsem,)),
            ],
            input_output_aliases={8 + nparts + index: index for index in range(len(earlier))},
            compiler_params=params(),
            cost_estimate=cost(
                8 * rows * model * 8 * part // calls, weight_bytes[0] + rows * model * 16 // calls
            ),
            name="attn_backward",
        )(core_s, counts, table, own, packed, lse, mid, norms, *parts_a, *earlier)

    def behind(pairs, *gate):
        left, right = pairs[0]
        return [(left, hold(right, *gate))] + pairs[1:]

    pairs_b = [(second, gpre), (gmid_low, attended)]
    other_b = side_grads(behind(pairs_b, outgoing), part, "grad_up_out_send")
    whole_c = whole_grads(behind([(glow, act), (final, emb_rows)], other_b), 256, "grad_down_emb")
    sum_c = lax.psum_scatter(
        whole_c.reshape(peers * cores * shard_rows, -1), AXES, scatter_dimension=0, tiled=True
    ).astype(F32)
    got_b = hold(swap(other_b, peers, 0, 1), whole_c)
    keep, send = side_grads(behind(pairs_b, whole_c), part, "grad_up_out_keep", got_b)
    sum_b = [(keep,), send]
    ln_one = jnp.zeros((8, model), F32)
    back = []
    for call in range(calls):
        gates = (keep, arrived) if call == 0 else leaves(sum_b[1])
        *back, sums = attn_backward_call(call, hold(gmid, *gates), back)
        ln_one = ln_one + sums
        if call == 0:
            sum_b = scatter_near(sum_b, peers, back[0])
    grad_packed, grad_own = back
    sum_b = scatter_far(sum_b, peers, grad_own)
    pairs_a = [(first, grad_packed)]
    other_a = side_grads(behind(pairs_a, *leaves(sum_b[1])), part, "grad_in_send")

    grad_other = swap(grad_own, peers, 0, 1)
    grad_tokens = jnp.where(
        core == 0,
        jnp.concatenate([grad_own, grad_other]),
        jnp.concatenate([grad_other, grad_own]),
    ).reshape(tokens.shape)

    decoded = pl.pallas_call(
        lambda *refs: put_cells(*refs, per_view=per_view),
        out_shape=shape((cells, nviews, dec), BF16),
        grid_spec=pltpu.PrefetchScalarGridSpec(
            num_scalar_prefetch=2,
            grid=(groups,),
            in_specs=[
                pl.BlockSpec((1, 1, each * stride_put), lambda i, *_: (i, 0, 0)),
                pl.BlockSpec((1, dec), lambda i, *_: (0, 0)),
                pl.BlockSpec((cells, dec), lambda i, *_: (0, 0)),
                pl.BlockSpec((npos, tall, dec), lambda i, *_: (0, 0, 0)),
            ],
            out_specs=pl.BlockSpec((cells, each, dec), lambda i, *_: (0, i, 0)),
            scratch_shapes=[pltpu.VMEM((each * stride_put, dec), BF16)],
        ),
        compiler_params=params(),
        cost_estimate=cost(2 * nviews * stride_put * cells * each * dec, cotangent.size * 2),
        name="put_cells",
    )(where_slot, live_slot, hold(put_marks, other_a), mask_token, positions, arrived)
    got_a = hold(swap(other_a, peers, 0, 1), decoded)
    keep, send = side_grads(behind(pairs_a, decoded), part, "grad_in_keep", got_a)
    sum_a = [(keep,), send]
    ln_sums = jnp.concatenate([hold(ln_one[:2], keep), ln_two[:2]])
    ln_send = ln_sums.reshape(4, peers, shard_rows).transpose(1, 0, 2).reshape(peers, nln)
    dec_send = dec_sums[:2].reshape(2, peers, dec // peers).transpose(1, 0, 2).reshape(peers, -1)
    small_send = jnp.concatenate([ln_send, dec_send], axis=1)
    small_send = jnp.broadcast_to(small_send[:, None], (peers, cores, small_send.shape[1]))
    small_got = lax.all_to_all(
        small_send.reshape(peers * cores, -1), AXES, split_axis=0, concat_axis=0, tiled=True
    ).reshape(peers, cores, -1)
    grad_ln = jnp.sum(small_got[:, :, :nln], axis=(0, 1)).reshape(4, shard_rows)
    grad_dec = jnp.sum(
        lax.dynamic_index_in_dim(small_got[:, :, nln:], core, 1, keepdims=False), axis=0
    ).reshape(2, dec // peers)

    sum_a = scatter_near(sum_a, peers, grad_tokens, grad_ln)
    sum_b = scatter_end(sum_b, peers, *leaves(sum_a[1])) if fast else scatter_end(sum_b, peers)
    sum_a = scatter_far(sum_a, peers, sum_b)
    sum_a = scatter_end(sum_a, peers)
    decoded = decoded.transpose(1, 0, 2)

    grads = [sum_a, sum_b, sum_c, grad_ln, grad_dec]
    world = peers * cores
    (tiles,) = whole(squares_kernel, [shape((world, 1, 128))], [once_s], grads + masters, name="squares")
    tiles = lax.all_to_all(tiles, AXES, split_axis=0, concat_axis=0, tiled=True)
    same_shapes = [shape(m.shape) for m in masters]
    lamb = whole(
        lamb_kernel,
        same_shapes * 4 + [shape((1, 128)), shape((world, 1, 128))],
        [once_s],
        [tiles] + grads + masters + moments + squares,
        name="lamb",
    )
    summed = lamb[28]
    steps_tiles = lax.all_to_all(lamb[29], AXES, split_axis=0, concat_axis=0, tiled=True)
    update = whole(
        update_kernel,
        same_shapes + [shape(m.shape, BF16) for m in masters] + [shape((2, 7)), shape((1, 1))],
        [],
        [steps_tiles, summed] + masters + list(lamb[21:28]),
        name="update",
    )
    results = [
        natural(group)
        for group in (lamb[:7], lamb[7:14], lamb[14:21], update[:7], update[7:14])
    ]
    outs = [decoded, grad_tokens, update[15].reshape(1), update[14]]
    for index in range(7):
        outs += [group[index] for group in results]
    return tuple(outs)


def solution(mesh):
    tensor_specs = [
        P("dp", None, "mp"),
        P("mp", "dp"),
        P("dp", "mp"),
        P("mp", "dp"),
        P("dp", "mp"),
        P(None, "dp"),
        P(None, "mp", "dp"),
    ]
    in_specs = (
        P("dp", None),
        P("dp"),
        P("dp", None),
        P("dp"),
        P("dp"),
        P("dp", None, "mp"),
    ) + tuple(spec for spec in tensor_specs for _ in range(3))
    out_specs = (P("dp", None, "mp"), P("dp", None), P(), P()) + tuple(
        spec for spec in tensor_specs for _ in range(5)
    )
    return jax.shard_map(
        per_device, mesh=mesh, in_specs=in_specs, out_specs=out_specs, check_vma=False
    )
```

```python
import math

import jax
import jax.numpy as jnp
from jax import lax
from jax.experimental import pallas as pl
from jax.experimental.pallas import tpu as pltpu
from jax.sharding import PartitionSpec as P

HEADDIM = 64
PARAMS = 7475200
NORM_EPS = 1e-06
MASK_FILL = -1e30
BETA_ONE = 0.5
BETA_TWO = 0.5
ADAM_EPS = 1e-06
DECAY_RATE = 0.01
LEARN_RATE = 0.5
TRUST_EPS = 1e-06

F32 = jnp.float32
BF16 = jnp.bfloat16
AXES = ("dp", "mp")
NT = (((1,), (1,)), ((), ()))
TN = (((0,), (0,)), ((), ()))
ROUND = 16
VMEM_BYTES = 58 << 20
COST = 3.0


def mm(a, b, dims=(((1,), (0,)), ((), ()))):
    return lax.dot_general(a, b, dims, preferred_element_type=F32)


def norm_rows(values):
    centre = values - jnp.mean(values, axis=-1, keepdims=True)
    spread = jnp.mean(centre * centre, axis=-1, keepdims=True)
    inverse = lax.rsqrt(spread + NORM_EPS)
    return centre * inverse, inverse


def norm_back(scaled, normed, inverse):
    return inverse * (
        scaled
        - jnp.mean(scaled, axis=-1, keepdims=True)
        - normed * jnp.mean(scaled * normed, axis=-1, keepdims=True)
    )


def grid_positions(side, width):
    quarter = width // 4
    rate = 1.0 / 10000.0 ** (jnp.arange(quarter, dtype=F32) / quarter)
    place = jnp.arange(side * side, dtype=jnp.int32)
    row_pos = (place // side).astype(F32)
    col_pos = (place % side).astype(F32)
    row_angle = row_pos[:, None] * rate[None, :]
    col_angle = col_pos[:, None] * rate[None, :]
    return jnp.concatenate(
        [jnp.sin(row_angle), jnp.cos(row_angle), jnp.sin(col_angle), jnp.cos(col_angle)], axis=1
    )


def any_spec():
    return pl.BlockSpec(memory_space=pl.ANY)


def params(limit=VMEM_BYTES):
    return pltpu.CompilerParams(vmem_limit_bytes=limit)


def cost(flops, nbytes):
    return pl.CostEstimate(flops=int(COST * flops), bytes_accessed=int(nbytes), transcendentals=0)


def swap(array, peers, bits, core=0):
    bits = bits if isinstance(bits, tuple) else (bits, bits)
    pairs = [
        (d * 2 + m, (d ^ bits[m]) * 2 + (m ^ core)) for d in range(peers) for m in range(2)
    ]
    return lax.ppermute(array, AXES, pairs)


FAST_PEERS = 16
Z_STEPS = (4, 8, 12)


def after(array, *others):
    return lax.optimization_barrier((array,) + others)[0]


def reach_z(shard, peers):
    return [swap(shard, peers, bits) for bits in Z_STEPS]


def hold_all(arrays, others):
    return list(lax.optimization_barrier((tuple(arrays), tuple(others)))[0])


def gather_plain(shard):
    return [lax.all_gather(lax.all_gather(shard, "dp", axis=0, tiled=True), "mp", axis=0)]


class Gather:
    def __init__(self, shards, peers):
        self.peers = peers
        self.one, self.two, self.three = shards

    def near(self, array):
        return swap(array, self.peers, (1, 2))

    def far(self, array):
        return swap(array, self.peers, (2, 1))

    def across(self, array):
        return swap(array, self.peers, 0, 1)

    def step_z(self, beside):
        z_one = reach_z(self.one, self.peers)
        (self.along_one,) = hold_all([jnp.stack([self.one] + z_one)], beside)
        (self.two,) = hold_all([self.two], z_one)
        return z_one

    def step_near(self, beside):
        near_one, z_two = self.near(self.along_one), reach_z(self.two, self.peers)
        (self.half_one,) = hold_all([jnp.concatenate([self.along_one, near_one])], beside)
        self.along_two, self.three = hold_all(
            [jnp.stack([self.two] + z_two), self.three], [near_one] + z_two
        )
        return [near_one]

    def step_far(self, beside):
        far_one, side_one = self.far(self.half_one), self.across(self.half_one)
        near_two, z_three = self.near(self.along_two), reach_z(self.three, self.peers)
        far_one, half_two, along_three = hold_all(
            [far_one, jnp.concatenate([self.along_two, near_two]), jnp.stack([self.three] + z_three)],
            [far_one, near_two] + z_three + list(beside),
        )
        self.half_two, self.along_three = half_two, along_three
        self.far_two, self.side_two = self.far(half_two), self.across(half_two)
        self.near_three = self.near(along_three)
        return [self.half_one, far_one, side_one, self.across(far_one)]

    def later(self):
        return [self.far_two, self.near_three, self.side_two]

    def second(self, beside):
        far_two, along_three, near_three = hold_all(
            [self.far_two, self.along_three, self.near_three], [beside]
        )
        self.half_three = jnp.concatenate([along_three, near_three])
        self.far_three, self.side_three = self.far(self.half_three), self.across(self.half_three)
        self.parts_two = [self.half_two, far_two, self.side_two, self.across(far_two)]

    def finish(self, beside):
        (far_three,) = hold_all([self.far_three], [beside] + self.parts_two[2:])
        parts_three = [self.half_three, far_three, self.side_three, self.across(far_three)]
        return self.parts_two, parts_three


PIECE = 8


def gather_table(me, core):
    one = jnp.where(core == 0, 1, 2)
    two = 3 - one
    along = jnp.array((0,) + Z_STEPS, jnp.int32)
    mine = jnp.concatenate([along, along ^ one])
    theirs = jnp.concatenate([along, along ^ two])
    apart = jnp.concatenate([mine, mine ^ two, theirs, theirs ^ one])
    cores = jnp.stack([core, core, 1 - core, 1 - core])
    return jnp.concatenate([me ^ apart, cores]).astype(jnp.int32)


def weight_copies(parts, table, target, sems):
    if len(parts) == 1:
        return [pltpu.make_async_copy(parts[0], target, sems.at[0])]
    copies = []
    for index, part in enumerate(parts):
        half = table[len(parts) * PIECE + index]
        for inner in range(PIECE):
            at = index * PIECE + inner
            rows = part.shape[1]
            start = pl.multiple_of(table[at] * rows, ROUND)
            copies.append(
                pltpu.make_async_copy(
                    part.at[inner], target.at[half, pl.ds(start, rows), :], sems.at[at]
                )
            )
    return copies


def place_table(me, core):
    near = jnp.where(core == 0, 2, 1)
    far = 3 - near
    apart = jnp.arange(FAST_PEERS, dtype=jnp.int32) ^ me
    return (
        jnp.where((apart & near) != 0, 8, 0) + jnp.where((apart & far) != 0, 4, 0) + (apart >> 2)
    ).astype(jnp.int32)


def add(*terms):
    return sum(term.astype(F32) for term in terms)


def scatter_near(state, peers, *held):
    if peers != FAST_PEERS:
        return state
    terms, send = state
    got = swap(send, peers, (2, 1))
    terms = terms + (after(got, *held) if held else got,)
    return [terms, add(*(term[4:8] for term in terms)).astype(BF16)]


def scatter_far(state, peers, *held):
    if peers != FAST_PEERS:
        return state
    terms, send = state
    got = swap(send, peers, (1, 2))
    terms = terms + (after(got, *held) if held else got,)
    return [terms, tuple(add(*(term[i] for term in terms)).astype(BF16) for i in (1, 2, 3))]


def scatter_end(state, peers, *held):
    if peers != FAST_PEERS:
        (keep,), send = state
        whole = jnp.concatenate([keep, send]).astype(F32)
        return lax.psum_scatter(
            whole.reshape(-1, whole.shape[-1]), "dp", scatter_dimension=0, tiled=True
        )
    terms, sends = state
    last = [swap(send, peers, bits) for send, bits in zip(sends, Z_STEPS)]
    last = hold_all(last, held) if held else last
    return add(*(term[0] for term in terms), *last)


def view_of(rows, per_view):
    view = jnp.zeros_like(rows)
    for edge in range(1, 5):
        view = view + (rows >= edge * per_view).astype(jnp.int32)
    return view


def allowed_bias(size, count, per_view):
    query = view_of(lax.broadcasted_iota(jnp.int32, (size, size), 0), per_view)
    key = view_of(lax.broadcasted_iota(jnp.int32, (size, size), 1), per_view)
    return jnp.where((key < count) | (key == query), 0.0, MASK_FILL)


def pair_masks(scale):
    lane = lax.broadcasted_iota(jnp.int32, (1, 2 * HEADDIM), 1)
    low = (lane < HEADDIM).astype(F32)
    return (low * scale).astype(BF16), ((1.0 - low) * scale).astype(BF16)


PARTS = 16


def head_lanes(head):
    lane = lax.broadcasted_iota(jnp.int32, (1, 2 * HEADDIM), 1)
    return ((lane & (PARTS - 1)) == head) & (lane < 3 * PARTS)


def in_parts(values):
    lane = lax.broadcasted_iota(jnp.int32, values.shape, 1)
    high = values.astype(BF16).astype(F32)
    rest = values - high
    middle = rest.astype(BF16).astype(F32)
    return jnp.where(lane < PARTS, high, jnp.where(lane < 2 * PARTS, middle, rest - middle)).astype(BF16)


def attn_forward(mp_s, counts_s, table, tokens, norms, *rest, nparts, per_view, part, begin, here):
    parts = rest[:nparts]
    first_o, packed_o, attended_o, middle_o, second_o, lse_o, weights, sems = rest[-8:]
    step = pl.program_id(0)
    copies = weight_copies(parts, table, weights, sems)

    @pl.when(step == 0)
    def _():
        for copy in copies:
            copy.start()
        for copy in copies:
            copy.wait()

    size = tokens.shape[0]
    scale = 1.0 / math.sqrt(HEADDIM)
    values = tokens[...].astype(F32)
    normed, _ = norm_rows(values)
    first = (normed * norms[0:1, :] + norms[1:2, :]).astype(BF16)
    first_o[...] = first
    bias = allowed_bias(size, counts_s[mp_s[0] * here + begin + step], per_view)
    bias = jnp.concatenate([bias, bias], axis=0)
    masks = pair_masks(scale)
    lane = lax.broadcasted_iota(jnp.int32, (size, 2 * HEADDIM), 1)
    wide = 2 * HEADDIM
    lse = jnp.zeros((size, wide), F32)
    ones = jnp.ones((size, wide), BF16)
    attn = jnp.zeros(values.shape, F32)
    for half in range(2):
        packed = mm(first, weights[half, :, : 3 * part]).astype(BF16)
        packed_o[:, half * 3 * part : (half + 1) * 3 * part] = packed
        pairs = range(part // wide)
        logits, probs = [], []
        for pair in pairs:
            at = pair * wide
            query = packed[:, at : at + wide]
            key = packed[:, part + at : part + at + wide]
            both = jnp.concatenate([query * masks[0], query * masks[1]], axis=0)
            logits.append(mm(both, key, NT) + bias)
        tops = []
        for pair in pairs:
            top = jnp.max(logits[pair], axis=-1, keepdims=True)
            probs.append(jnp.exp(logits[pair] - top).astype(BF16))
            tops.append(top)
        for pair in pairs:
            at = pair * wide
            value = packed[:, 2 * part + at : 2 * part + at + wide]
            outs = mm(probs[pair], jnp.concatenate([value, ones], axis=1))
            totals = outs[:, wide:]
            outs = outs[:, :wide] / totals
            low_lse = -(tops[pair] + jnp.log(totals))
            index = half * (part // HEADDIM) + pair * 2
            lse = jnp.where(head_lanes(index), low_lse[:size], lse)
            lse = jnp.where(head_lanes(index + 1), low_lse[size:], lse)
            both = jnp.where(lane < HEADDIM, outs[:size], outs[size:]).astype(BF16)
            attended_o[:, half * part + at : half * part + at + wide] = both
        attn = attn + mm(
            attended_o[:, half * part : (half + 1) * part], weights[half, :, 3 * part :], NT
        )
    lse_o[...] = in_parts(lse)
    middle = values + attn
    middle_o[...] = middle
    normed, _ = norm_rows(middle)
    second_o[...] = (normed * norms[2:3, :] + norms[3:4, :]).astype(BF16)


def mlp_forward(mp_s, table, second, middle, dec_bias, *rest, nparts, per_view, part, wide, rows_each):
    up_parts, down_parts = rest[:nparts], rest[nparts : 2 * nparts]
    act_o, slope_o, final_o, keep_o, send_o = rest[2 * nparts : 2 * nparts + 5]
    up, down, up_sems, down_sems = rest[2 * nparts + 5 :]
    up_copies = weight_copies(up_parts, table, up, up_sems)
    down_copies = weight_copies(down_parts, table, down, down_sems)

    @pl.when(pl.program_id(0) == 0)
    def _():
        for copy in up_copies + down_copies:
            copy.start()
        for copy in up_copies + down_copies:
            copy.wait()

    acc = middle[...]
    rows = second[...]
    for half in range(2):
        for start in range(0, part, wide):
            pre = mm(rows, up[half, :, start : start + wide])
            cumulative = 0.5 * (1.0 + lax.erf(pre * (1.0 / math.sqrt(2.0))))
            act = (pre * cumulative).astype(BF16)
            slope = cumulative + pre * jnp.exp(-0.5 * pre * pre) * (1.0 / math.sqrt(2.0 * math.pi))
            act_o[:, half * part + start : half * part + start + wide] = act
            slope_o[:, half * part + start : half * part + start + wide] = slope.astype(BF16)

            acc = acc + mm(act, down[half, :, start : start + wide], NT)
    final = acc.astype(BF16)
    final_o[...] = final
    outs = [
        mm(final, down[half, :, part:]) + dec_bias[half : half + 1, :] for half in range(2)
    ]
    mine = jnp.where(mp_s[0] == 0, outs[0], outs[1])
    theirs = jnp.where(mp_s[0] == 0, outs[1], outs[0])
    views = rows_each // per_view
    for view in range(keep_o.shape[0]):
        at = (view // views) * rows_each + (view % views) * per_view
        keep_o[view, :per_view, :] = mine[at : at + per_view].astype(BF16)
        send_o[view, :per_view, :] = theirs[at : at + per_view].astype(BF16)


def mlp_backward(
    mp_s, where_s, table, mine, theirs, slope, middle, norms, *rest, nparts, per_view, part, wide, rows_each
):
    up_parts, down_parts = rest[:nparts], rest[nparts : 2 * nparts]
    rows_o, low_o, pre_o, mid_o, midlow_o, sums_o = rest[2 * nparts : 2 * nparts + 6]
    up, down, pieces, flat, up_sems, down_sems, piece_sems = rest[2 * nparts + 6 :]
    step = pl.program_id(0)
    nviews = pieces.shape[1]
    up_copies = weight_copies(up_parts, table, up, up_sems)
    down_copies = weight_copies(down_parts, table, down, down_sems)
    fetch = []
    for view in range(nviews):
        at = where_s[step * nviews + view]
        fetch.append(
            pltpu.make_async_copy(mine.at[at], pieces.at[mp_s[0], view], piece_sems.at[0, view])
        )
        fetch.append(
            pltpu.make_async_copy(theirs.at[at], pieces.at[1 - mp_s[0], view], piece_sems.at[1, view])
        )
    for copy in fetch:
        copy.start()

    @pl.when(step == 0)
    def _():
        for copy in down_copies + up_copies:
            copy.start()
        flat[...] = jnp.zeros_like(flat)
        sums_o[...] = jnp.zeros_like(sums_o)
        for copy in down_copies + up_copies:
            copy.wait()

    for copy in fetch:
        copy.wait()
    dec = pieces.shape[3]
    views = rows_each // per_view
    for view in range(nviews):
        at = (view // views) * rows_each + (view % views) * per_view
        for half in range(2):
            flat[at : at + per_view, half * dec : (half + 1) * dec] = pieces[half, view][
                :per_view
            ].astype(F32)
    rows = flat[...].astype(BF16)
    rows_o[...] = rows
    final = mm(rows[:, :dec], down[0, :, part:], NT) + mm(rows[:, dec:], down[1, :, part:], NT)
    low = final.astype(BF16)
    low_o[...] = low
    acc = jnp.zeros(final.shape, F32)
    for half in range(2):
        for start in range(0, part, wide):
            at = half * part + start
            hidden = mm(low, down[half, :, start : start + wide])
            pre = (hidden * slope[:, at : at + wide].astype(F32)).astype(BF16)
            pre_o[:, at : at + wide] = pre

            acc = acc + mm(pre, up[half, :, start : start + wide], NT)
    normed, inverse = norm_rows(middle[...])
    sums_o[0:1, :] += jnp.sum(acc * normed, axis=0, keepdims=True)
    sums_o[1:2, :] += jnp.sum(acc, axis=0, keepdims=True)
    mid = final + norm_back(acc * norms[2:3, :], normed, inverse)
    mid_o[...] = mid
    midlow_o[...] = mid.astype(BF16)


def attn_backward(
    mp_s, counts_s, table, tokens, packed, attended, lse, mid, norms, *rest, nparts, per_view, part, begin, here, rows_out
):
    parts = rest[:nparts]
    packed_o, tokens_o, sums_o, weights, sems = rest[-5:]
    earlier = rest[-6] if begin else None
    step = pl.program_id(0)
    copies = weight_copies(parts, table, weights, sems)

    @pl.when(step == 0)
    def _():
        for copy in copies:
            copy.start()
        sums_o[...] = jnp.zeros_like(sums_o)
        for copy in copies:
            copy.wait()

    size = tokens.shape[0]
    scale = 1.0 / math.sqrt(HEADDIM)
    wide = 2 * HEADDIM
    bias = allowed_bias(size, counts_s[mp_s[0] * here + begin + step], per_view)
    bias = jnp.concatenate([bias, bias], axis=0)
    masks, scaled = pair_masks(1.0), pair_masks(scale)
    key_scale = jnp.full((1, wide), scale, F32).astype(BF16)
    lane = lax.broadcasted_iota(jnp.int32, (size, wide), 1)
    low = lane < HEADDIM
    ones = jnp.ones((size, wide), BF16)
    shifts = lse[...]
    owner = lax.broadcasted_iota(jnp.int32, (part, wide), 0) // HEADDIM
    slot = lax.broadcasted_iota(jnp.int32, (part, wide), 1)
    owners = [
        (((slot & (PARTS - 1)) == owner + half * (part // HEADDIM)) & (slot < 3 * PARTS))
        .astype(F32)
        .astype(BF16)
        for half in range(2)
    ]
    middle = mid[...]
    middle_low = middle.astype(BF16)
    back = jnp.zeros(middle.shape, F32)
    for half in range(2):
        grad_att = mm(middle_low, weights[half, :, 3 * part :]).astype(BF16)
        base = half * 3 * part
        pairs = range(part // wide)
        weighted = grad_att.astype(F32) * attended[:, half * part : (half + 1) * part].astype(F32)
        high = weighted.astype(BF16)
        centre = mm(high, owners[half]) + mm((weighted - high.astype(F32)).astype(BF16), owners[half])
        centre = in_parts(-centre)
        sides, logits, grad_probs, lows = [], [], [], []
        for pair in pairs:
            at = pair * wide
            query = packed[:, base + at : base + at + wide]
            key = packed[:, base + part + at : base + part + at + wide]
            value = packed[:, base + 2 * part + at : base + 2 * part + at + wide]
            grad = grad_att[:, at : at + wide]
            query = jnp.concatenate([query * scaled[0], query * scaled[1]], axis=0)
            grad = jnp.concatenate([grad * masks[0], grad * masks[1]], axis=0)
            index = half * (part // HEADDIM) + pair * 2
            picks = [head_lanes(index + which).astype(F32).astype(BF16) for which in range(2)]
            minus_lse = jnp.concatenate([shifts * pick for pick in picks], axis=0)
            minus_centre = jnp.concatenate([centre * pick for pick in picks], axis=0)
            sides.append((query, key * key_scale, grad))
            logits.append(
                mm(
                    jnp.concatenate([query, minus_lse], axis=1),
                    jnp.concatenate([key, ones], axis=1),
                    NT,
                )
                + bias
            )
            grad_probs.append(
                mm(
                    jnp.concatenate([grad, minus_centre], axis=1),
                    jnp.concatenate([value, ones], axis=1),
                    NT,
                )
            )
        for pair in pairs:
            probs = jnp.exp(logits[pair])
            lows.append(((probs * grad_probs[pair]).astype(BF16), probs.astype(BF16)))
        for pair in pairs:
            query, key, grad = sides[pair]
            scores, probs = lows[pair]
            at = base + pair * wide
            grad_query = mm(scores, key)
            packed_o[:, at : at + wide] = jnp.where(
                low, grad_query[:size], grad_query[size:]
            ).astype(BF16)
            at = at + part
            packed_o[:, at : at + wide] = mm(query, scores, TN).T.astype(BF16)
            at = at + part
            packed_o[:, at : at + wide] = mm(grad, probs, TN).T.astype(BF16)
        back = back + mm(packed_o[:, base : base + 3 * part], weights[half, :, : 3 * part], NT)
    normed, inverse = norm_rows(tokens[...].astype(F32))
    sums_o[0:1, :] += jnp.sum(back * normed, axis=0, keepdims=True)
    sums_o[1:2, :] += jnp.sum(back, axis=0, keepdims=True)
    grads = middle + norm_back(back * norms[0:1, :], normed, inverse)
    span = rows_out
    if tokens_o.ndim == 3:
        tokens_o[0] = grads[:span].astype(BF16)
    else:
        for index in range(tokens_o.shape[0] // span - begin):

            @pl.when(step == index)
            def _(index=index):
                at = (begin + index) * span
                tokens_o[at : at + span, :] = grads[:span].astype(BF16)

        if earlier is not None:

            @pl.when(step == 0)
            def _():
                for index in range(begin):
                    tokens_o[index * span : (index + 1) * span, :] = earlier[index]


def weight_grad(side_s, places, *rest, steps, rows_each, add_other):
    count = len(steps)
    sides, rest = rest[: 2 * count], rest[2 * count :]
    left_pad, right_pad = rest[-2:]
    step = pl.program_id(0 if places is not None else 1)
    begin = 0

    @pl.when(step == 0)
    def _():
        left_pad[...] = jnp.zeros_like(left_pad)
        right_pad[...] = jnp.zeros_like(right_pad)

    for index, length in enumerate(steps):
        left, right = sides[2 * index], sides[2 * index + 1]

        @pl.when(step == begin)
        def _(left=left):
            left_pad[: left.shape[0], :] = left[...]

        @pl.when((step >= begin) & (step < begin + length))
        def _(right=right):
            right_pad[: right.shape[0], :] = right[...]

        begin += length
    product = mm(left_pad[...], right_pad[...], TN)
    if places is None:
        grads_o = rest[0]
        for block in range(grads_o.shape[0]):
            grads_o[block, 0] = product[block * rows_each : (block + 1) * rows_each].astype(BF16)
    elif add_other:
        other, keep_o, send_o, held = rest[:4]
        half = keep_o.shape[0]
        for block in range(2 * half):
            held[places[block]] = product[block * rows_each : (block + 1) * rows_each]
        keep_o[...] = (held[:half] + other[:half].astype(F32)).astype(BF16)
        send_o[...] = (held[half:] + other[half:].astype(F32)).astype(BF16)
    else:
        product = product.astype(BF16)
        grads_o = rest[0]
        for block in range(grads_o.shape[0]):
            grads_o[places[block]] = product[block * rows_each : (block + 1) * rows_each]


def take_cells(where_s, marks, live_row, cells, rows_o, sums_o, *, per_view, stride):
    step = pl.program_id(0)

    @pl.when(step == 0)
    def _():
        sums_o[...] = jnp.zeros_like(sums_o)

    grid, each, dec = cells.shape
    flat = cells[...].reshape(grid * each, dec)
    lane = lax.broadcasted_iota(jnp.int32, (each * stride, grid * each), 1)
    pick = (marks[...] == lane).astype(F32)
    covered = jnp.sum(pick, axis=0, keepdims=True)
    open_cells = jnp.broadcast_to(live_row[0] - covered, (8, grid * each)).astype(BF16)
    taken = mm(pick.astype(BF16), flat)
    masked = mm(open_cells, flat)
    for index in range(each):
        rows_o[where_s[step * each + index]] = taken[index * stride : (index + 1) * stride].astype(BF16)
    sums_o[0:1, :] += jnp.sum(taken, axis=0, keepdims=True)
    sums_o[1:2, :] += masked[0:1]


def put_cells(where_s, live_s, marks, mask, positions, rows, cells_o, held, *, per_view):
    step = pl.program_id(0)
    grid, each, dec = cells_o.shape
    stride = held.shape[0] // each

    @pl.when(step == 0)
    def _():
        held[...] = jnp.zeros_like(held)

    slot = lax.broadcasted_iota(jnp.int32, (1, each, 1), 1)
    live = jnp.zeros((1, each, 1), F32)
    for index in range(each):
        at = step * each + index
        held[index * stride : index * stride + per_view, :] = rows[where_s[at]][:per_view]
        live = jnp.where(slot == index, live_s[at].astype(F32), live)
    line = lax.broadcasted_iota(jnp.int32, (grid * each, held.shape[0]), 0)
    place = (marks[0] == line).astype(F32)
    covered = jnp.sum(place, axis=1, keepdims=True)
    live = jnp.broadcast_to(live, (grid, each, 1)).reshape(grid * each, 1)
    filled = mm(place.astype(BF16), held[...]) + (live - covered) * mask[...]
    filled = filled.reshape(grid, each, dec) + positions[...][:, None, :]
    cells_o[...] = filled.astype(BF16)


def order_views(where_s, mp_s, own, theirs, out, sems):
    count = own.shape[0]
    copies = []
    for view in range(count):
        mine, other = mp_s[0] * count + view, (1 - mp_s[0]) * count + view
        copies.append(pltpu.make_async_copy(own.at[view], out.at[where_s[mine]], sems.at[view]))
        copies.append(
            pltpu.make_async_copy(theirs.at[view], out.at[where_s[other]], sems.at[count + view])
        )
    for copy in copies:
        copy.start()
    for copy in copies:
        copy.wait()


def tile_of(scalars, begin=0):
    lane = lax.broadcasted_iota(jnp.int32, (1, 128), 1)
    tile = jnp.zeros((1, 128), F32)
    for index, value in enumerate(scalars):
        tile = jnp.where(lane == begin + index, value, tile)
    return tile


def total(values):
    return jnp.sum(jnp.sum(values, axis=1, keepdims=True), axis=0, keepdims=True)


def grad_views(refs, masters):
    first, second, third, norms, dec = refs
    wide, thin = masters[2].shape[1], masters[4].shape[1]
    return [
        first,
        second.at[:, pl.ds(wide, masters[1].shape[1])],
        second.at[:, pl.ds(0, wide)],
        third.at[:, pl.ds(0, wide)],
        third.at[:, pl.ds(wide, thin)],
        norms,
        dec,
    ]


def squares_kernel(once_s, *refs):
    masters, (tiles_o,) = refs[5:12], refs[12:]
    grads = grad_views(refs[:5], masters)
    single = [1.0] * 5 + [once_s[0].astype(F32), 1.0]
    grad_sq, weight_sq = [], []
    for index in range(7):
        value = grads[index][...].astype(F32)
        grad_sq.append(total(value * value) * single[index])
        if index == 0:
            weight = sum(total(masters[0][k] * masters[0][k]) for k in range(3))
        else:
            weight = total(masters[index][...] * masters[index][...])
        weight_sq.append(weight * single[index])
    tile = tile_of(grad_sq) + tile_of(weight_sq, 64)
    for peer in range(tiles_o.shape[0]):
        tiles_o[peer] = tile


def lamb_kernel(once_s, tiles, *refs):
    masters, moments, squares = refs[5:12], refs[12:19], refs[19:26]
    grads = grad_views(refs[:5], masters)
    outs = refs[26:]
    clip_o, moment_o, square_o, step_o = outs[:7], outs[7:14], outs[14:21], outs[21:28]
    sum_o, tiles_o = outs[28:]
    summed = jnp.sum(tiles[...], axis=0)
    sum_o[...] = summed
    lane = lax.broadcasted_iota(jnp.int32, (1, 128), 1)
    clip = jnp.sqrt(total(jnp.where(lane < 7, summed, 0.0)))
    factor = jnp.minimum(1.0, 0.5 * math.sqrt(PARAMS) / clip)
    single = [1.0] * 5 + [once_s[0].astype(F32), 1.0]
    update_sq = []
    for index in range(7):
        amount = jnp.zeros((1, 1), F32)
        for piece in range(3 if index == 0 else 1):
            at = piece if index == 0 else Ellipsis
            value = grads[index][...].astype(F32)
            if index == 0:
                width = masters[0].shape[2]
                value = value[:, piece * width : (piece + 1) * width]
            clipped = value * factor
            moment = BETA_ONE * moments[index][at] + (1.0 - BETA_ONE) * clipped
            square = BETA_TWO * squares[index][at] + (1.0 - BETA_TWO) * clipped * clipped
            step = moment / (jnp.sqrt(square) + ADAM_EPS) + DECAY_RATE * masters[index][at]
            clip_o[index][at] = clipped
            moment_o[index][at] = moment
            square_o[index][at] = square
            step_o[index][at] = step
            amount = amount + total(step * step)
        update_sq.append(amount * single[index])
    tile = tile_of(update_sq)
    for peer in range(tiles_o.shape[0]):
        tiles_o[peer] = tile


def update_kernel(tiles, summed, *refs):
    masters, steps, outs = refs[:7], refs[7:14], refs[14:]
    updated_o, copy_o, (norms_o, clip_o) = outs[:7], outs[7:14], outs[14:]
    lane = lax.broadcasted_iota(jnp.int32, (1, 128), 1)
    squared = summed[...]
    clip = jnp.sqrt(total(jnp.where(lane < 7, squared, 0.0)))
    weight_norm = jnp.sqrt(jnp.concatenate([squared[:, 64:], squared[:, :64]], axis=1))
    update_norm = jnp.sqrt(jnp.sum(tiles[...], axis=0))
    ratio = weight_norm / (update_norm + TRUST_EPS)
    norms_o[0:1, :] = weight_norm[:, :7]
    norms_o[1:2, :] = update_norm[:, :7]
    clip_o[...] = clip
    for index in range(7):
        rate = LEARN_RATE * total(jnp.where(lane == index, ratio, 0.0))
        for piece in range(3 if index == 0 else 1):
            at = piece if index == 0 else Ellipsis
            updated = masters[index][at] - rate * steps[index][at]
            updated_o[index][at] = updated
            copy_o[index][at] = updated.astype(BF16)


def shape(dims, dtype=F32):
    return jax.ShapeDtypeStruct(tuple(dims), dtype)


def whole(kernel, outs, scalars, operands, **kw):
    return pl.pallas_call(
        kernel,
        out_shape=outs,
        in_specs=[pl.BlockSpec(memory_space=pltpu.SMEM)] * len(scalars)
        + [pl.BlockSpec(memory_space=pltpu.VMEM)] * len(operands),
        out_specs=[pl.BlockSpec(memory_space=pltpu.VMEM)] * len(outs),
        compiler_params=params(),
        **kw,
    )(*scalars, *operands)


def per_device(
    tokens,
    counts,
    visible,
    dest_device,
    dest_slot,
    cotangent,
    *state,
):
    masters = [state[3 * index] for index in range(7)]
    moments = [state[3 * index + 1] for index in range(7)]
    squares = [state[3 * index + 2] for index in range(7)]

    def flat_state(arrays):
        a, b, c, d, e, f, g = arrays
        return [a.transpose(1, 0, 2), b.T, c, d.T, e, f, g[:, 0, :]]

    def natural(arrays):
        a, b, c, d, e, f, g = arrays
        return [a.transpose(1, 0, 2), b.T, c, d.T, e, f, g[:, None, :]]

    masters, moments, squares = flat_state(masters), flat_state(moments), flat_state(squares)

    peers, cores = lax.axis_size("dp"), lax.axis_size("mp")
    me, core = lax.axis_index("dp"), lax.axis_index("mp")
    core_s = core.astype(jnp.int32).reshape(1)
    once_s = 1 - core_s
    model = tokens.shape[1]
    nviews, per_view = visible.shape
    episodes = counts.shape[0]
    views_each = nviews // episodes
    span = views_each * per_view
    size = -(-span // ROUND) * ROUND
    here = episodes // cores
    rows = here * size
    cells, dec = cotangent.shape[1:]
    part = masters[1].shape[1]
    hidden = masters[2].shape[1]
    shard_rows = masters[2].shape[0]
    room = (nviews + peers - 1) // peers
    npos = peers * room
    fast = peers == FAST_PEERS

    low = [m.astype(BF16) for m in masters]
    chunk_a = jnp.concatenate([low[0][0], low[0][1], low[0][2], low[1]], axis=1)
    chunk_b = low[2]
    chunk_c = jnp.concatenate([low[3], low[4]], axis=1)

    same = dest_device[:, None] == dest_device[None, :]
    earlier = jnp.arange(nviews)[None, :] < jnp.arange(nviews)[:, None]
    rank = jnp.sum((same & earlier).astype(jnp.int32), axis=1)
    where_view = (dest_device * room + rank).astype(jnp.int32)
    layout = jnp.arange(npos, dtype=jnp.int32)[:, None] == where_view[None, :]
    live_view = (
        jnp.arange(nviews, dtype=jnp.int32) % views_each < jnp.repeat(counts, views_each)
    ).astype(jnp.int32)
    details = jnp.concatenate(
        [jnp.ones((nviews, 1), jnp.int32), dest_slot[:, None], live_view[:, None], visible], axis=1
    )
    fields = details.shape[1]
    sent = jnp.dot(layout.astype(BF16), details.astype(BF16), preferred_element_type=F32)
    sent = sent.astype(BF16).reshape(peers, room * fields)
    small = jnp.concatenate([low[5].reshape(-1), low[6].reshape(-1)])
    message = jnp.concatenate(
        [sent, jnp.broadcast_to(small[None], (peers, small.shape[0]))], axis=1
    )
    message = jnp.broadcast_to(message[:, None], (peers, cores, message.shape[1]))
    if fast:
        gather = Gather((chunk_a, chunk_b, chunk_c), peers)
        z_one = gather.step_z((message,))
    message = lax.all_to_all(
        message.reshape(peers * cores, -1), AXES, split_axis=0, concat_axis=0, tiled=True
    ).reshape(peers, cores, -1)
    if fast:
        message = after(message, *z_one)
    got = message[:, 0, : room * fields].reshape(npos, fields).astype(jnp.int32)
    nln = 4 * shard_rows
    ln_full = (
        message[:, 0, room * fields : room * fields + nln]
        .reshape(peers, 4, shard_rows)
        .transpose(1, 0, 2)
        .reshape(4, model)
        .astype(F32)
    )
    norms = jnp.concatenate([ln_full, jnp.zeros((4, model), F32)], axis=0)
    dec_full = (
        message[:, :, room * fields + nln :]
        .reshape(peers, cores, 2, dec // peers)
        .transpose(2, 1, 0, 3)
        .reshape(2, cores, dec)
        .astype(F32)
    )
    mask_token = lax.dynamic_index_in_dim(dec_full[1], core, 0, keepdims=True)
    held_slot = got[:, 1]
    filled = (held_slot[None, :] == jnp.arange(nviews, dtype=jnp.int32)[:, None]) & (
        got[:, 0][None, :] > 0
    )
    where_slot = jnp.sum(
        jnp.where(filled, jnp.arange(npos, dtype=jnp.int32)[None, :], 0), axis=1
    ).astype(jnp.int32)
    owned = jnp.dot(
        filled.astype(BF16), got.astype(BF16), preferred_element_type=F32
    ).astype(jnp.int32)
    live_slot, owned_spots = owned[:, 2], owned[:, 3:]
    each = 8
    groups = nviews // each
    marks = jnp.where(
        live_slot[:, None] > 0,
        owned_spots * each + (jnp.arange(nviews, dtype=jnp.int32) % each)[:, None],
        -1,
    )
    tall = -(-per_view // 8) * 8
    stride_take, stride_put = tall, -(-per_view // 64) * 64
    take_marks = jnp.pad(marks, ((0, 0), (0, stride_take - per_view)), constant_values=-1)
    take_marks = take_marks.reshape(nviews * stride_take, 1)
    put_marks = jnp.pad(marks, ((0, 0), (0, stride_put - per_view)), constant_values=-1)
    put_marks = put_marks.reshape(groups, 1, each * stride_put)
    live_row = jnp.broadcast_to(
        live_slot.astype(F32).reshape(groups, 1, each), (groups, cells, each)
    ).reshape(groups, 1, cells * each)

    take_call = pl.pallas_call(
        lambda *refs: take_cells(*refs, per_view=per_view, stride=stride_take),
        out_shape=[shape((npos, tall, dec), BF16), shape((8, dec))],
        grid_spec=pltpu.PrefetchScalarGridSpec(
            num_scalar_prefetch=1,
            grid=(groups,),
            in_specs=[
                pl.BlockSpec((each * stride_take, 1), lambda i, _: (i, 0)),
                pl.BlockSpec((1, 1, cells * each), lambda i, _: (i, 0, 0)),
                pl.BlockSpec((cells, each, dec), lambda i, _: (0, i, 0)),
            ],
            out_specs=[
                pl.BlockSpec((npos, tall, dec), lambda i, _: (0, 0, 0)),
                pl.BlockSpec((8, dec), lambda i, _: (0, 0)),
            ],
        ),
        compiler_params=params(),
        cost_estimate=cost(2 * nviews * stride_take * cells * each * dec, cotangent.size * 2),
        name="take_cells",
    )

    positions = lax.dynamic_slice_in_dim(
        grid_positions(math.isqrt(cells), dec * cores), core * dec, dec, 1
    )
    own = lax.dynamic_slice_in_dim(
        after(tokens, *z_one) if fast else tokens, core * (here * span), here * span, 0
    ).reshape(here, span, model)
    own = jnp.pad(own, ((0, 0), (0, size - span), (0, 0))).reshape(rows, model)
    begun = gather.step_near((take_marks, live_row, own)) if fast else []
    hold = after if fast else (lambda array, *others: array)
    leaves = jax.tree.leaves
    returned, dec_sums = take_call(
        where_slot, hold(take_marks, *begun), live_row, cotangent.transpose(1, 0, 2)
    )
    if fast:
        later = (positions, mask_token, put_marks, dec_full, norms)
        parts_a = gather.step_far((returned,) + later)
        positions, mask_token, put_marks, dec_full, norms = hold_all(later, parts_a[:1])
    else:
        parts_a = gather_plain(chunk_a)
    nparts = len(parts_a)
    table = gather_table(me, core)
    nsem = PIECE * nparts if fast else 1

    smem = pl.BlockSpec(memory_space=pltpu.SMEM)
    fixed = lambda dims: pl.BlockSpec(dims, lambda i: (0,) * len(dims))
    chunk_cols = [chunk_a.shape[1], chunk_b.shape[1], chunk_c.shape[1]]
    weight_bytes = [2 * 2 * model * cols for cols in chunk_cols]
    calls = 2 if here % 2 == 0 else 1
    each_call = here // calls

    def attn_forward_call(call, own, earlier):
        begin = call * each_call
        ep = lambda cols: pl.BlockSpec((size, cols), lambda i: (i + begin, 0))
        return pl.pallas_call(
            lambda *refs: attn_forward(
                *refs, nparts=nparts, per_view=per_view, part=part, begin=begin, here=here
            ),
            grid=(each_call,),
            out_shape=[
                shape((rows, model), BF16),
                shape((rows, 6 * part), BF16),
                shape((rows, 2 * part), BF16),
                shape((rows, model)),
                shape((rows, model), BF16),
                shape((rows, 2 * HEADDIM), BF16),
            ],
            in_specs=[smem, smem, smem, ep(model), fixed((8, model))]
            + [any_spec()] * (nparts + len(earlier)),
            out_specs=[ep(model), ep(6 * part), ep(2 * part), ep(model), ep(model), ep(2 * HEADDIM)],
            scratch_shapes=[
                pltpu.VMEM((2, model, chunk_cols[0]), BF16),
                pltpu.SemaphoreType.DMA((nsem,)),
            ],
            input_output_aliases={5 + nparts + index: index for index in range(len(earlier))},
            compiler_params=params(),
            cost_estimate=cost(
                6 * rows * model * 8 * part // calls, weight_bytes[0] + rows * model * 16 // calls
            ),
            name="attn_forward",
        )(core_s, counts, table, own, norms, *parts_a, *earlier)

    attn = []
    for call in range(calls):
        gates = gather.later() if fast and call > 0 else []
        attn = attn_forward_call(call, after(own, *gates) if gates else own, attn)
        if call == 0 and fast:
            returned = after(returned, attn[0])
            gather.second(attn[0])
    if fast:
        parts_b, parts_c = gather.finish(attn[0])
    else:
        parts_b, parts_c = gather_plain(chunk_b), gather_plain(chunk_c)
    came_mine = lax.all_to_all(returned, "dp", split_axis=0, concat_axis=0, tiled=True)
    came_theirs = swap(came_mine, peers, 0, 1)
    first, packed, attended, middle, second, lse = attn

    group = 2
    chunk = group * size
    steps = here // group
    gviews = group * views_each
    blk = lambda cols: pl.BlockSpec((chunk, cols), lambda i: (i, 0))
    wide = hidden
    mlp_scratch = [
        pltpu.VMEM((2, model, chunk_cols[1]), BF16),
        pltpu.VMEM((2, model, chunk_cols[2]), BF16),
    ]
    act, slope, final, emb_keep, emb_send = pl.pallas_call(
        lambda *refs: mlp_forward(
            *refs, nparts=nparts, per_view=per_view, part=hidden, wide=wide, rows_each=size
        ),
        grid=(steps,),
        out_shape=[
            shape((rows, 2 * hidden), BF16),
            shape((rows, 2 * hidden), BF16),
            shape((rows, model), BF16),
            shape((steps * gviews, tall, dec), BF16),
            shape((steps * gviews, tall, dec), BF16),
        ],
        in_specs=[smem, smem, blk(model), blk(model), fixed((2, dec))] + [any_spec()] * (2 * nparts),
        out_specs=[
            blk(2 * hidden),
            blk(2 * hidden),
            blk(model),
            pl.BlockSpec((gviews, tall, dec), lambda i: (i, 0, 0)),
            pl.BlockSpec((gviews, tall, dec), lambda i: (i, 0, 0)),
        ],
        scratch_shapes=mlp_scratch + [pltpu.SemaphoreType.DMA((nsem,))] * 2,
        compiler_params=params(),
        cost_estimate=cost(
            4 * rows * model * 2 * hidden, weight_bytes[1] + weight_bytes[2] + rows * hidden * 8
        ),
        name="mlp_forward",
    )(core_s, table, second, middle, dec_full[0], *parts_b, *parts_c)

    where_mine = lax.dynamic_slice_in_dim(where_view, core * (nviews // cores), nviews // cores)
    emb_rows, glow, gpre, gmid, gmid_low, ln_two = pl.pallas_call(
        lambda *refs: mlp_backward(
            *refs, nparts=nparts, per_view=per_view, part=hidden, wide=wide, rows_each=size
        ),
        grid=(steps,),
        out_shape=[
            shape((rows, 2 * dec), BF16),
            shape((rows, model), BF16),
            shape((rows, 2 * hidden), BF16),
            shape((rows, model)),
            shape((rows, model), BF16),
            shape((8, model)),
        ],
        in_specs=[smem, smem, smem, any_spec(), any_spec(), blk(2 * hidden), blk(model), fixed((8, model))]
        + [any_spec()] * (2 * nparts),
        out_specs=[blk(2 * dec), blk(model), blk(2 * hidden), blk(model), blk(model), fixed((8, model))],
        scratch_shapes=mlp_scratch
        + [
            pltpu.VMEM((2, gviews, tall, dec), BF16),
            pltpu.VMEM((chunk, 2 * dec), F32),
            pltpu.SemaphoreType.DMA((nsem,)),
            pltpu.SemaphoreType.DMA((nsem,)),
            pltpu.SemaphoreType.DMA((2, gviews)),
        ],
        compiler_params=params(),
        cost_estimate=cost(
            4 * rows * model * 2 * hidden, weight_bytes[1] + weight_bytes[2] + rows * hidden * 8
        ),
        name="mlp_backward",
    )(core_s, where_mine, table, came_mine, came_theirs, slope, middle, norms, *parts_b, *parts_c)

    emb_other = swap(emb_send, peers, 0, 1)
    if fast:
        emb_other = after(emb_other, glow)
    outgoing = pl.pallas_call(
        order_views,
        out_shape=shape((npos, tall, dec), BF16),
        in_specs=[smem, smem, any_spec(), any_spec()],
        out_specs=any_spec(),
        scratch_shapes=[pltpu.SemaphoreType.DMA((nviews,))],
        compiler_params=params(8 << 20),
        cost_estimate=cost(0, 4 * nviews * per_view * dec),
        name="order_views",
    )(where_view, core_s, emb_keep, emb_other)
    arrived = lax.all_to_all(outgoing, "dp", split_axis=0, concat_axis=0, tiled=True)

    blocks = FAST_PEERS
    if fast:
        places = [place_table(me, core), place_table(me, 1 - core)]
    else:
        places = [jnp.arange(blocks, dtype=jnp.int32)] * 2

    deep = -(-rows // 256) * 256

    deep = -(-rows // 256) * 256

    def side_grads(pairs, block, name, other=None):
        lengths = [right.shape[1] // 2 // block for _, right in pairs]
        many = sum(lengths)
        begins = [sum(lengths[:index]) for index in range(len(lengths))]

        def column(begin, length):
            return lambda j, side, _: (0, side[0] * length + jnp.clip(j - begin, 0, length - 1))

        in_specs, operands = [], []
        for index, (left, right) in enumerate(pairs):
            in_specs += [
                pl.BlockSpec((rows, model), lambda j, *_: (0, 0)),
                pl.BlockSpec((rows, block), column(begins[index], lengths[index])),
            ]
            operands += [left, right]
        each_row = model // blocks
        spec = lambda count: pl.BlockSpec((count, each_row, block), lambda j, *_: (0, 0, j))
        dims = lambda count: shape((count, each_row, many * block), BF16)
        adding = other is not None
        return pl.pallas_call(
            lambda *refs: weight_grad(*refs, steps=lengths, rows_each=each_row, add_other=adding),
            out_shape=[dims(blocks // 2)] * 2 if adding else dims(blocks),
            grid_spec=pltpu.PrefetchScalarGridSpec(
                num_scalar_prefetch=2,
                grid=(many,),
                in_specs=in_specs + [spec(blocks)] * adding,
                out_specs=[spec(blocks // 2)] * 2 if adding else spec(blocks),
                scratch_shapes=[pltpu.VMEM((blocks, each_row, block), F32)] * adding
                + [pltpu.VMEM((deep, model), BF16), pltpu.VMEM((deep, block), BF16)],
            ),
            compiler_params=params(),
            cost_estimate=cost(2 * rows * model * many * block, 2 * rows * (many * block + model)),
            name=name,
        )(
            core_s if adding else 1 - core_s,
            places[0 if adding else 1],
            *operands,
            *([other] if adding else []),
        )

    def whole_grads(pairs, block, name):
        lengths = [right.shape[1] // 2 // block for _, right in pairs]
        many = sum(lengths)
        begins = [sum(lengths[:index]) for index in range(len(lengths))]

        def column(begin, length):
            return lambda h, j: (0, h * length + jnp.clip(j - begin, 0, length - 1))

        in_specs, operands = [], []
        for index, (left, right) in enumerate(pairs):
            in_specs += [
                pl.BlockSpec((rows, model), lambda h, j: (0, 0)),
                pl.BlockSpec((rows, block), column(begins[index], lengths[index])),
            ]
            operands += [left, right]
        return pl.pallas_call(
            lambda *refs: weight_grad(
                None, None, *refs, steps=lengths, rows_each=shard_rows, add_other=False
            ),
            out_shape=shape((peers, 2, shard_rows, many * block), BF16),
            grid=(2, many),
            in_specs=in_specs,
            out_specs=pl.BlockSpec((peers, 1, shard_rows, block), lambda h, j: (0, h, 0, j)),
            scratch_shapes=[pltpu.VMEM((deep, model), BF16), pltpu.VMEM((deep, block), BF16)],
            compiler_params=params(),
            cost_estimate=cost(4 * rows * model * many * block, 4 * rows * (many * block + model)),
            name=name,
        )(*operands)

    def attn_backward_call(call, mid, earlier):
        begin = call * each_call
        last = call == calls - 1
        ep = lambda cols: pl.BlockSpec((size, cols), lambda i: (i + begin, 0))
        if last:
            own_shape, own_spec = shape((here * span, model), BF16), fixed((here * span, model))
        else:
            own_shape = shape((each_call, span, model), BF16)
            own_spec = pl.BlockSpec((1, span, model), lambda i: (i, 0, 0))
        return pl.pallas_call(
            lambda *refs: attn_backward(
                *refs,
                nparts=nparts,
                per_view=per_view,
                part=part,
                begin=begin,
                here=here,
                rows_out=span,
            ),
            grid=(each_call,),
            out_shape=[shape((rows, 6 * part), BF16), own_shape, shape((8, model))],
            in_specs=[smem, smem, smem, ep(model), ep(6 * part), ep(2 * part), ep(2 * HEADDIM), ep(model), fixed((8, model))]
            + [any_spec()] * nparts
            + ([any_spec(), fixed((each_call, span, model))] if earlier else []),
            out_specs=[ep(6 * part), own_spec, fixed((8, model))],
            scratch_shapes=[
                pltpu.VMEM((2, model, chunk_cols[0]), BF16),
                pltpu.SemaphoreType.DMA((nsem,)),
            ],
            input_output_aliases={9 + nparts: 0} if earlier else {},
            compiler_params=params(),
            cost_estimate=cost(
                8 * rows * model * 8 * part // calls, weight_bytes[0] + rows * model * 16 // calls
            ),
            name="attn_backward",
        )(core_s, counts, table, own, packed, attended, lse, mid, norms, *parts_a, *earlier)

    def behind(pairs, *gate):
        left, right = pairs[0]
        return [(left, hold(right, *gate))] + pairs[1:]

    pairs_b = [(second, gpre), (gmid_low, attended)]
    other_b = side_grads(behind(pairs_b, outgoing), part, "grad_up_out_send")
    whole_c = whole_grads(behind([(glow, act), (final, emb_rows)], other_b), 256, "grad_down_emb")
    sum_c = lax.psum_scatter(
        whole_c.reshape(peers * cores * shard_rows, -1), AXES, scatter_dimension=0, tiled=True
    )
    got_b = hold(swap(other_b, peers, 0, 1), whole_c)
    keep, send = side_grads(behind(pairs_b, whole_c), part, "grad_up_out_keep", got_b)
    sum_b = [(keep,), send]
    ln_one = jnp.zeros((8, model), F32)
    back = []
    for call in range(calls):
        gates = (keep, arrived) if call == 0 else leaves(sum_b[1])
        *back, sums = attn_backward_call(call, hold(gmid, *gates), back)
        ln_one = ln_one + sums
        if call == 0:
            sum_b = scatter_near(sum_b, peers, back[0])
    grad_packed, grad_own = back
    sum_b = scatter_far(sum_b, peers, grad_own)
    pairs_a = [(first, grad_packed)]
    other_a = side_grads(behind(pairs_a, *leaves(sum_b[1])), part, "grad_in_send")

    grad_other = swap(grad_own, peers, 0, 1)
    grad_tokens = jnp.where(
        core == 0,
        jnp.concatenate([grad_own, grad_other]),
        jnp.concatenate([grad_other, grad_own]),
    )

    decoded = pl.pallas_call(
        lambda *refs: put_cells(*refs, per_view=per_view),
        out_shape=shape((cells, nviews, dec), BF16),
        grid_spec=pltpu.PrefetchScalarGridSpec(
            num_scalar_prefetch=2,
            grid=(groups,),
            in_specs=[
                pl.BlockSpec((1, 1, each * stride_put), lambda i, *_: (i, 0, 0)),
                pl.BlockSpec((1, dec), lambda i, *_: (0, 0)),
                pl.BlockSpec((cells, dec), lambda i, *_: (0, 0)),
                pl.BlockSpec((npos, tall, dec), lambda i, *_: (0, 0, 0)),
            ],
            out_specs=pl.BlockSpec((cells, each, dec), lambda i, *_: (0, i, 0)),
            scratch_shapes=[pltpu.VMEM((each * stride_put, dec), BF16)],
        ),
        compiler_params=params(),
        cost_estimate=cost(2 * nviews * stride_put * cells * each * dec, cotangent.size * 2),
        name="put_cells",
    )(where_slot, live_slot, hold(put_marks, other_a), mask_token, positions, arrived)
    got_a = hold(swap(other_a, peers, 0, 1), decoded)
    ln_sums = jnp.concatenate([hold(ln_one[:2], other_a), ln_two[:2]])
    ln_send = ln_sums.reshape(4, peers, shard_rows).transpose(1, 0, 2).reshape(peers, nln)
    dec_send = dec_sums[:2].reshape(2, peers, dec // peers).transpose(1, 0, 2).reshape(peers, -1)
    small_send = jnp.concatenate([ln_send, dec_send], axis=1)
    small_send = jnp.broadcast_to(small_send[:, None], (peers, cores, small_send.shape[1]))
    small_got = lax.all_to_all(
        small_send.reshape(peers * cores, -1), AXES, split_axis=0, concat_axis=0, tiled=True
    ).reshape(peers, cores, -1)
    grad_ln = jnp.sum(small_got[:, :, :nln], axis=(0, 1)).reshape(4, shard_rows)
    grad_dec = jnp.sum(
        lax.dynamic_index_in_dim(small_got[:, :, nln:], core, 1, keepdims=False), axis=0
    ).reshape(2, dec // peers)

    keep, send = side_grads(behind(pairs_a, decoded), part, "grad_in_keep", got_a)
    sum_a = [(keep,), hold(send, grad_ln)]
    sum_a = scatter_near(sum_a, peers, grad_tokens)
    sum_b = scatter_end(sum_b, peers, *leaves(sum_a[1])) if fast else scatter_end(sum_b, peers)
    sum_a = scatter_far(sum_a, peers, sum_b)
    sum_a = scatter_end(sum_a, peers)
    decoded = decoded.transpose(1, 0, 2)

    grads = [sum_a, sum_b, sum_c, grad_ln, grad_dec]
    world = peers * cores
    (tiles,) = whole(squares_kernel, [shape((world, 1, 128))], [once_s], grads + masters, name="squares")
    tiles = lax.all_to_all(tiles, AXES, split_axis=0, concat_axis=0, tiled=True)
    same_shapes = [shape(m.shape) for m in masters]
    lamb = whole(
        lamb_kernel,
        same_shapes * 4 + [shape((1, 128)), shape((world, 1, 128))],
        [once_s],
        [tiles] + grads + masters + moments + squares,
        name="lamb",
    )
    summed = lamb[28]
    steps_tiles = lax.all_to_all(lamb[29], AXES, split_axis=0, concat_axis=0, tiled=True)
    update = whole(
        update_kernel,
        same_shapes + [shape(m.shape, BF16) for m in masters] + [shape((2, 7)), shape((1, 1))],
        [],
        [steps_tiles, summed] + masters + list(lamb[21:28]),
        name="update",
    )
    results = [
        natural(group)
        for group in (lamb[:7], lamb[7:14], lamb[14:21], update[:7], update[7:14])
    ]
    outs = [decoded, grad_tokens, update[15].reshape(1), update[14]]
    for index in range(7):
        outs += [group[index] for group in results]
    return tuple(outs)


def solution(mesh):
    tensor_specs = [
        P("dp", None, "mp"),
        P("mp", "dp"),
        P("dp", "mp"),
        P("mp", "dp"),
        P("dp", "mp"),
        P(None, "dp"),
        P(None, "mp", "dp"),
    ]
    in_specs = (
        P("dp", None),
        P("dp"),
        P("dp", None),
        P("dp"),
        P("dp"),
        P("dp", None, "mp"),
    ) + tuple(spec for spec in tensor_specs for _ in range(3))
    out_specs = (P("dp", None, "mp"), P("dp", None), P(), P()) + tuple(
        spec for spec in tensor_specs for _ in range(5)
    )
    return jax.shard_map(
        per_device, mesh=mesh, in_specs=in_specs, out_specs=out_specs, check_vma=False
    )
```

```python
import math

import jax
import jax.numpy as jnp
from jax import lax
from jax.experimental import pallas as pl
from jax.experimental.pallas import tpu as pltpu
from jax.sharding import PartitionSpec as P

HEADDIM = 64
PARAMS = 7475200
NORM_EPS = 1e-06
MASK_FILL = -1e30
BETA_ONE = 0.5
BETA_TWO = 0.5
ADAM_EPS = 1e-06
DECAY_RATE = 0.01
LEARN_RATE = 0.5
TRUST_EPS = 1e-06

F32 = jnp.float32
BF16 = jnp.bfloat16
AXES = ("dp", "mp")
NT = (((1,), (1,)), ((), ()))
TN = (((0,), (0,)), ((), ()))
ROUND = 16
VMEM_BYTES = 58 << 20
COST = 3.0


def mm(a, b, dims=(((1,), (0,)), ((), ()))):
    return lax.dot_general(a, b, dims, preferred_element_type=F32)


def norm_rows(values):
    centre = values - jnp.mean(values, axis=-1, keepdims=True)
    spread = jnp.mean(centre * centre, axis=-1, keepdims=True)
    inverse = lax.rsqrt(spread + NORM_EPS)
    return centre * inverse, inverse


def norm_back(scaled, normed, inverse):
    return inverse * (
        scaled
        - jnp.mean(scaled, axis=-1, keepdims=True)
        - normed * jnp.mean(scaled * normed, axis=-1, keepdims=True)
    )


def grid_positions(side, width):
    quarter = width // 4
    rate = 1.0 / 10000.0 ** (jnp.arange(quarter, dtype=F32) / quarter)
    place = jnp.arange(side * side, dtype=jnp.int32)
    row_pos = (place // side).astype(F32)
    col_pos = (place % side).astype(F32)
    row_angle = row_pos[:, None] * rate[None, :]
    col_angle = col_pos[:, None] * rate[None, :]
    return jnp.concatenate(
        [jnp.sin(row_angle), jnp.cos(row_angle), jnp.sin(col_angle), jnp.cos(col_angle)], axis=1
    )


def any_spec():
    return pl.BlockSpec(memory_space=pl.ANY)


def params(limit=VMEM_BYTES):
    return pltpu.CompilerParams(vmem_limit_bytes=limit)


def cost(flops, nbytes):
    return pl.CostEstimate(flops=int(COST * flops), bytes_accessed=int(nbytes), transcendentals=0)


def swap(array, peers, bits, core=0):
    bits = bits if isinstance(bits, tuple) else (bits, bits)
    pairs = [
        (d * 2 + m, (d ^ bits[m]) * 2 + (m ^ core)) for d in range(peers) for m in range(2)
    ]
    return lax.ppermute(array, AXES, pairs)


FAST_PEERS = 16
Z_STEPS = (4, 8, 12)


def after(array, *others):
    return lax.optimization_barrier((array,) + others)[0]


def reach_z(shard, peers):
    return [swap(shard, peers, bits) for bits in Z_STEPS]


def hold_all(arrays, others):
    return list(lax.optimization_barrier((tuple(arrays), tuple(others)))[0])


def gather_plain(shard):
    return [lax.all_gather(lax.all_gather(shard, "dp", axis=0, tiled=True), "mp", axis=0)]


class Gather:
    def __init__(self, shards, peers):
        self.peers = peers
        self.one, self.two, self.three = shards

    def near(self, array):
        return swap(array, self.peers, (1, 2))

    def far(self, array):
        return swap(array, self.peers, (2, 1))

    def across(self, array):
        return swap(array, self.peers, 0, 1)

    def step_z(self, beside):
        z_one = reach_z(self.one, self.peers)
        (self.along_one,) = hold_all([jnp.stack([self.one] + z_one)], beside)
        (self.two,) = hold_all([self.two], z_one)
        return z_one

    def step_near(self, beside):
        near_one, z_two = self.near(self.along_one), reach_z(self.two, self.peers)
        (self.half_one,) = hold_all([jnp.concatenate([self.along_one, near_one])], beside)
        self.along_two, self.three = hold_all(
            [jnp.stack([self.two] + z_two), self.three], [near_one] + z_two
        )
        return [near_one]

    def step_far(self, beside):
        far_one, side_one = self.far(self.half_one), self.across(self.half_one)
        near_two, z_three = self.near(self.along_two), reach_z(self.three, self.peers)
        far_one, half_two, along_three = hold_all(
            [far_one, jnp.concatenate([self.along_two, near_two]), jnp.stack([self.three] + z_three)],
            [far_one, near_two] + z_three + list(beside),
        )
        self.half_two, self.along_three = half_two, along_three
        self.far_two, self.side_two = self.far(half_two), self.across(half_two)
        self.near_three = self.near(along_three)
        return [self.half_one, far_one, side_one, self.across(far_one)]

    def later(self):
        return [self.far_two, self.near_three, self.side_two]

    def second(self, beside):
        far_two, along_three, near_three = hold_all(
            [self.far_two, self.along_three, self.near_three], [beside]
        )
        self.half_three = jnp.concatenate([along_three, near_three])
        self.far_three, self.side_three = self.far(self.half_three), self.across(self.half_three)
        self.parts_two = [self.half_two, far_two, self.side_two, self.across(far_two)]

    def finish(self, beside):
        (far_three,) = hold_all([self.far_three], [beside] + self.parts_two[2:])
        parts_three = [self.half_three, far_three, self.side_three, self.across(far_three)]
        return self.parts_two, parts_three


PIECE = 8


def gather_table(me, core):
    one = jnp.where(core == 0, 1, 2)
    two = 3 - one
    along = jnp.array((0,) + Z_STEPS, jnp.int32)
    mine = jnp.concatenate([along, along ^ one])
    theirs = jnp.concatenate([along, along ^ two])
    apart = jnp.concatenate([mine, mine ^ two, theirs, theirs ^ one])
    cores = jnp.stack([core, core, 1 - core, 1 - core])
    return jnp.concatenate([me ^ apart, cores]).astype(jnp.int32)


def weight_copies(parts, table, target, sems):
    if len(parts) == 1:
        return [pltpu.make_async_copy(parts[0], target, sems.at[0])]
    copies = []
    for index, part in enumerate(parts):
        half = table[len(parts) * PIECE + index]
        for inner in range(PIECE):
            at = index * PIECE + inner
            rows = part.shape[1]
            start = pl.multiple_of(table[at] * rows, ROUND)
            copies.append(
                pltpu.make_async_copy(
                    part.at[inner], target.at[half, pl.ds(start, rows), :], sems.at[at]
                )
            )
    return copies


def place_table(me, core):
    near = jnp.where(core == 0, 2, 1)
    far = 3 - near
    apart = jnp.arange(FAST_PEERS, dtype=jnp.int32) ^ me
    return (
        jnp.where((apart & near) != 0, 8, 0) + jnp.where((apart & far) != 0, 4, 0) + (apart >> 2)
    ).astype(jnp.int32)


def add(*terms):
    return sum(term.astype(F32) for term in terms)


def scatter_near(state, peers, *held):
    if peers != FAST_PEERS:
        return state
    terms, send = state
    got = swap(send, peers, (2, 1))
    terms = terms + (after(got, *held) if held else got,)
    return [terms, add(*(term[4:8] for term in terms)).astype(BF16)]


def scatter_far(state, peers, *held):
    if peers != FAST_PEERS:
        return state
    terms, send = state
    got = swap(send, peers, (1, 2))
    terms = terms + (after(got, *held) if held else got,)
    return [terms, tuple(add(*(term[i] for term in terms)).astype(BF16) for i in (1, 2, 3))]


def scatter_end(state, peers, *held):
    if peers != FAST_PEERS:
        (keep,), send = state
        whole = jnp.concatenate([keep, send]).astype(F32)
        return lax.psum_scatter(
            whole.reshape(-1, whole.shape[-1]), "dp", scatter_dimension=0, tiled=True
        )
    terms, sends = state
    last = [swap(send, peers, bits) for send, bits in zip(sends, Z_STEPS)]
    last = hold_all(last, held) if held else last
    return add(*(term[0] for term in terms), *last)


def view_of(rows, per_view):
    view = jnp.zeros_like(rows)
    for edge in range(1, 5):
        view = view + (rows >= edge * per_view).astype(jnp.int32)
    return view


def allowed_bias(size, count, per_view):
    query = view_of(lax.broadcasted_iota(jnp.int32, (size, size), 0), per_view)
    key = view_of(lax.broadcasted_iota(jnp.int32, (size, size), 1), per_view)
    return jnp.where((key < count) | (key == query), 0.0, MASK_FILL)


def pair_masks(scale):
    lane = lax.broadcasted_iota(jnp.int32, (1, 2 * HEADDIM), 1)
    low = (lane < HEADDIM).astype(F32)
    return (low * scale).astype(BF16), ((1.0 - low) * scale).astype(BF16)


PARTS = 16


def head_lanes(head):
    lane = lax.broadcasted_iota(jnp.int32, (1, 2 * HEADDIM), 1)
    return ((lane & (PARTS - 1)) == head) & (lane < 3 * PARTS)


def in_parts(values):
    lane = lax.broadcasted_iota(jnp.int32, values.shape, 1)
    high = values.astype(BF16).astype(F32)
    rest = values - high
    middle = rest.astype(BF16).astype(F32)
    return jnp.where(lane < PARTS, high, jnp.where(lane < 2 * PARTS, middle, rest - middle)).astype(BF16)


def attn_forward(mp_s, counts_s, table, tokens, norms, *rest, nparts, per_view, part, begin, here):
    parts = rest[:nparts]
    first_o, packed_o, attended_o, middle_o, second_o, lse_o, weights, sems = rest[-8:]
    step = pl.program_id(0)
    copies = weight_copies(parts, table, weights, sems)

    @pl.when(step == 0)
    def _():
        for copy in copies:
            copy.start()
        for copy in copies:
            copy.wait()

    size = tokens.shape[0]
    scale = 1.0 / math.sqrt(HEADDIM)
    values = tokens[...].astype(F32)
    normed, _ = norm_rows(values)
    first = (normed * norms[0:1, :] + norms[1:2, :]).astype(BF16)
    first_o[...] = first
    bias = allowed_bias(size, counts_s[mp_s[0] * here + begin + step], per_view)
    bias = jnp.concatenate([bias, bias], axis=0)
    masks = pair_masks(scale)
    lane = lax.broadcasted_iota(jnp.int32, (size, 2 * HEADDIM), 1)
    wide = 2 * HEADDIM
    lse = jnp.zeros((size, wide), F32)
    ones = jnp.ones((size, wide), BF16)
    attn = jnp.zeros(values.shape, F32)
    for half in range(2):
        packed = mm(first, weights[half, :, : 3 * part]).astype(BF16)
        packed_o[:, half * 3 * part : (half + 1) * 3 * part] = packed
        pairs = range(part // wide)
        logits, probs = [], []
        for pair in pairs:
            at = pair * wide
            query = packed[:, at : at + wide]
            key = packed[:, part + at : part + at + wide]
            both = jnp.concatenate([query * masks[0], query * masks[1]], axis=0)
            logits.append(mm(both, key, NT) + bias)
        tops = []
        for pair in pairs:
            top = jnp.max(logits[pair], axis=-1, keepdims=True)
            probs.append(jnp.exp(logits[pair] - top).astype(BF16))
            tops.append(top)
        for pair in pairs:
            at = pair * wide
            value = packed[:, 2 * part + at : 2 * part + at + wide]
            outs = mm(probs[pair], jnp.concatenate([value, ones], axis=1))
            totals = outs[:, wide:]
            outs = outs[:, :wide] / totals
            low_lse = -(tops[pair] + jnp.log(totals))
            index = half * (part // HEADDIM) + pair * 2
            lse = jnp.where(head_lanes(index), low_lse[:size], lse)
            lse = jnp.where(head_lanes(index + 1), low_lse[size:], lse)
            both = jnp.where(lane < HEADDIM, outs[:size], outs[size:]).astype(BF16)
            attended_o[:, half * part + at : half * part + at + wide] = both
        attn = attn + mm(
            attended_o[:, half * part : (half + 1) * part], weights[half, :, 3 * part :], NT
        )
    lse_o[...] = in_parts(lse)
    middle = values + attn
    middle_o[...] = middle
    normed, _ = norm_rows(middle)
    second_o[...] = (normed * norms[2:3, :] + norms[3:4, :]).astype(BF16)


def mlp_forward(mp_s, table, second, middle, dec_bias, *rest, nparts, per_view, part, wide, rows_each):
    up_parts, down_parts = rest[:nparts], rest[nparts : 2 * nparts]
    act_o, slope_o, final_o, keep_o, send_o = rest[2 * nparts : 2 * nparts + 5]
    up, down, up_sems, down_sems = rest[2 * nparts + 5 :]
    up_copies = weight_copies(up_parts, table, up, up_sems)
    down_copies = weight_copies(down_parts, table, down, down_sems)

    @pl.when(pl.program_id(0) == 0)
    def _():
        for copy in up_copies + down_copies:
            copy.start()
        for copy in up_copies + down_copies:
            copy.wait()

    acc = middle[...]
    rows = second[...]
    for half in range(2):
        for start in range(0, part, wide):
            pre = mm(rows, up[half, :, start : start + wide])
            cumulative = 0.5 * (1.0 + lax.erf(pre * (1.0 / math.sqrt(2.0))))
            act = (pre * cumulative).astype(BF16)
            slope = cumulative + pre * jnp.exp(-0.5 * pre * pre) * (1.0 / math.sqrt(2.0 * math.pi))
            act_o[:, half * part + start : half * part + start + wide] = act
            slope_o[:, half * part + start : half * part + start + wide] = slope.astype(BF16)

            acc = acc + mm(act, down[half, :, start : start + wide], NT)
    final = acc.astype(BF16)
    final_o[...] = final
    outs = [
        mm(final, down[half, :, part:]) + dec_bias[half : half + 1, :] for half in range(2)
    ]
    mine = jnp.where(mp_s[0] == 0, outs[0], outs[1])
    theirs = jnp.where(mp_s[0] == 0, outs[1], outs[0])
    views = rows_each // per_view
    for view in range(keep_o.shape[0]):
        at = (view // views) * rows_each + (view % views) * per_view
        keep_o[view, :per_view, :] = mine[at : at + per_view].astype(BF16)
        send_o[view, :per_view, :] = theirs[at : at + per_view].astype(BF16)


def mlp_backward(
    mp_s, where_s, table, mine, theirs, slope, middle, norms, *rest, nparts, per_view, part, wide, rows_each
):
    up_parts, down_parts = rest[:nparts], rest[nparts : 2 * nparts]
    rows_o, low_o, pre_o, mid_o, midlow_o, sums_o = rest[2 * nparts : 2 * nparts + 6]
    up, down, pieces, flat, up_sems, down_sems, piece_sems = rest[2 * nparts + 6 :]
    step = pl.program_id(0)
    nviews = pieces.shape[2]
    up_copies = weight_copies(up_parts, table, up, up_sems)
    down_copies = weight_copies(down_parts, table, down, down_sems)

    def fetch(turn):
        slot = lax.rem(turn, 2)
        copies = []
        for view in range(nviews):
            at = where_s[turn * nviews + view]
            for side, (rows_in, half) in enumerate(((mine, mp_s[0]), (theirs, 1 - mp_s[0]))):
                copies.append(
                    pltpu.make_async_copy(
                        rows_in.at[at], pieces.at[slot, half, view], piece_sems.at[slot, side, view]
                    )
                )
        return copies

    @pl.when(step == 0)
    def _():
        for copy in fetch(step):
            copy.start()

    @pl.when(step + 1 < pl.num_programs(0))
    def _():
        for copy in fetch(step + 1):
            copy.start()

    @pl.when(step == 0)
    def _():
        for copy in down_copies + up_copies:
            copy.start()
        flat[...] = jnp.zeros_like(flat)
        sums_o[...] = jnp.zeros_like(sums_o)
        for copy in down_copies + up_copies:
            copy.wait()

    for copy in fetch(step):
        copy.wait()
    slot = lax.rem(step, 2)
    dec = pieces.shape[4]
    views = rows_each // per_view
    for view in range(nviews):
        at = (view // views) * rows_each + (view % views) * per_view
        for half in range(2):
            flat[at : at + per_view, half * dec : (half + 1) * dec] = pieces[slot, half, view][
                :per_view
            ].astype(F32)
    rows = flat[...].astype(BF16)
    rows_o[...] = rows
    final = mm(rows[:, :dec], down[0, :, part:], NT) + mm(rows[:, dec:], down[1, :, part:], NT)
    low = final.astype(BF16)
    low_o[...] = low
    acc = jnp.zeros(final.shape, F32)
    for half in range(2):
        for start in range(0, part, wide):
            at = half * part + start
            hidden = mm(low, down[half, :, start : start + wide])
            pre = (hidden * slope[:, at : at + wide].astype(F32)).astype(BF16)
            pre_o[:, at : at + wide] = pre

            acc = acc + mm(pre, up[half, :, start : start + wide], NT)
    normed, inverse = norm_rows(middle[...])
    sums_o[0:1, :] += jnp.sum(acc * normed, axis=0, keepdims=True)
    sums_o[1:2, :] += jnp.sum(acc, axis=0, keepdims=True)
    mid = final + norm_back(acc * norms[2:3, :], normed, inverse)
    mid_o[...] = mid
    midlow_o[...] = mid.astype(BF16)


def attn_backward(
    half_s, mp_s, counts_s, table, tokens, packed, attended, lse, mid, norms, *rest, nparts, per_view, part, piece, rows_out
):
    parts, rest = rest[:nparts], rest[nparts:]
    weights, sems = rest[-2:]
    last = len(rest) == 6
    packed_o = rest[1] if last else rest[0]
    half = half_s[0]
    step = pl.program_id(0)
    copies = []
    if len(parts) == 1:
        copies.append(pltpu.make_async_copy(parts[0].at[half], weights, sems.at[0]))
    else:
        for index, array in enumerate(parts):
            for inner in range(PIECE):
                rows = array.shape[1]
                start = pl.multiple_of(table[(piece + index) * PIECE + inner] * rows, ROUND)
                copies.append(
                    pltpu.make_async_copy(
                        array.at[inner], weights.at[pl.ds(start, rows), :], sems.at[index * PIECE + inner]
                    )
                )

    @pl.when(step == 0)
    def _():
        for copy in copies:
            copy.start()
        if last:
            rest[3][...] = jnp.zeros_like(rest[3])
        for copy in copies:
            copy.wait()

    size = tokens.shape[0]
    scale = 1.0 / math.sqrt(HEADDIM)
    wide = 2 * HEADDIM
    heads = part // HEADDIM
    bias = allowed_bias(size, counts_s[mp_s[0] * pl.num_programs(0) + step], per_view)
    bias = jnp.concatenate([bias, bias], axis=0)
    masks, scaled = pair_masks(1.0), pair_masks(scale)
    key_scale = jnp.full((1, wide), scale, F32).astype(BF16)
    lane = lax.broadcasted_iota(jnp.int32, (size, wide), 1)
    low = lane < HEADDIM
    ones = jnp.ones((size, wide), BF16)
    shifts = lse[...]
    owner = lax.broadcasted_iota(jnp.int32, (part, wide), 0) // HEADDIM + half * heads
    slot = lax.broadcasted_iota(jnp.int32, (part, wide), 1)
    owners = (((slot & (PARTS - 1)) == owner) & (slot < 3 * PARTS)).astype(F32).astype(BF16)
    middle = mid[...]
    middle_low = middle.astype(BF16)
    grad_att = mm(middle_low, weights[:, 3 * part :]).astype(BF16)
    weighted = grad_att.astype(F32) * attended[...].astype(F32)
    high = weighted.astype(BF16)
    centre = mm(high, owners) + mm((weighted - high.astype(F32)).astype(BF16), owners)
    centre = in_parts(-centre)
    pairs = range(part // wide)
    sides, logits, grad_probs, lows = [], [], [], []
    for pair in pairs:
        at = pair * wide
        query = packed[:, at : at + wide]
        key = packed[:, part + at : part + at + wide]
        value = packed[:, 2 * part + at : 2 * part + at + wide]
        grad = grad_att[:, at : at + wide]
        query = jnp.concatenate([query * scaled[0], query * scaled[1]], axis=0)
        grad = jnp.concatenate([grad * masks[0], grad * masks[1]], axis=0)
        index = half * heads + pair * 2
        picks = [head_lanes(index + which).astype(F32).astype(BF16) for which in range(2)]
        minus_lse = jnp.concatenate([shifts * pick for pick in picks], axis=0)
        minus_centre = jnp.concatenate([centre * pick for pick in picks], axis=0)
        sides.append((query, key * key_scale, grad))
        logits.append(
            mm(jnp.concatenate([query, minus_lse], axis=1), jnp.concatenate([key, ones], axis=1), NT)
            + bias
        )
        grad_probs.append(
            mm(jnp.concatenate([grad, minus_centre], axis=1), jnp.concatenate([value, ones], axis=1), NT)
        )
    for pair in pairs:
        probs = jnp.exp(logits[pair])
        lows.append(((probs * grad_probs[pair]).astype(BF16), probs.astype(BF16)))
    for pair in pairs:
        query, key, grad = sides[pair]
        scores, probs = lows[pair]
        at = pair * wide
        grad_query = mm(scores, key)
        packed_o[:, at : at + wide] = jnp.where(low, grad_query[:size], grad_query[size:]).astype(BF16)
        at = at + part
        packed_o[:, at : at + wide] = mm(query, scores, TN).T.astype(BF16)
        at = at + part
        packed_o[:, at : at + wide] = mm(grad, probs, TN).T.astype(BF16)
    back = mm(packed_o[...], weights[:, : 3 * part], NT)
    if not last:
        rest[1][...] = back
        return
    back_in, tokens_o, sums_o = rest[0], rest[2], rest[3]
    back = back + back_in[...]
    normed, inverse = norm_rows(tokens[...].astype(F32))
    sums_o[0:1, :] += jnp.sum(back * normed, axis=0, keepdims=True)
    sums_o[1:2, :] += jnp.sum(back, axis=0, keepdims=True)
    grads = middle + norm_back(back * norms[0:1, :], normed, inverse)
    for index in range(tokens_o.shape[0] // rows_out):

        @pl.when(step == index)
        def _(index=index):
            tokens_o[index * rows_out : (index + 1) * rows_out, :] = grads[:rows_out].astype(BF16)


def weight_grad(side_s, places, *rest, steps, rows_each, add_other):
    sides, rest = rest[: 2 * len(steps)], rest[2 * len(steps) :]
    step = pl.program_id(0 if places is not None else 1)
    begin = 0
    for index, length in enumerate(steps):
        left, right = sides[2 * index], sides[2 * index + 1]

        @pl.when((step >= begin) & (step < begin + length))
        def _(left=left, right=right):
            weight_block(mm(left[...], right[...], TN), places, rest, rows_each, add_other)

        begin += length


def weight_block(product, places, rest, rows_each, add_other):
    if places is None:
        grads_o = rest[0]
        for block in range(grads_o.shape[0]):
            grads_o[block, 0] = product[block * rows_each : (block + 1) * rows_each].astype(BF16)
    elif add_other:
        other, keep_o, send_o, held = rest[:4]
        half = keep_o.shape[0]
        for block in range(2 * half):
            held[places[block]] = product[block * rows_each : (block + 1) * rows_each]
        keep_o[...] = (held[:half] + other[:half].astype(F32)).astype(BF16)
        send_o[...] = (held[half:] + other[half:].astype(F32)).astype(BF16)
    else:
        product = product.astype(BF16)
        grads_o = rest[0]
        for block in range(grads_o.shape[0]):
            grads_o[places[block]] = product[block * rows_each : (block + 1) * rows_each]


def take_cells(where_s, marks, live_row, cells, rows_o, sums_o, *, per_view, stride):
    step = pl.program_id(0)

    @pl.when(step == 0)
    def _():
        sums_o[...] = jnp.zeros_like(sums_o)

    grid, each, dec = cells.shape
    flat = cells[...].reshape(grid * each, dec)
    lane = lax.broadcasted_iota(jnp.int32, (each * stride, grid * each), 1)
    pick = (marks[...] == lane).astype(F32)
    covered = jnp.sum(pick, axis=0, keepdims=True)
    open_cells = jnp.broadcast_to(live_row[0] - covered, (8, grid * each)).astype(BF16)
    taken = mm(pick.astype(BF16), flat)
    masked = mm(open_cells, flat)
    for index in range(each):
        rows_o[where_s[step * each + index]] = taken[index * stride : (index + 1) * stride].astype(BF16)
    sums_o[0:1, :] += jnp.sum(taken, axis=0, keepdims=True)
    sums_o[1:2, :] += masked[0:1]


def put_cells(where_s, live_s, marks, mask, positions, rows, cells_o, held, *, per_view):
    step = pl.program_id(0)
    grid, each, dec = cells_o.shape
    stride = held.shape[0] // each

    @pl.when(step == 0)
    def _():
        held[...] = jnp.zeros_like(held)

    slot = lax.broadcasted_iota(jnp.int32, (1, each, 1), 1)
    live = jnp.zeros((1, each, 1), F32)
    for index in range(each):
        at = step * each + index
        held[index * stride : index * stride + per_view, :] = rows[where_s[at]][:per_view]
        live = jnp.where(slot == index, live_s[at].astype(F32), live)
    line = lax.broadcasted_iota(jnp.int32, (grid * each, held.shape[0]), 0)
    place = (marks[0] == line).astype(F32)
    covered = jnp.sum(place, axis=1, keepdims=True)
    live = jnp.broadcast_to(live, (grid, each, 1)).reshape(grid * each, 1)
    filled = mm(place.astype(BF16), held[...]) + (live - covered) * mask[...]
    filled = filled.reshape(grid, each, dec) + positions[...][:, None, :]
    cells_o[...] = filled.astype(BF16)


def order_views(where_s, mp_s, own, theirs, out, sems):
    count = own.shape[0]
    copies = []
    for view in range(count):
        mine, other = mp_s[0] * count + view, (1 - mp_s[0]) * count + view
        copies.append(pltpu.make_async_copy(own.at[view], out.at[where_s[mine]], sems.at[view]))
        copies.append(
            pltpu.make_async_copy(theirs.at[view], out.at[where_s[other]], sems.at[count + view])
        )
    for copy in copies:
        copy.start()
    for copy in copies:
        copy.wait()


def tile_of(scalars, begin=0):
    lane = lax.broadcasted_iota(jnp.int32, (1, 128), 1)
    tile = jnp.zeros((1, 128), F32)
    for index, value in enumerate(scalars):
        tile = jnp.where(lane == begin + index, value, tile)
    return tile


def total(values):
    return jnp.sum(jnp.sum(values, axis=1, keepdims=True), axis=0, keepdims=True)


def grad_views(refs, masters):
    first, second, third, norms, dec = refs
    wide, thin = masters[2].shape[1], masters[4].shape[1]
    return [
        first,
        second.at[:, pl.ds(wide, masters[1].shape[1])],
        second.at[:, pl.ds(0, wide)],
        third.at[:, pl.ds(0, wide)],
        third.at[:, pl.ds(wide, thin)],
        norms,
        dec,
    ]


def squares_kernel(once_s, *refs):
    masters, (tiles_o,) = refs[5:12], refs[12:]
    grads = grad_views(refs[:5], masters)
    single = [1.0] * 5 + [once_s[0].astype(F32), 1.0]
    grad_sq, weight_sq = [], []
    for index in range(7):
        value = grads[index][...].astype(F32)
        grad_sq.append(total(value * value) * single[index])
        if index == 0:
            weight = sum(total(masters[0][k] * masters[0][k]) for k in range(3))
        else:
            weight = total(masters[index][...] * masters[index][...])
        weight_sq.append(weight * single[index])
    tile = tile_of(grad_sq) + tile_of(weight_sq, 64)
    for peer in range(tiles_o.shape[0]):
        tiles_o[peer] = tile


def lamb_kernel(once_s, tiles, *refs):
    masters, moments, squares = refs[5:12], refs[12:19], refs[19:26]
    grads = grad_views(refs[:5], masters)
    outs = refs[26:]
    clip_o, moment_o, square_o, step_o = outs[:7], outs[7:14], outs[14:21], outs[21:28]
    sum_o, tiles_o = outs[28:]
    summed = jnp.sum(tiles[...], axis=0)
    sum_o[...] = summed
    lane = lax.broadcasted_iota(jnp.int32, (1, 128), 1)
    clip = jnp.sqrt(total(jnp.where(lane < 7, summed, 0.0)))
    factor = jnp.minimum(1.0, 0.5 * math.sqrt(PARAMS) / clip)
    single = [1.0] * 5 + [once_s[0].astype(F32), 1.0]
    update_sq = []
    for index in range(7):
        amount = jnp.zeros((1, 1), F32)
        for piece in range(3 if index == 0 else 1):
            at = piece if index == 0 else Ellipsis
            value = grads[index][...].astype(F32)
            if index == 0:
                width = masters[0].shape[2]
                value = value[:, piece * width : (piece + 1) * width]
            clipped = value * factor
            moment = BETA_ONE * moments[index][at] + (1.0 - BETA_ONE) * clipped
            square = BETA_TWO * squares[index][at] + (1.0 - BETA_TWO) * clipped * clipped
            step = moment / (jnp.sqrt(square) + ADAM_EPS) + DECAY_RATE * masters[index][at]
            clip_o[index][at] = clipped
            moment_o[index][at] = moment
            square_o[index][at] = square
            step_o[index][at] = step
            amount = amount + total(step * step)
        update_sq.append(amount * single[index])
    tile = tile_of(update_sq)
    for peer in range(tiles_o.shape[0]):
        tiles_o[peer] = tile


def update_kernel(tiles, summed, *refs):
    masters, steps, outs = refs[:7], refs[7:14], refs[14:]
    updated_o, copy_o, (norms_o, clip_o) = outs[:7], outs[7:14], outs[14:]
    lane = lax.broadcasted_iota(jnp.int32, (1, 128), 1)
    squared = summed[...]
    clip = jnp.sqrt(total(jnp.where(lane < 7, squared, 0.0)))
    weight_norm = jnp.sqrt(jnp.concatenate([squared[:, 64:], squared[:, :64]], axis=1))
    update_norm = jnp.sqrt(jnp.sum(tiles[...], axis=0))
    ratio = weight_norm / (update_norm + TRUST_EPS)
    norms_o[0:1, :] = weight_norm[:, :7]
    norms_o[1:2, :] = update_norm[:, :7]
    clip_o[...] = clip
    for index in range(7):
        rate = LEARN_RATE * total(jnp.where(lane == index, ratio, 0.0))
        for piece in range(3 if index == 0 else 1):
            at = piece if index == 0 else Ellipsis
            updated = masters[index][at] - rate * steps[index][at]
            updated_o[index][at] = updated
            copy_o[index][at] = updated.astype(BF16)


def shape(dims, dtype=F32):
    return jax.ShapeDtypeStruct(tuple(dims), dtype)


def whole(kernel, outs, scalars, operands, **kw):
    return pl.pallas_call(
        kernel,
        out_shape=outs,
        in_specs=[pl.BlockSpec(memory_space=pltpu.SMEM)] * len(scalars)
        + [pl.BlockSpec(memory_space=pltpu.VMEM)] * len(operands),
        out_specs=[pl.BlockSpec(memory_space=pltpu.VMEM)] * len(outs),
        compiler_params=params(),
        **kw,
    )(*scalars, *operands)


def per_device(
    tokens,
    counts,
    visible,
    dest_device,
    dest_slot,
    cotangent,
    *state,
):
    masters = [state[3 * index] for index in range(7)]
    moments = [state[3 * index + 1] for index in range(7)]
    squares = [state[3 * index + 2] for index in range(7)]

    def flat_state(arrays):
        a, b, c, d, e, f, g = arrays
        return [a.transpose(1, 0, 2), b.T, c, d.T, e, f, g[:, 0, :]]

    def natural(arrays):
        a, b, c, d, e, f, g = arrays
        return [a.transpose(1, 0, 2), b.T, c, d.T, e, f, g[:, None, :]]

    masters, moments, squares = flat_state(masters), flat_state(moments), flat_state(squares)

    peers, cores = lax.axis_size("dp"), lax.axis_size("mp")
    me, core = lax.axis_index("dp"), lax.axis_index("mp")
    core_s = core.astype(jnp.int32).reshape(1)
    once_s = 1 - core_s
    model = tokens.shape[1]
    nviews, per_view = visible.shape
    episodes = counts.shape[0]
    views_each = nviews // episodes
    span = views_each * per_view
    size = -(-span // ROUND) * ROUND
    here = episodes // cores
    rows = here * size
    cells, dec = cotangent.shape[1:]
    part = masters[1].shape[1]
    hidden = masters[2].shape[1]
    shard_rows = masters[2].shape[0]
    room = (nviews + peers - 1) // peers
    npos = peers * room
    fast = peers == FAST_PEERS

    low = [m.astype(BF16) for m in masters]
    chunk_a = jnp.concatenate([low[0][0], low[0][1], low[0][2], low[1]], axis=1)
    chunk_b = low[2]
    chunk_c = jnp.concatenate([low[3], low[4]], axis=1)

    same = dest_device[:, None] == dest_device[None, :]
    earlier = jnp.arange(nviews)[None, :] < jnp.arange(nviews)[:, None]
    rank = jnp.sum((same & earlier).astype(jnp.int32), axis=1)
    where_view = (dest_device * room + rank).astype(jnp.int32)
    layout = jnp.arange(npos, dtype=jnp.int32)[:, None] == where_view[None, :]
    live_view = (
        jnp.arange(nviews, dtype=jnp.int32) % views_each < jnp.repeat(counts, views_each)
    ).astype(jnp.int32)
    details = jnp.concatenate(
        [jnp.ones((nviews, 1), jnp.int32), dest_slot[:, None], live_view[:, None], visible], axis=1
    )
    fields = details.shape[1]
    sent = jnp.dot(layout.astype(BF16), details.astype(BF16), preferred_element_type=F32)
    sent = sent.astype(BF16).reshape(peers, room * fields)
    small = jnp.concatenate([low[5].reshape(-1), low[6].reshape(-1)])
    message = jnp.concatenate(
        [sent, jnp.broadcast_to(small[None], (peers, small.shape[0]))], axis=1
    )
    message = jnp.broadcast_to(message[:, None], (peers, cores, message.shape[1]))
    if fast:
        gather = Gather((chunk_a, chunk_b, chunk_c), peers)
        z_one = gather.step_z((message,))
    message = lax.all_to_all(
        message.reshape(peers * cores, -1), AXES, split_axis=0, concat_axis=0, tiled=True
    ).reshape(peers, cores, -1)
    if fast:
        message = after(message, *z_one)
    got = message[:, 0, : room * fields].reshape(npos, fields).astype(jnp.int32)
    nln = 4 * shard_rows
    ln_full = (
        message[:, 0, room * fields : room * fields + nln]
        .reshape(peers, 4, shard_rows)
        .transpose(1, 0, 2)
        .reshape(4, model)
        .astype(F32)
    )
    norms = jnp.concatenate([ln_full, jnp.zeros((4, model), F32)], axis=0)
    dec_full = (
        message[:, :, room * fields + nln :]
        .reshape(peers, cores, 2, dec // peers)
        .transpose(2, 1, 0, 3)
        .reshape(2, cores, dec)
        .astype(F32)
    )
    mask_token = lax.dynamic_index_in_dim(dec_full[1], core, 0, keepdims=True)
    held_slot = got[:, 1]
    filled = (held_slot[None, :] == jnp.arange(nviews, dtype=jnp.int32)[:, None]) & (
        got[:, 0][None, :] > 0
    )
    where_slot = jnp.sum(
        jnp.where(filled, jnp.arange(npos, dtype=jnp.int32)[None, :], 0), axis=1
    ).astype(jnp.int32)
    owned = jnp.dot(
        filled.astype(BF16), got.astype(BF16), preferred_element_type=F32
    ).astype(jnp.int32)
    live_slot, owned_spots = owned[:, 2], owned[:, 3:]
    each = 8
    groups = nviews // each
    marks = jnp.where(
        live_slot[:, None] > 0,
        owned_spots * each + (jnp.arange(nviews, dtype=jnp.int32) % each)[:, None],
        -1,
    )
    tall = -(-per_view // 8) * 8
    stride_take, stride_put = tall, -(-per_view // 64) * 64
    take_marks = jnp.pad(marks, ((0, 0), (0, stride_take - per_view)), constant_values=-1)
    take_marks = take_marks.reshape(nviews * stride_take, 1)
    put_marks = jnp.pad(marks, ((0, 0), (0, stride_put - per_view)), constant_values=-1)
    put_marks = put_marks.reshape(groups, 1, each * stride_put)
    live_row = jnp.broadcast_to(
        live_slot.astype(F32).reshape(groups, 1, each), (groups, cells, each)
    ).reshape(groups, 1, cells * each)

    take_call = pl.pallas_call(
        lambda *refs: take_cells(*refs, per_view=per_view, stride=stride_take),
        out_shape=[shape((npos, tall, dec), BF16), shape((8, dec))],
        grid_spec=pltpu.PrefetchScalarGridSpec(
            num_scalar_prefetch=1,
            grid=(groups,),
            in_specs=[
                pl.BlockSpec((each * stride_take, 1), lambda i, _: (i, 0)),
                pl.BlockSpec((1, 1, cells * each), lambda i, _: (i, 0, 0)),
                pl.BlockSpec((cells, each, dec), lambda i, _: (0, i, 0)),
            ],
            out_specs=[
                pl.BlockSpec((npos, tall, dec), lambda i, _: (0, 0, 0)),
                pl.BlockSpec((8, dec), lambda i, _: (0, 0)),
            ],
        ),
        compiler_params=params(),
        cost_estimate=cost(2 * nviews * stride_take * cells * each * dec, cotangent.size * 2),
        name="take_cells",
    )

    positions = lax.dynamic_slice_in_dim(
        grid_positions(math.isqrt(cells), dec * cores), core * dec, dec, 1
    )
    own = lax.dynamic_slice_in_dim(
        after(tokens, *z_one) if fast else tokens, core * (here * span), here * span, 0
    ).reshape(here, span, model)
    own = jnp.pad(own, ((0, 0), (0, size - span), (0, 0))).reshape(rows, model)
    begun = gather.step_near((take_marks, live_row, own)) if fast else []
    hold = after if fast else (lambda array, *others: array)
    leaves = jax.tree.leaves
    returned, dec_sums = take_call(
        where_slot, hold(take_marks, *begun), live_row, cotangent.transpose(1, 0, 2)
    )
    if fast:
        later = (positions, mask_token, put_marks, dec_full, norms)
        parts_a = gather.step_far((returned,) + later)
        positions, mask_token, put_marks, dec_full, norms = hold_all(later, parts_a[:1])
    else:
        parts_a = gather_plain(chunk_a)
    nparts = len(parts_a)
    table = gather_table(me, core)
    nsem = PIECE * nparts if fast else 1

    smem = pl.BlockSpec(memory_space=pltpu.SMEM)
    fixed = lambda dims: pl.BlockSpec(dims, lambda i: (0,) * len(dims))
    chunk_cols = [chunk_a.shape[1], chunk_b.shape[1], chunk_c.shape[1]]
    weight_bytes = [2 * 2 * model * cols for cols in chunk_cols]
    calls = 2 if here % 2 == 0 else 1
    each_call = here // calls

    def attn_forward_call(call, own, earlier):
        begin = call * each_call
        ep = lambda cols: pl.BlockSpec((size, cols), lambda i: (i + begin, 0))
        return pl.pallas_call(
            lambda *refs: attn_forward(
                *refs, nparts=nparts, per_view=per_view, part=part, begin=begin, here=here
            ),
            grid=(each_call,),
            out_shape=[
                shape((rows, model), BF16),
                shape((rows, 6 * part), BF16),
                shape((rows, 2 * part), BF16),
                shape((rows, model)),
                shape((rows, model), BF16),
                shape((rows, 2 * HEADDIM), BF16),
            ],
            in_specs=[smem, smem, smem, ep(model), fixed((8, model))]
            + [any_spec()] * (nparts + len(earlier)),
            out_specs=[ep(model), ep(6 * part), ep(2 * part), ep(model), ep(model), ep(2 * HEADDIM)],
            scratch_shapes=[
                pltpu.VMEM((2, model, chunk_cols[0]), BF16),
                pltpu.SemaphoreType.DMA((nsem,)),
            ],
            input_output_aliases={5 + nparts + index: index for index in range(len(earlier))},
            compiler_params=params(),
            cost_estimate=cost(
                6 * rows * model * 8 * part // calls, weight_bytes[0] + rows * model * 16 // calls
            ),
            name="attn_forward",
        )(core_s, counts, table, own, norms, *parts_a, *earlier)

    attn = []
    for call in range(calls):
        gates = gather.later() if fast and call > 0 else []
        attn = attn_forward_call(call, after(own, *gates) if gates else own, attn)
        if call == 0 and fast:
            returned = after(returned, attn[0])
            gather.second(attn[0])
    if fast:
        parts_b, parts_c = gather.finish(attn[0])
    else:
        parts_b, parts_c = gather_plain(chunk_b), gather_plain(chunk_c)
    came_mine = lax.all_to_all(returned, "dp", split_axis=0, concat_axis=0, tiled=True)
    came_theirs = swap(came_mine, peers, 0, 1)
    first, packed, attended, middle, second, lse = attn

    group = 2
    chunk = group * size
    steps = here // group
    gviews = group * views_each
    blk = lambda cols: pl.BlockSpec((chunk, cols), lambda i: (i, 0))
    wide = hidden
    mlp_scratch = [
        pltpu.VMEM((2, model, chunk_cols[1]), BF16),
        pltpu.VMEM((2, model, chunk_cols[2]), BF16),
    ]
    act, slope, final, emb_keep, emb_send = pl.pallas_call(
        lambda *refs: mlp_forward(
            *refs, nparts=nparts, per_view=per_view, part=hidden, wide=wide, rows_each=size
        ),
        grid=(steps,),
        out_shape=[
            shape((rows, 2 * hidden), BF16),
            shape((rows, 2 * hidden), BF16),
            shape((rows, model), BF16),
            shape((steps * gviews, tall, dec), BF16),
            shape((steps * gviews, tall, dec), BF16),
        ],
        in_specs=[smem, smem, blk(model), blk(model), fixed((2, dec))] + [any_spec()] * (2 * nparts),
        out_specs=[
            blk(2 * hidden),
            blk(2 * hidden),
            blk(model),
            pl.BlockSpec((gviews, tall, dec), lambda i: (i, 0, 0)),
            pl.BlockSpec((gviews, tall, dec), lambda i: (i, 0, 0)),
        ],
        scratch_shapes=mlp_scratch + [pltpu.SemaphoreType.DMA((nsem,))] * 2,
        compiler_params=params(),
        cost_estimate=cost(
            4 * rows * model * 2 * hidden, weight_bytes[1] + weight_bytes[2] + rows * hidden * 8
        ),
        name="mlp_forward",
    )(core_s, table, second, middle, dec_full[0], *parts_b, *parts_c)

    where_mine = lax.dynamic_slice_in_dim(where_view, core * (nviews // cores), nviews // cores)
    emb_rows, glow, gpre, gmid, gmid_low, ln_two = pl.pallas_call(
        lambda *refs: mlp_backward(
            *refs, nparts=nparts, per_view=per_view, part=hidden, wide=wide, rows_each=size
        ),
        grid=(steps,),
        out_shape=[
            shape((rows, 2 * dec), BF16),
            shape((rows, model), BF16),
            shape((rows, 2 * hidden), BF16),
            shape((rows, model)),
            shape((rows, model), BF16),
            shape((8, model)),
        ],
        in_specs=[smem, smem, smem, any_spec(), any_spec(), blk(2 * hidden), blk(model), fixed((8, model))]
        + [any_spec()] * (2 * nparts),
        out_specs=[blk(2 * dec), blk(model), blk(2 * hidden), blk(model), blk(model), fixed((8, model))],
        scratch_shapes=mlp_scratch
        + [
            pltpu.VMEM((2, 2, gviews, tall, dec), BF16),
            pltpu.VMEM((chunk, 2 * dec), F32),
            pltpu.SemaphoreType.DMA((nsem,)),
            pltpu.SemaphoreType.DMA((nsem,)),
            pltpu.SemaphoreType.DMA((2, 2, gviews)),
        ],
        compiler_params=params(),
        cost_estimate=cost(
            4 * rows * model * 2 * hidden, weight_bytes[1] + weight_bytes[2] + rows * hidden * 8
        ),
        name="mlp_backward",
    )(core_s, where_mine, table, came_mine, came_theirs, slope, middle, norms, *parts_b, *parts_c)

    emb_other = swap(emb_send, peers, 0, 1)
    if fast:
        emb_other = after(emb_other, glow)
    outgoing = pl.pallas_call(
        order_views,
        out_shape=shape((npos, tall, dec), BF16),
        in_specs=[smem, smem, any_spec(), any_spec()],
        out_specs=any_spec(),
        scratch_shapes=[pltpu.SemaphoreType.DMA((nviews,))],
        compiler_params=params(8 << 20),
        cost_estimate=cost(0, 4 * nviews * per_view * dec),
        name="order_views",
    )(where_view, core_s, emb_keep, emb_other)
    arrived = lax.all_to_all(outgoing, "dp", split_axis=0, concat_axis=0, tiled=True)

    blocks = FAST_PEERS
    if fast:
        places = [place_table(me, core), place_table(me, 1 - core)]
    else:
        places = [jnp.arange(blocks, dtype=jnp.int32)] * 2

    def side_grads(pairs, block, name, other=None, one_side=False):
        lengths = [right.shape[1] // (1 if one_side else 2) // block for _, right in pairs]
        many = sum(lengths)
        begins = [sum(lengths[:index]) for index in range(len(lengths))]

        def column(begin, length):
            shift = 0 if one_side else length
            return lambda j, side, _: (0, side[0] * shift + jnp.clip(j - begin, 0, length - 1))

        in_specs, operands = [], []
        for index, (left, right) in enumerate(pairs):
            in_specs += [
                pl.BlockSpec((rows, model), lambda j, *_: (0, 0)),
                pl.BlockSpec((rows, block), column(begins[index], lengths[index])),
            ]
            operands += [left, right]
        each_row = model // blocks
        spec = lambda count: pl.BlockSpec((count, each_row, block), lambda j, *_: (0, 0, j))
        dims = lambda count: shape((count, each_row, many * block), BF16)
        adding = other is not None
        return pl.pallas_call(
            lambda *refs: weight_grad(*refs, steps=lengths, rows_each=each_row, add_other=adding),
            out_shape=[dims(blocks // 2)] * 2 if adding else dims(blocks),
            grid_spec=pltpu.PrefetchScalarGridSpec(
                num_scalar_prefetch=2,
                grid=(many,),
                in_specs=in_specs + [spec(blocks)] * adding,
                out_specs=[spec(blocks // 2)] * 2 if adding else spec(blocks),
                scratch_shapes=[pltpu.VMEM((blocks, each_row, block), F32)] * adding,
            ),
            compiler_params=params(),
            cost_estimate=cost(2 * rows * model * many * block, 2 * rows * (many * block + model)),
            name=name,
        )(
            core_s if adding else 1 - core_s,
            places[0 if adding else 1],
            *operands,
            *([other] if adding else []),
        )

    def whole_grads(pairs, block, name):
        lengths = [right.shape[1] // 2 // block for _, right in pairs]
        many = sum(lengths)
        begins = [sum(lengths[:index]) for index in range(len(lengths))]

        def column(begin, length):
            return lambda h, j: (0, h * length + jnp.clip(j - begin, 0, length - 1))

        in_specs, operands = [], []
        for index, (left, right) in enumerate(pairs):
            in_specs += [
                pl.BlockSpec((rows, model), lambda h, j: (0, 0)),
                pl.BlockSpec((rows, block), column(begins[index], lengths[index])),
            ]
            operands += [left, right]
        return pl.pallas_call(
            lambda *refs: weight_grad(
                None, None, *refs, steps=lengths, rows_each=shard_rows, add_other=False
            ),
            out_shape=shape((peers, 2, shard_rows, many * block), BF16),
            grid=(2, many),
            in_specs=in_specs,
            out_specs=pl.BlockSpec((peers, 1, shard_rows, block), lambda h, j: (0, h, 0, j)),
            compiler_params=params(),
            cost_estimate=cost(4 * rows * model * many * block, 4 * rows * (many * block + model)),
            name=name,
        )(*operands)

    def attn_backward_call(half, mid, earlier):
        last = earlier is not None
        ep = lambda cols: pl.BlockSpec((size, cols), lambda i, _: (i, 0))
        ep_half = lambda cols: pl.BlockSpec((size, cols), lambda i, half_ref: (i, half_ref[0]))
        full = lambda dims: pl.BlockSpec(dims, lambda i, _: (0,) * len(dims))
        if fast:
            piece = 0 if last else 2
            mine = parts_a[piece : piece + 2]
        else:
            piece, mine = 0, parts_a
        packed_shape = shape((rows, 3 * part), BF16)
        return pl.pallas_call(
            lambda *refs: attn_backward(
                *refs, nparts=len(mine), per_view=per_view, part=part, piece=piece, rows_out=span
            ),
            out_shape=[packed_shape, shape((here * span, model), BF16), shape((8, model))]
            if last
            else [packed_shape, shape((rows, model))],
            grid_spec=pltpu.PrefetchScalarGridSpec(
                num_scalar_prefetch=1,
                grid=(here,),
                in_specs=[smem, smem, smem, ep(model), ep_half(3 * part), ep_half(part), ep(2 * HEADDIM)]
                + [ep(model), full((8, model))]
                + [any_spec()] * len(mine)
                + [ep(model)] * last,
                out_specs=[ep(3 * part), full((here * span, model)), full((8, model))]
                if last
                else [ep(3 * part), ep(model)],
                scratch_shapes=[
                    pltpu.VMEM((model, chunk_cols[0]), BF16),
                    pltpu.SemaphoreType.DMA((2 * PIECE,)),
                ],
            ),
            compiler_params=params(),
            cost_estimate=cost(4 * rows * model * 8 * part, weight_bytes[0] // 2 + rows * model * 8),
            name="attn_backward",
        )(half, core_s, counts, table, own, packed, attended, lse, mid, norms, *mine, *([earlier] if last else []))

    def behind(pairs, *gate):
        left, right = pairs[0]
        return [(left, hold(right, *gate))] + pairs[1:]

    pairs_b = [(second, gpre), (gmid_low, attended)]
    other_b = side_grads(behind(pairs_b, outgoing), part, "grad_up_out_send")
    whole_c = whole_grads(behind([(glow, act), (final, emb_rows)], other_b), 256, "grad_down_emb")
    sum_c = lax.psum_scatter(
        whole_c.reshape(peers * cores * shard_rows, -1), AXES, scatter_dimension=0, tiled=True
    )
    got_b = hold(swap(other_b, peers, 0, 1), whole_c)
    keep, send = side_grads(behind(pairs_b, whole_c), part, "grad_up_out_keep", got_b)
    sum_b = [(keep,), send]
    packed_other, back = attn_backward_call(1 - core_s, hold(gmid, keep, arrived), None)
    sum_b = scatter_near(sum_b, peers, packed_other)
    other_a = side_grads(
        [(first, hold(packed_other, *leaves(sum_b[1])))], part, "grad_in_send", one_side=True
    )
    packed_own, grad_own, ln_one = attn_backward_call(core_s, hold(gmid, other_a), back)
    sum_b = scatter_far(sum_b, peers, packed_own)
    got_a = hold(swap(other_a, peers, 0, 1), packed_own)


    keep, send = side_grads([(first, packed_own)], part, "grad_in_keep", got_a, one_side=True)
    sum_a = [(keep,), send]
    grad_other = hold(swap(grad_own, peers, 0, 1), keep)
    grad_tokens = jnp.where(
        core == 0,
        jnp.concatenate([grad_own, grad_other]),
        jnp.concatenate([grad_other, grad_own]),
    )

    ln_sums = jnp.concatenate([hold(ln_one[:2], keep), ln_two[:2]])
    ln_send = ln_sums.reshape(4, peers, shard_rows).transpose(1, 0, 2).reshape(peers, nln)
    dec_send = dec_sums[:2].reshape(2, peers, dec // peers).transpose(1, 0, 2).reshape(peers, -1)
    small_send = jnp.concatenate([ln_send, dec_send], axis=1)
    small_send = jnp.broadcast_to(small_send[:, None], (peers, cores, small_send.shape[1]))
    small_got = lax.all_to_all(
        small_send.reshape(peers * cores, -1), AXES, split_axis=0, concat_axis=0, tiled=True
    ).reshape(peers, cores, -1)
    grad_ln = jnp.sum(small_got[:, :, :nln], axis=(0, 1)).reshape(4, shard_rows)
    grad_dec = jnp.sum(
        lax.dynamic_index_in_dim(small_got[:, :, nln:], core, 1, keepdims=False), axis=0
    ).reshape(2, dec // peers)

    sum_b = scatter_end(sum_b, peers, grad_tokens) if fast else scatter_end(sum_b, peers)
    sum_a = scatter_near(sum_a, peers, sum_b)

    decoded = pl.pallas_call(
        lambda *refs: put_cells(*refs, per_view=per_view),
        out_shape=shape((cells, nviews, dec), BF16),
        grid_spec=pltpu.PrefetchScalarGridSpec(
            num_scalar_prefetch=2,
            grid=(groups,),
            in_specs=[
                pl.BlockSpec((1, 1, each * stride_put), lambda i, *_: (i, 0, 0)),
                pl.BlockSpec((1, dec), lambda i, *_: (0, 0)),
                pl.BlockSpec((cells, dec), lambda i, *_: (0, 0)),
                pl.BlockSpec((npos, tall, dec), lambda i, *_: (0, 0, 0)),
            ],
            out_specs=pl.BlockSpec((cells, each, dec), lambda i, *_: (0, i, 0)),
            scratch_shapes=[pltpu.VMEM((each * stride_put, dec), BF16)],
        ),
        compiler_params=params(),
        cost_estimate=cost(2 * nviews * stride_put * cells * each * dec, cotangent.size * 2),
        name="put_cells",
    )(where_slot, live_slot, hold(put_marks, *leaves(sum_a[1])), mask_token, positions, arrived)
    sum_a = scatter_end(scatter_far(sum_a, peers, grad_ln, decoded), peers)
    decoded = decoded.transpose(1, 0, 2)

    grads = [sum_a, sum_b, sum_c, grad_ln, grad_dec]
    world = peers * cores
    (tiles,) = whole(squares_kernel, [shape((world, 1, 128))], [once_s], grads + masters, name="squares")
    tiles = lax.all_to_all(tiles, AXES, split_axis=0, concat_axis=0, tiled=True)
    same_shapes = [shape(m.shape) for m in masters]
    lamb = whole(
        lamb_kernel,
        same_shapes * 4 + [shape((1, 128)), shape((world, 1, 128))],
        [once_s],
        [tiles] + grads + masters + moments + squares,
        name="lamb",
    )
    summed = lamb[28]
    steps_tiles = lax.all_to_all(lamb[29], AXES, split_axis=0, concat_axis=0, tiled=True)
    update = whole(
        update_kernel,
        same_shapes + [shape(m.shape, BF16) for m in masters] + [shape((2, 7)), shape((1, 1))],
        [],
        [steps_tiles, summed] + masters + list(lamb[21:28]),
        name="update",
    )
    results = [
        natural(group)
        for group in (lamb[:7], lamb[7:14], lamb[14:21], update[:7], update[7:14])
    ]
    outs = [decoded, grad_tokens, update[15].reshape(1), update[14]]
    for index in range(7):
        outs += [group[index] for group in results]
    return tuple(outs)


def solution(mesh):
    tensor_specs = [
        P("dp", None, "mp"),
        P("mp", "dp"),
        P("dp", "mp"),
        P("mp", "dp"),
        P("dp", "mp"),
        P(None, "dp"),
        P(None, "mp", "dp"),
    ]
    in_specs = (
        P("dp", None),
        P("dp"),
        P("dp", None),
        P("dp"),
        P("dp"),
        P("dp", None, "mp"),
    ) + tuple(spec for spec in tensor_specs for _ in range(3))
    out_specs = (P("dp", None, "mp"), P("dp", None), P(), P()) + tuple(
        spec for spec in tensor_specs for _ in range(5)
    )
    return jax.shard_map(
        per_device, mesh=mesh, in_specs=in_specs, out_specs=out_specs, check_vma=False
    )
```
